128 devices in a mesh: segment: 8 (over x_hi, z), dp: 16 (over y, x_lo, core).
Axes of the slice: x: 4 (x_hi: 2, x_lo: 2; x = x_hi * 2 + x_lo), y: 4, z: 4, core: 2. Of those that a mesh axis runs over, the one named last changes fastest.
Arguments:
- images: bfloat16 [64, 16, 16, 256], P('dp'), may hold values from -6 to 6
- latent: float32 [64, 512], P('dp'), may hold values from -6 to 6
- weight: bfloat16 [8, 3, 3, 256, 256], P('segment'), may hold values from -0.125 to 0.125
- affine: float32 [8, 512, 256], P('segment'), may hold values from -0.25 to 0.25
- biases: float32 [8, 256], P('segment'), may hold values from -0.5 to 0.5
- cotangent: bfloat16 [64, 16, 16, 256], P('dp'), may hold values from -6 to 6
Outputs:
- grad_weight: float32 [8, 3, 3, 256, 256], P('segment')
- grad_affine: float32 [8, 512, 256], P('segment')
- grad_bias: float32 [8, 256], P('segment')
- grad_latent: float32 [64, 512], P('dp')
The draws below stay inside these ranges and needn't reach their ends.
All inputs are finite; a program needn't handle non-finite values.
Results may differ from the reference program's by a relative error of at most 0.038.
Values may be sent and summed in bfloat16 or wider, within the bound.
No kernel may reach another device: no remote copies, remote signals or barrier semaphores. Data moves between devices by JAX's collectives and lax.ppermute only.
A program may use at most 64 MiB of HBM per device.

```python
import math
import jax
import jax.numpy as jnp
from jax import lax

C = 256
WDIM = 512
RES = 16
MICRO = 1
LAYERS = 8
BATCH = 64


def levels(rng, dims, shards, low, largest):
    factor_of, own = 1.0, jax.random.fold_in(rng, 6)
    for dim, shards_of in shards:
        heights = jnp.exp(jax.random.uniform(jax.random.fold_in(own, dim), (shards_of,), jnp.float32, low / len(shards), largest / len(shards)))
        factor_of = factor_of * jnp.repeat(heights, dims[dim] // shards_of).reshape([-1 if axis == dim else 1 for axis in range(len(dims))])
    return factor_of


def normal_values(stream_key, dims, spread, reach, pieces=(), held_as=jnp.bfloat16):
    array = jax.random.normal(stream_key, dims, jnp.float32) * spread
    if len(pieces) > 0:
        array = levels(stream_key, dims, pieces, -0.22, 0.18) * array
    return jnp.clip(array, min=-reach, max=reach).astype(held_as)


def setup_inputs(seed: int = 0) -> dict:
    seeds = jax.random.split(jax.random.key(seed), 7)
    return {
        "images": normal_values(seeds[0], (BATCH, RES, RES, C), 1.0, 6.0, ((0, 16),)),
        "latent": normal_values(seeds[1], (BATCH, WDIM), 1.0, 6.0, ((0, 16),), jnp.float32),
        "weight": normal_values(seeds[2], (LAYERS, 3, 3, C, C), (9 * C) ** -0.5, 0.125, ((0, 8),)),
        "affine": normal_values(seeds[3], (LAYERS, WDIM, C), WDIM ** -0.5, 0.25, ((0, 8),), jnp.float32),
        "biases": jnp.clip(jax.random.uniform(seeds[4], (LAYERS, C), jnp.float32, -0.5, 0.5) * levels(seeds[4], (LAYERS, C), ((0, 8),), -0.4, 0.0), -0.5, 0.5),
        "cotangent": normal_values(seeds[5], (BATCH, RES, RES, C), 1.0, 6.0, ((0, 16),)),
    }


GAIN = math.sqrt(2.0)

def synth_layer(inputs, latent_rows, kernel, affine_map, offsets):
    styles = jnp.dot(latent_rows, affine_map, precision=lax.Precision.HIGHEST) + 1.0
    energy = lax.optimization_barrier(jnp.sum(jnp.square(kernel.astype(jnp.float32)), axis=(0, 1)))
    demodulate = lax.rsqrt(jnp.dot(styles * styles, energy, precision=lax.Precision.HIGHEST) + 1e-08)
    scaled = (inputs.astype(jnp.float32) * styles[:, None, None, :]).astype(jnp.bfloat16)
    convolved = lax.conv_general_dilated(scaled, kernel, (1, 1), 'SAME', dimension_numbers=('NHWC', 'HWIO', 'NHWC'), preferred_element_type=jnp.float32)
    hidden = convolved * demodulate[:, None, None, :] + offsets
    return (GAIN * hidden * (0.6 + 0.4 * jnp.tanh(hidden))).astype(jnp.bfloat16)

def reference(images, latent, weight, affine, biases, cotangent):
    group_count = BATCH // MICRO
    image_groups = images.reshape(group_count, MICRO, RES, RES, C)
    latent_groups = latent.reshape(group_count, MICRO, WDIM)
    upstream_groups = cotangent.reshape(group_count, MICRO, RES, RES, C)

    def one_group(totals, item):
        inputs, latent_rows, upstream = item
        stored = []
        current = inputs
        for level in range(LAYERS):
            stored.append(current)
            current = synth_layer(current, latent_rows, weight[level], affine[level], biases[level])
        weight_parts = [None] * LAYERS
        affine_parts = [None] * LAYERS
        bias_parts = [None] * LAYERS
        latent_total = jnp.zeros((MICRO, WDIM), jnp.float32)
        for level in reversed(range(LAYERS)):
            result, pull = jax.vjp(synth_layer, stored[level], latent_rows, weight[level], affine[level], biases[level])
            upstream, part_latent, part_weight, part_affine, part_bias = pull(upstream)
            weight_parts[level] = part_weight.astype(jnp.float32)
            affine_parts[level] = part_affine
            bias_parts[level] = part_bias
            latent_total = latent_total + part_latent
        grad_w, grad_a, grad_b = totals
        totals = (grad_w + jnp.stack(weight_parts), grad_a + jnp.stack(affine_parts), grad_b + jnp.stack(bias_parts))
        return (totals, latent_total)
    start = (jnp.zeros((LAYERS, 3, 3, C, C), jnp.float32), jnp.zeros((LAYERS, WDIM, C), jnp.float32), jnp.zeros((LAYERS, C), jnp.float32))
    totals, latent_out = lax.scan(one_group, start, (image_groups, latent_groups, upstream_groups))
    return (totals[0], totals[1], totals[2], latent_out.reshape(BATCH, WDIM))
```

```python
import functools
import math

import jax
import jax.numpy as jnp
from jax import lax
from jax.experimental import pallas as pl
from jax.experimental.pallas import tpu as pltpu
from jax.sharding import PartitionSpec as P

GAIN = math.sqrt(2.0)
EPS = 1e-08
BF = jnp.bfloat16
F32 = jnp.float32
C = 256
PX = 256
TAPS = 9
ROWS = TAPS * C
HALF = ROWS // 2
STAT = 16
DEPTH = 4
ROW = 16
PAD = PX + 2 * ROW
HI = lax.Precision.HIGHEST


def any_spec():
    return pl.BlockSpec(memory_space=pl.ANY)


def vmem_spec():
    return pl.BlockSpec(memory_space=pltpu.VMEM)


def params():
    return pltpu.CompilerParams(vmem_limit_bytes=56 << 20)


def place():
    seg = lax.axis_index("segment")
    return seg // DEPTH, seg % DEPTH, lax.axis_index("dp") % 2


def split3(value):
    hi = value.astype(BF).astype(F32)
    rest = value - hi
    mid = rest.astype(BF).astype(F32)
    return hi, mid, rest - mid


def pack_rows(values):
    row = lax.broadcasted_iota(jnp.int32, (STAT, C), 0)
    out = jnp.zeros((STAT, C), F32)
    k = 0
    for value in values:
        for part in split3(value):
            out = jnp.where(row == k, jnp.broadcast_to(part, (STAT, C)), out)
            k += 1
    return out.astype(BF)


def unpack_rows(tile):
    t = tile.astype(F32)
    return [t[3 * k : 3 * k + 1] + t[3 * k + 1 : 3 * k + 2] + t[3 * k + 2 : 3 * k + 3] for k in range(3)]


def stack_rows(rows):
    index = lax.broadcasted_iota(jnp.int32, (8, C), 0)
    out = jnp.zeros((8, C), F32)
    for k, row in enumerate(rows):
        out = jnp.where(index == k, jnp.broadcast_to(row, (8, C)), out)
    return out


def prepare_kernel(latent_ref, affine_ref, w_ref, bias_ref, w_any, send_ref, styles_ref, demod_ref, energy_ref, tile_ref, sem):
    _, _, core = place()
    copies = [
        pltpu.make_async_copy(
            w_any.at[pl.ds(pl.multiple_of(core * HALF, HALF), HALF)], send_ref.at[k, pl.ds(0, HALF)], sem.at[k]
        )
        for k in range(DEPTH)
    ]
    for copy in copies:
        copy.start()
    styles = jnp.dot(latent_ref[...], affine_ref[...], precision=HI, preferred_element_type=F32) + 1.0
    energy = jnp.zeros((C, C), F32)
    for tap in range(TAPS):
        part = w_ref[tap * C : (tap + 1) * C, :].astype(F32)
        energy += part * part
    energy_ref[...] = energy
    demod = lax.rsqrt(jnp.dot(styles * styles, energy, precision=HI, preferred_element_type=F32) + EPS)
    styles_ref[...] = styles
    demod_ref[...] = demod
    for k in range(DEPTH):
        tile_ref[k] = pack_rows([styles[k : k + 1], demod[k : k + 1], bias_ref[...]])
    stats = [
        pltpu.make_async_copy(tile_ref.at[k], send_ref.at[k, pl.ds(HALF, STAT)], sem.at[DEPTH + k])
        for k in range(DEPTH)
    ]
    for copy in stats:
        copy.start()
    for copy in copies + stats:
        copy.wait()


def prepare(latent8, affine, w, bias):
    return pl.pallas_call(
        prepare_kernel,
        out_shape=(
            jax.ShapeDtypeStruct((DEPTH, HALF + STAT, C), BF),
            jax.ShapeDtypeStruct((8, C), F32),
            jax.ShapeDtypeStruct((8, C), F32),
            jax.ShapeDtypeStruct((C, C), F32),
        ),
        in_specs=[vmem_spec()] * 4 + [any_spec()],
        out_specs=(any_spec(), vmem_spec(), vmem_spec(), vmem_spec()),
        scratch_shapes=[pltpu.VMEM((DEPTH, STAT, C), BF), pltpu.SemaphoreType.DMA((2 * DEPTH,))],
        compiler_params=params(),
        name="prepare",
    )(latent8, affine, w, bias, w)


def weight_copies(a_any, b_any, w_buf, stat_buf, sem):
    _, _, core = place()
    mine = pl.ds(pl.multiple_of(core * HALF, HALF), HALF)
    other = pl.ds(pl.multiple_of((1 - core) * HALF, HALF), HALF)
    return [
        (
            pltpu.make_async_copy(a_any.at[l, pl.ds(HALF, STAT)], stat_buf.at[l], sem.at[0, l]),
            pltpu.make_async_copy(a_any.at[l, pl.ds(0, HALF)], w_buf.at[l, mine], sem.at[1, l]),
            pltpu.make_async_copy(b_any.at[l, pl.ds(0, HALF)], w_buf.at[l, other], sem.at[2, l]),
        )
        for l in range(DEPTH)
    ]


def clear_pads(pad_ref):
    for k in range(3):
        pad_ref[k, 0:ROW, :] = jnp.zeros((ROW, C), BF)
        pad_ref[k, ROW + PX : PAD, :] = jnp.zeros((ROW, C), BF)


def spread(pad_ref, value):
    column = lax.broadcasted_iota(jnp.int32, (PX, C), 0) % ROW
    pad_ref[1, ROW : ROW + PX, :] = value.astype(BF)
    pad_ref[0, ROW : ROW + PX, :] = jnp.where(column == 0, 0.0, pltpu.roll(value, 1, 0)).astype(BF)
    pad_ref[2, ROW : ROW + PX, :] = jnp.where(column == ROW - 1, 0.0, pltpu.roll(value, PX - 1, 0)).astype(BF)


def forward_layer(x, l, w_buf, stat, pad_ref):
    styles, demod, bias = stat
    scaled = (x.astype(F32) * styles).astype(BF).astype(F32)
    spread(pad_ref, scaled)
    conv = None
    for ky in range(3):
        lhs = jnp.concatenate([pad_ref[kx, ky * ROW : ky * ROW + PX, :] for kx in range(3)], axis=1)
        part = jnp.dot(lhs, w_buf[l, ky * 3 * C : (ky + 1) * 3 * C, :], preferred_element_type=F32)
        conv = part if conv is None else conv + part
    return conv


def activate(conv, stat):
    _, demod, bias = stat
    hidden = conv * demod + bias
    return (GAIN * hidden * (0.6 + 0.4 * jnp.tanh(hidden))).astype(BF)


def backward_layer(upstream, x, conv, l, w_buf, stat, pad_ref, send_ref):
    styles, demod, bias = stat
    hidden = conv * demod + bias
    t = jnp.tanh(hidden)
    dh = upstream.astype(F32) * (GAIN * (0.6 + 0.4 * t + 0.4 * hidden * (1.0 - t * t)))
    grad_bias = jnp.sum(dh, axis=0, keepdims=True)
    grad_demod = jnp.sum(dh * conv, axis=0, keepdims=True)
    grad_conv = (dh * demod).astype(BF).astype(F32)
    spread(pad_ref, grad_conv)
    send_ref[l, PX : 2 * PX, :] = pad_ref[1, ROW : ROW + PX, :]
    total = None
    for ky in range(3):
        for kx in range(3):
            lhs = pad_ref[2 - kx, (2 - ky) * ROW : (2 - ky) * ROW + PX, :]
            tap = ky * 3 + kx
            part = lax.dot_general(
                lhs, w_buf[l, tap * C : (tap + 1) * C, :], (((1,), (1,)), ((), ())), preferred_element_type=F32
            )
            total = part if total is None else total + part
    grad_scaled = total.astype(BF).astype(F32)
    xf = x.astype(F32)
    grad_styles = jnp.sum(grad_scaled * xf, axis=0, keepdims=True)
    send_ref[l, 0:PX, :] = (xf * styles).astype(BF)
    send_ref[l, 2 * PX : 2 * PX + STAT, :] = pack_rows([grad_styles, grad_demod, grad_bias])
    return (grad_scaled * styles).astype(BF)


def first_kernel(images_any, a_any, b_any, out_ref, w_buf, stat_buf, x_buf, pad_ref, sem, x_sem):
    _, z, _ = place()
    x_copy = pltpu.make_async_copy(images_any.at[z], x_buf, x_sem)
    x_copy.start()
    copies = weight_copies(a_any, b_any, w_buf, stat_buf, sem)
    for group in copies:
        for copy in group:
            copy.start()
    clear_pads(pad_ref)
    x_copy.wait()
    x = x_buf[...]
    for l in range(DEPTH):
        for copy in copies[l]:
            copy.wait()
        stat = unpack_rows(stat_buf[l])
        x = activate(forward_layer(x, l, w_buf, stat, pad_ref), stat)
    out_ref[...] = x


def middle_kernel(
    images_any, cot_any, recv_ref, a_any, b_any, dx_ref, xs_ref, conv_ref, send_ref,
    w_buf, stat_buf, x_buf, u_buf, pad_ref, sem, x_sem,
):
    half, z, _ = place()
    x_copy = pltpu.make_async_copy(images_any.at[z], x_buf, x_sem.at[0])
    u_copy = pltpu.make_async_copy(cot_any.at[z], u_buf, x_sem.at[1])
    x_copy.start()
    copies = weight_copies(a_any, b_any, w_buf, stat_buf, sem)
    for group in copies:
        for copy in group:
            copy.start()
    u_copy.start()
    clear_pads(pad_ref)
    x_copy.wait()
    x = jnp.where(half == 1, recv_ref[...], x_buf[...])
    stats = []
    for l in range(DEPTH):
        for copy in copies[l]:
            copy.wait()
        stats.append(unpack_rows(stat_buf[l]))
        xs_ref[l] = x
        conv = forward_layer(x, l, w_buf, stats[l], pad_ref)
        conv_ref[l] = conv
        if l < DEPTH - 1:
            x = activate(conv, stats[l])
    u_copy.wait()
    upstream = u_buf[...]
    for l in reversed(range(DEPTH)):
        upstream = backward_layer(upstream, xs_ref[l], conv_ref[l], l, w_buf, stats[l], pad_ref, send_ref)
    dx_ref[...] = upstream


def last_kernel(
    cot_any, recv_ref, xs_any, conv_any, a_any, b_any, send_ref,
    w_buf, stat_buf, xs_buf, conv_buf, u_buf, pad_ref, sem, s_sem, u_sem,
):
    half, z, _ = place()
    u_copy = pltpu.make_async_copy(cot_any.at[z], u_buf, u_sem)
    u_copy.start()
    copies = weight_copies(a_any, b_any, w_buf, stat_buf, sem)
    saves = [
        (
            pltpu.make_async_copy(xs_any.at[l], xs_buf.at[l], s_sem.at[0, l]),
            pltpu.make_async_copy(conv_any.at[l], conv_buf.at[l], s_sem.at[1, l]),
        )
        for l in range(DEPTH)
    ]
    for l in reversed(range(DEPTH)):
        for copy in saves[l] + copies[l]:
            copy.start()
    clear_pads(pad_ref)
    u_copy.wait()
    upstream = jnp.where(half == 1, u_buf[...], recv_ref[...])
    for l in reversed(range(DEPTH)):
        for copy in saves[l] + copies[l]:
            copy.wait()
        stat = unpack_rows(stat_buf[l])
        upstream = backward_layer(upstream, xs_buf[l], conv_buf[l], l, w_buf, stat, pad_ref, send_ref)


def weight_scratch():
    return [pltpu.VMEM((DEPTH, ROWS, C), BF), pltpu.VMEM((DEPTH, STAT, C), BF)]


MAP = jax.ShapeDtypeStruct((PX, C), BF)
SENT = jax.ShapeDtypeStruct((DEPTH, 2 * PX + STAT, C), BF)


def first(images, a, b):
    return pl.pallas_call(
        first_kernel,
        out_shape=MAP,
        in_specs=[any_spec()] * 3,
        out_specs=vmem_spec(),
        scratch_shapes=weight_scratch()
        + [
            pltpu.VMEM((PX, C), BF),
            pltpu.VMEM((3, PAD, C), BF),
            pltpu.SemaphoreType.DMA((3, DEPTH)),
            pltpu.SemaphoreType.DMA,
        ],
        compiler_params=params(),
        name="first",
    )(images, a, b)


def middle(images, cot, recv, a, b):
    return pl.pallas_call(
        middle_kernel,
        out_shape=(
            MAP,
            jax.ShapeDtypeStruct((DEPTH, PX, C), BF),
            jax.ShapeDtypeStruct((DEPTH, PX, C), F32),
            SENT,
        ),
        in_specs=[any_spec(), any_spec(), vmem_spec(), any_spec(), any_spec()],
        out_specs=(vmem_spec(),) * 4,
        scratch_shapes=weight_scratch()
        + [
            pltpu.VMEM((PX, C), BF),
            pltpu.VMEM((PX, C), BF),
            pltpu.VMEM((3, PAD, C), BF),
            pltpu.SemaphoreType.DMA((3, DEPTH)),
            pltpu.SemaphoreType.DMA((2,)),
        ],
        compiler_params=params(),
        name="middle",
    )(images, cot, recv, a, b)


def last(cot, recv, xs, conv, a, b):
    return pl.pallas_call(
        last_kernel,
        out_shape=SENT,
        in_specs=[any_spec(), vmem_spec(), any_spec(), any_spec(), any_spec(), any_spec()],
        out_specs=vmem_spec(),
        scratch_shapes=weight_scratch()
        + [
            pltpu.VMEM((DEPTH, PX, C), BF),
            pltpu.VMEM((DEPTH, PX, C), F32),
            pltpu.VMEM((PX, C), BF),
            pltpu.VMEM((3, PAD, C), BF),
            pltpu.SemaphoreType.DMA((3, DEPTH)),
            pltpu.SemaphoreType.DMA((2, DEPTH)),
            pltpu.SemaphoreType.DMA,
        ],
        compiler_params=params(),
        name="last",
    )(cot, recv, xs, conv, a, b)


def gradient_kernel(
    r_ref, w_ref, styles_ref, demod_ref, energy_ref, affine_ref,
    keep_ref, give_ref, rows_ref, latent_ref, flip_ref, pad_ref, total_ref,
):
    _, _, core = place()
    parts = [unpack_rows(r_ref[n, 2 * PX : 2 * PX + STAT, :]) for n in range(DEPTH)]
    styles = styles_ref[...]
    demod = demod_ref[...]
    grad_sum = stack_rows([p[1] for p in parts]) * (-0.5) * demod * demod * demod
    squares = styles * styles
    grad_squares = lax.dot_general(
        grad_sum, energy_ref[...], (((1,), (1,)), ((), ())), precision=HI, preferred_element_type=F32
    )
    grad_styles = stack_rows([p[0] for p in parts]) + 2.0 * styles * grad_squares
    index = lax.broadcasted_iota(jnp.int32, (8, C), 0)
    grad_bias = parts[0][2] + parts[1][2] + parts[2][2] + parts[3][2]
    rows_ref[...] = jnp.where(
        index < DEPTH, grad_styles, jnp.where(index == DEPTH, jnp.broadcast_to(grad_bias, (8, C)), 0.0)
    )
    latent_ref[...] = lax.dot_general(
        grad_styles, affine_ref[...], (((1,), (1,)), ((), ())), precision=HI, preferred_element_type=F32
    )
    grad_energy = 2.0 * lax.dot_general(
        squares, grad_sum, (((0,), (0,)), ((), ())), precision=HI, preferred_element_type=F32
    )
    for n in range(DEPTH):
        clear_pads(pad_ref.at[n])
        spread(pad_ref.at[n], r_ref[n, PX : 2 * PX, :].astype(F32))
        flip_ref[:, n * PX : (n + 1) * PX] = r_ref[n, 0:PX, :].astype(F32).T.astype(BF)
    for ky in range(3):
        for kx in range(3):
            tap = ky * 3 + kx
            rhs = jnp.concatenate(
                [pad_ref[n, 2 - kx, (2 - ky) * ROW : (2 - ky) * ROW + PX, :] for n in range(DEPTH)], axis=0
            )
            part = jnp.dot(flip_ref[...], rhs, preferred_element_type=F32)
            at = slice(tap * C, (tap + 1) * C)
            total_ref[at, :] = (part + w_ref[at, :].astype(F32) * grad_energy).astype(BF)
    keep_ref[...] = total_ref[pl.ds(pl.multiple_of(core * HALF, HALF), HALF), :]
    give_ref[...] = total_ref[pl.ds(pl.multiple_of((1 - core) * HALF, HALF), HALF), :]


def gradients(r, w, styles, demod, energy, affine):
    return pl.pallas_call(
        gradient_kernel,
        out_shape=(
            jax.ShapeDtypeStruct((HALF, C), BF),
            jax.ShapeDtypeStruct((HALF, C), BF),
            jax.ShapeDtypeStruct((8, C), F32),
            jax.ShapeDtypeStruct((8, affine.shape[0]), F32),
        ),
        in_specs=[vmem_spec()] * 6,
        out_specs=(vmem_spec(),) * 4,
        scratch_shapes=[
            pltpu.VMEM((C, DEPTH * PX), BF),
            pltpu.VMEM((DEPTH, 3, PAD, C), BF),
            pltpu.VMEM((ROWS, C), BF),
        ],
        compiler_params=params(),
        name="gradients",
    )(r, w, styles, demod, energy, affine)


def body(images, latent, weight, affine, biases, cotangent):
    width = latent.shape[1]
    replicas = lax.axis_size("dp")
    segments = lax.axis_size("segment")
    core = lax.axis_index("dp") % 2
    planes = [list(range(k, k + DEPTH)) for k in range(0, segments, DEPTH)]
    across = [(i, (i + DEPTH) % segments) for i in range(segments)]
    sibling = [(i, i ^ 1) for i in range(replicas)]
    cores = [list(range(k, replicas, 2)) for k in range(2)]
    peers = replicas // 2

    w = weight.reshape(ROWS, C)
    images = images.reshape(DEPTH, PX, C)
    cotangent = cotangent.reshape(DEPTH, PX, C)
    latent8 = jnp.pad(latent, ((0, 8 - DEPTH), (0, 0)))
    latent_all = lax.all_gather(latent, "dp", tiled=True)

    send, styles, demod, energy = prepare(latent8, affine[0], w, biases)
    a = lax.all_to_all(send, "segment", 0, 0, axis_index_groups=planes)
    b = lax.ppermute(a, "dp", sibling)

    act = first(images, a, b)
    arrived = lax.ppermute(act, "segment", across)
    dx, xs, conv, _ = middle(images, cotangent, arrived, a, b)
    returned = lax.ppermute(dx, "segment", across)
    sent = last(cotangent, returned, xs, conv, a, b)

    r = lax.all_to_all(sent, "segment", 0, 0, axis_index_groups=planes)
    keep, give, rows, latent_part = gradients(r, w, styles, demod, energy, affine[0])

    rows_all = lax.all_gather(rows, "dp")
    latent_parts = lax.all_gather(latent_part[:DEPTH], "segment")

    got = lax.ppermute(give, "dp", sibling)
    pair = (keep.astype(F32) + got.astype(F32)).astype(BF).reshape(peers, HALF // peers, C)
    shares = lax.all_to_all(pair, "dp", 0, 0, axis_index_groups=cores)
    share = jnp.sum(shares.astype(F32), axis=0).astype(BF)
    mine = lax.all_to_all(
        jnp.broadcast_to(share[None], (peers,) + share.shape), "dp", 0, 0, axis_index_groups=cores
    ).reshape(HALF, C)
    other = lax.ppermute(mine, "dp", sibling)
    low = jnp.where(core == 0, mine, other)
    high = jnp.where(core == 0, other, mine)
    grad_weight = jnp.concatenate([low, high], axis=0).astype(F32).reshape(weight.shape)

    grad_styles = rows_all[:, :DEPTH].reshape(replicas * DEPTH, C)
    grad_affine = lax.dot_general(latent_all, grad_styles, (((0,), (0,)), ((), ())), precision=HI)
    grad_bias = jnp.sum(rows_all[:, DEPTH], axis=0)
    grad_latent = jnp.sum(latent_parts, axis=0)
    return (grad_weight, grad_affine[None], grad_bias[None], grad_latent)


def solution(mesh):
    placed = (
        P("dp", None, None, None),
        P("dp", None),
        P("segment", None, None, None, None),
        P("segment", None, None),
        P("segment", None),
        P("dp", None, None, None),
    )
    return jax.shard_map(
        body,
        mesh=mesh,
        in_specs=placed,
        out_specs=(
            P("segment", None, None, None, None),
            P("segment", None, None),
            P("segment", None),
            P("dp", None),
        ),
        check_vma=False,
    )
```

```python
import functools
import math

import jax
import jax.numpy as jnp
from jax import lax
from jax.experimental import pallas as pl
from jax.experimental.pallas import tpu as pltpu
from jax.sharding import PartitionSpec as P

GAIN = math.sqrt(2.0)
EPS = 1e-08
BF = jnp.bfloat16
F32 = jnp.float32
C = 256
PX = 256
TAPS = 9
ROWS = TAPS * C
HALF = ROWS // 2
STAT = 16
DEPTH = 4
PEERS = 8
SHARE = HALF // PEERS
ROW = 16
PAD = PX + 2 * ROW
HI = lax.Precision.HIGHEST


def any_spec():
    return pl.BlockSpec(memory_space=pl.ANY)


def vmem_spec():
    return pl.BlockSpec(memory_space=pltpu.VMEM)


def params():
    return pltpu.CompilerParams(vmem_limit_bytes=28 << 20)


def near(value):
    return pltpu.with_memory_space_constraint(value, pltpu.VMEM)


def place():
    seg = lax.axis_index("segment")
    return seg // DEPTH, seg % DEPTH, lax.axis_index("dp") % 2


def split3(value):
    hi = value.astype(BF).astype(F32)
    rest = value - hi
    mid = rest.astype(BF).astype(F32)
    return hi, mid, rest - mid


def pack_rows(values):
    row = lax.broadcasted_iota(jnp.int32, (STAT, C), 0)
    out = jnp.zeros((STAT, C), F32)
    k = 0
    for value in values:
        for part in split3(value):
            out = jnp.where(row == k, jnp.broadcast_to(part, (STAT, C)), out)
            k += 1
    return out.astype(BF)


def unpack_rows(tile):
    t = tile.astype(F32)
    return [t[3 * k : 3 * k + 1] + t[3 * k + 1 : 3 * k + 2] + t[3 * k + 2 : 3 * k + 3] for k in range(3)]


def stack_rows(rows):
    index = lax.broadcasted_iota(jnp.int32, (8, C), 0)
    out = jnp.zeros((8, C), F32)
    for k, row in enumerate(rows):
        out = jnp.where(index == k, jnp.broadcast_to(row, (8, C)), out)
    return out


def prepare_kernel(latent_ref, affine_ref, w_ref, bias_ref, send_ref, styles_ref, demod_ref, energy_ref, rows_ref, tile_ref, sem):
    _, _, core = place()
    mine = pl.ds(pl.multiple_of(core * HALF, HALF), HALF)
    copies = [
        pltpu.make_async_copy(w_ref.at[mine], send_ref.at[k, pl.ds(0, HALF)], sem.at[k]) for k in range(DEPTH)
    ]
    for copy in copies:
        copy.start()
    rows_ref[...] = jnp.zeros_like(rows_ref)
    rows_ref[0:DEPTH, :] = latent_ref[...]
    styles = jnp.dot(rows_ref[...], affine_ref[...], precision=HI, preferred_element_type=F32) + 1.0
    energy = jnp.zeros((C, C), F32)
    for tap in range(TAPS):
        part = w_ref[tap * C : (tap + 1) * C, :].astype(F32)
        energy += part * part
    energy_ref[...] = energy
    demod = lax.rsqrt(jnp.dot(styles * styles, energy, precision=HI, preferred_element_type=F32) + EPS)
    styles_ref[...] = styles
    demod_ref[...] = demod
    for k in range(DEPTH):
        tile_ref[k] = pack_rows([styles[k : k + 1], demod[k : k + 1], bias_ref[...]])
    stats = [
        pltpu.make_async_copy(tile_ref.at[k], send_ref.at[k, pl.ds(HALF, STAT)], sem.at[DEPTH + k])
        for k in range(DEPTH)
    ]
    for copy in stats:
        copy.start()
    for copy in copies + stats:
        copy.wait()


def prepare(latent, affine, w, bias):
    return pl.pallas_call(
        prepare_kernel,
        out_shape=(
            jax.ShapeDtypeStruct((DEPTH, HALF + STAT, C), BF),
            jax.ShapeDtypeStruct((8, C), F32),
            jax.ShapeDtypeStruct((8, C), F32),
            jax.ShapeDtypeStruct((C, C), F32),
        ),
        in_specs=[vmem_spec()] * 4,
        out_specs=(any_spec(), vmem_spec(), vmem_spec(), vmem_spec()),
        scratch_shapes=[
            pltpu.VMEM((8, latent.shape[1]), F32),
            pltpu.VMEM((DEPTH, STAT, C), BF),
            pltpu.SemaphoreType.DMA((2 * DEPTH,)),
        ],
        compiler_params=params(),
        name="prepare",
    )(latent, affine, w, bias)


def weight_copies(a_any, b_any, w_buf, stat_buf, sem):
    _, _, core = place()
    mine = pl.ds(pl.multiple_of(core * HALF, HALF), HALF)
    other = pl.ds(pl.multiple_of((1 - core) * HALF, HALF), HALF)
    return [
        (
            pltpu.make_async_copy(a_any.at[l, pl.ds(HALF, STAT)], stat_buf.at[l], sem.at[0, l]),
            pltpu.make_async_copy(a_any.at[l, pl.ds(0, HALF)], w_buf.at[l, mine], sem.at[1, l]),
            pltpu.make_async_copy(b_any.at[l, pl.ds(0, HALF)], w_buf.at[l, other], sem.at[2, l]),
        )
        for l in range(DEPTH)
    ]


def clear_pads(pad_ref):
    for k in range(3):
        pad_ref[k, 0:ROW, :] = jnp.zeros((ROW, C), BF)
        pad_ref[k, ROW + PX : PAD, :] = jnp.zeros((ROW, C), BF)


def spread(pad_ref, value):
    column = lax.broadcasted_iota(jnp.int32, (PX, C), 0) % ROW
    pad_ref[1, ROW : ROW + PX, :] = value.astype(BF)
    pad_ref[0, ROW : ROW + PX, :] = jnp.where(column == 0, 0.0, pltpu.roll(value, 1, 0)).astype(BF)
    pad_ref[2, ROW : ROW + PX, :] = jnp.where(column == ROW - 1, 0.0, pltpu.roll(value, PX - 1, 0)).astype(BF)


def forward_layer(x, l, w_buf, stat, pad_ref):
    styles, demod, bias = stat
    scaled = (x.astype(F32) * styles).astype(BF).astype(F32)
    spread(pad_ref, scaled)
    conv = None
    for ky in range(3):
        lhs = jnp.concatenate([pad_ref[kx, ky * ROW : ky * ROW + PX, :] for kx in range(3)], axis=1)
        part = jnp.dot(lhs, w_buf[l, ky * 3 * C : (ky + 1) * 3 * C, :], preferred_element_type=F32)
        conv = part if conv is None else conv + part
    return conv


def activate(conv, stat):
    _, demod, bias = stat
    hidden = conv * demod + bias
    return (GAIN * hidden * (0.6 + 0.4 * jnp.tanh(hidden))).astype(BF)


def backward_layer(upstream, x, conv, l, w_buf, stat, pad_ref, send_ref):
    styles, demod, bias = stat
    hidden = conv * demod + bias
    t = jnp.tanh(hidden)
    dh = upstream.astype(F32) * (GAIN * (0.6 + 0.4 * t + 0.4 * hidden * (1.0 - t * t)))
    grad_bias = jnp.sum(dh, axis=0, keepdims=True)
    grad_demod = jnp.sum(dh * conv, axis=0, keepdims=True)
    grad_conv = (dh * demod).astype(BF).astype(F32)
    spread(pad_ref, grad_conv)
    send_ref[l, PX : 2 * PX, :] = pad_ref[1, ROW : ROW + PX, :]
    total = None
    for ky in range(3):
        for kx in range(3):
            lhs = pad_ref[2 - kx, (2 - ky) * ROW : (2 - ky) * ROW + PX, :]
            tap = ky * 3 + kx
            part = lax.dot_general(
                lhs, w_buf[l, tap * C : (tap + 1) * C, :], (((1,), (1,)), ((), ())), preferred_element_type=F32
            )
            total = part if total is None else total + part
    grad_scaled = total.astype(BF).astype(F32)
    xf = x.astype(F32)
    grad_styles = jnp.sum(grad_scaled * xf, axis=0, keepdims=True)
    send_ref[l, 0:PX, :] = (xf * styles).astype(BF)
    send_ref[l, 2 * PX : 2 * PX + STAT, :] = pack_rows([grad_styles, grad_demod, grad_bias])
    return (grad_scaled * styles).astype(BF)


def first_kernel(images_any, a_any, b_any, out_ref, w_buf, stat_buf, x_buf, pad_ref, sem, x_sem):
    _, z, _ = place()
    x_copy = pltpu.make_async_copy(images_any.at[z], x_buf, x_sem)
    x_copy.start()
    copies = weight_copies(a_any, b_any, w_buf, stat_buf, sem)
    for group in copies:
        for copy in group:
            copy.start()
    clear_pads(pad_ref)
    x_copy.wait()
    x = x_buf[...]
    for l in range(DEPTH):
        for copy in copies[l]:
            copy.wait()
        stat = unpack_rows(stat_buf[l])
        x = activate(forward_layer(x, l, w_buf, stat, pad_ref), stat)
    out_ref[...] = x


def middle_kernel(
    images_any, cot_any, recv_ref, a_any, b_any, dx_ref, xs_ref, conv_ref, send_ref,
    w_buf, stat_buf, x_buf, u_buf, pad_ref, sem, x_sem,
):
    half, z, _ = place()
    x_copy = pltpu.make_async_copy(images_any.at[z], x_buf, x_sem.at[0])
    u_copy = pltpu.make_async_copy(cot_any.at[z], u_buf, x_sem.at[1])
    x_copy.start()
    copies = weight_copies(a_any, b_any, w_buf, stat_buf, sem)
    for group in copies:
        for copy in group:
            copy.start()
    u_copy.start()
    clear_pads(pad_ref)
    x_copy.wait()
    x = jnp.where(half == 1, recv_ref[...], x_buf[...])
    stats = []
    for l in range(DEPTH):
        for copy in copies[l]:
            copy.wait()
        stats.append(unpack_rows(stat_buf[l]))
        xs_ref[l] = x
        conv = forward_layer(x, l, w_buf, stats[l], pad_ref)
        conv_ref[l] = conv
        if l < DEPTH - 1:
            x = activate(conv, stats[l])
    u_copy.wait()
    upstream = u_buf[...]
    for l in reversed(range(DEPTH)):
        upstream = backward_layer(upstream, xs_ref[l], conv_ref[l], l, w_buf, stats[l], pad_ref, send_ref)
    dx_ref[...] = upstream


def last_kernel(
    cot_any, recv_ref, xs_any, conv_any, a_any, b_any, send_ref,
    w_buf, stat_buf, xs_buf, conv_buf, u_buf, pad_ref, sem, s_sem, u_sem,
):
    half, z, _ = place()
    u_copy = pltpu.make_async_copy(cot_any.at[z], u_buf, u_sem)
    u_copy.start()
    copies = weight_copies(a_any, b_any, w_buf, stat_buf, sem)
    saves = [
        (
            pltpu.make_async_copy(xs_any.at[l], xs_buf.at[l], s_sem.at[0, l]),
            pltpu.make_async_copy(conv_any.at[l], conv_buf.at[l], s_sem.at[1, l]),
        )
        for l in range(DEPTH)
    ]
    for l in reversed(range(DEPTH)):
        for copy in saves[l] + copies[l]:
            copy.start()
    clear_pads(pad_ref)
    u_copy.wait()
    upstream = jnp.where(half == 1, u_buf[...], recv_ref[...])
    for l in reversed(range(DEPTH)):
        for copy in saves[l] + copies[l]:
            copy.wait()
        stat = unpack_rows(stat_buf[l])
        upstream = backward_layer(upstream, xs_buf[l], conv_buf[l], l, w_buf, stat, pad_ref, send_ref)


def weight_scratch():
    return [pltpu.VMEM((DEPTH, ROWS, C), BF), pltpu.VMEM((DEPTH, STAT, C), BF)]


MAP = jax.ShapeDtypeStruct((PX, C), BF)
SENT = jax.ShapeDtypeStruct((DEPTH, 2 * PX + STAT, C), BF)


def first(images, a, b):
    return pl.pallas_call(
        first_kernel,
        out_shape=MAP,
        in_specs=[any_spec(), vmem_spec(), vmem_spec()],
        out_specs=vmem_spec(),
        scratch_shapes=weight_scratch()
        + [
            pltpu.VMEM((PX, C), BF),
            pltpu.VMEM((3, PAD, C), BF),
            pltpu.SemaphoreType.DMA((3, DEPTH)),
            pltpu.SemaphoreType.DMA,
        ],
        compiler_params=params(),
        name="first",
    )(images, a, b)


def middle(images, cot, recv, a, b):
    return pl.pallas_call(
        middle_kernel,
        out_shape=(
            MAP,
            jax.ShapeDtypeStruct((DEPTH, PX, C), BF),
            jax.ShapeDtypeStruct((DEPTH, PX, C), F32),
            SENT,
        ),
        in_specs=[any_spec(), any_spec(), vmem_spec(), vmem_spec(), vmem_spec()],
        out_specs=(vmem_spec(),) * 4,
        scratch_shapes=weight_scratch()
        + [
            pltpu.VMEM((PX, C), BF),
            pltpu.VMEM((PX, C), BF),
            pltpu.VMEM((3, PAD, C), BF),
            pltpu.SemaphoreType.DMA((3, DEPTH)),
            pltpu.SemaphoreType.DMA((2,)),
        ],
        compiler_params=params(),
        name="middle",
    )(images, cot, recv, a, b)


def last(cot, recv, xs, conv, a, b):
    return pl.pallas_call(
        last_kernel,
        out_shape=SENT,
        in_specs=[any_spec(), vmem_spec(), any_spec(), any_spec(), vmem_spec(), vmem_spec()],
        out_specs=vmem_spec(),
        scratch_shapes=weight_scratch()
        + [
            pltpu.VMEM((DEPTH, PX, C), BF),
            pltpu.VMEM((DEPTH, PX, C), F32),
            pltpu.VMEM((PX, C), BF),
            pltpu.VMEM((3, PAD, C), BF),
            pltpu.SemaphoreType.DMA((3, DEPTH)),
            pltpu.SemaphoreType.DMA((2, DEPTH)),
            pltpu.SemaphoreType.DMA,
        ],
        compiler_params=params(),
        name="last",
    )(cot, recv, xs, conv, a, b)


def gradient_kernel(
    r_ref, w_ref, styles_ref, demod_ref, energy_ref, affine_ref, latent_ref,
    keep_ref, give_ref, extra_ref, grad_latent_ref, flip_ref, pad_ref, total_ref, rows_ref,
):
    _, _, core = place()
    parts = [unpack_rows(r_ref[n, 2 * PX : 2 * PX + STAT, :]) for n in range(DEPTH)]
    styles = styles_ref[...]
    demod = demod_ref[...]
    grad_sum = stack_rows([p[1] for p in parts]) * (-0.5) * demod * demod * demod
    squares = styles * styles
    grad_squares = lax.dot_general(
        grad_sum, energy_ref[...], (((1,), (1,)), ((), ())), precision=HI, preferred_element_type=F32
    )
    grad_styles = stack_rows([p[0] for p in parts]) + 2.0 * styles * grad_squares
    grad_bias = parts[0][2] + parts[1][2] + parts[2][2] + parts[3][2]
    rows_ref[...] = jnp.zeros_like(rows_ref)
    rows_ref[0:DEPTH, :] = grad_styles[0:DEPTH]
    rows_ref[DEPTH : DEPTH + 1, :] = grad_bias
    rows_ref[8 : 8 + DEPTH, :] = latent_ref[:, 0:C]
    rows_ref[8 + DEPTH : 8 + 2 * DEPTH, :] = latent_ref[:, C : 2 * C]
    extra = rows_ref[...].astype(BF)
    extra_ref[...] = extra
    give_ref[HALF : HALF + STAT, :] = extra
    grad_latent_ref[...] = lax.dot_general(
        grad_styles, affine_ref[...], (((1,), (1,)), ((), ())), precision=HI, preferred_element_type=F32
    )
    grad_energy = 2.0 * lax.dot_general(
        squares, grad_sum, (((0,), (0,)), ((), ())), precision=HI, preferred_element_type=F32
    )
    for n in range(DEPTH):
        clear_pads(pad_ref.at[n])
        spread(pad_ref.at[n], r_ref[n, PX : 2 * PX, :].astype(F32))
        flip_ref[:, n * PX : (n + 1) * PX] = r_ref[n, 0:PX, :].astype(F32).T.astype(BF)
    for ky in range(3):
        for kx in range(3):
            tap = ky * 3 + kx
            rhs = jnp.concatenate(
                [pad_ref[n, 2 - kx, (2 - ky) * ROW : (2 - ky) * ROW + PX, :] for n in range(DEPTH)], axis=0
            )
            part = jnp.dot(flip_ref[...], rhs, preferred_element_type=F32)
            at = slice(tap * C, (tap + 1) * C)
            total_ref[at, :] = (part + w_ref[at, :].astype(F32) * grad_energy).astype(BF)
    keep_ref[...] = total_ref[pl.ds(pl.multiple_of(core * HALF, HALF), HALF), :]
    give_ref[0:HALF, :] = total_ref[pl.ds(pl.multiple_of((1 - core) * HALF, HALF), HALF), :]


def gradients(r, w, styles, demod, energy, affine, latent):
    return pl.pallas_call(
        gradient_kernel,
        out_shape=(
            jax.ShapeDtypeStruct((HALF, C), BF),
            jax.ShapeDtypeStruct((HALF + STAT, C), BF),
            jax.ShapeDtypeStruct((STAT, C), BF),
            jax.ShapeDtypeStruct((8, affine.shape[0]), F32),
        ),
        in_specs=[vmem_spec()] * 7,
        out_specs=(vmem_spec(),) * 4,
        scratch_shapes=[
            pltpu.VMEM((C, DEPTH * PX), BF),
            pltpu.VMEM((DEPTH, 3, PAD, C), BF),
            pltpu.VMEM((ROWS, C), BF),
            pltpu.VMEM((STAT, C), F32),
        ],
        compiler_params=params(),
        name="gradients",
    )(r, w, styles, demod, energy, affine, latent)


def pair_kernel(keep_ref, extra_ref, got_ref, out_ref):
    for k in range(PEERS):
        at = slice(k * SHARE, (k + 1) * SHARE)
        out_ref[k, 0:SHARE, :] = (keep_ref[at, :].astype(F32) + got_ref[at, :].astype(F32)).astype(BF)
        out_ref[k, SHARE : SHARE + STAT, :] = extra_ref[...]
        out_ref[k, SHARE + STAT : SHARE + 2 * STAT, :] = got_ref[HALF : HALF + STAT, :]


def pair(keep, extra, got):
    return pl.pallas_call(
        pair_kernel,
        out_shape=jax.ShapeDtypeStruct((PEERS, SHARE + 2 * STAT, C), BF),
        in_specs=[vmem_spec()] * 3,
        out_specs=vmem_spec(),
        compiler_params=params(),
        name="pair",
    )(keep, extra, got)


def share_kernel(shares_ref, out_ref):
    total = shares_ref[0, 0:SHARE, :].astype(F32)
    for k in range(1, PEERS):
        total += shares_ref[k, 0:SHARE, :].astype(F32)
    total = total.astype(BF)
    for k in range(PEERS):
        out_ref[k] = total


def share(shares):
    return pl.pallas_call(
        share_kernel,
        out_shape=jax.ShapeDtypeStruct((PEERS, SHARE, C), BF),
        in_specs=[vmem_spec()],
        out_specs=vmem_spec(),
        compiler_params=params(),
        name="share",
    )(shares)


def affine_kernel(shares_ref, affine_ref, bias_ref, grads_ref, low_ref, high_ref):
    row = lax.broadcasted_iota(jnp.int32, (STAT, C), 0)
    bias = jnp.zeros((1, C), F32)
    for k in range(2 * PEERS):
        start = SHARE + (k % 2) * STAT
        tile = shares_ref[k // 2, start : start + STAT, :].astype(F32)
        bias += tile[DEPTH : DEPTH + 1]
        at = slice(k * STAT, (k + 1) * STAT)
        grads_ref[at, :] = jnp.where(row < DEPTH, tile, 0.0).astype(BF)
        low_ref[at, :] = pltpu.roll(tile, 8, 0).astype(BF)
        high_ref[at, :] = pltpu.roll(tile, 4, 0).astype(BF)
    bias_ref[...] = bias
    for k, ref in enumerate((low_ref, high_ref)):
        affine_ref[k * C : (k + 1) * C, :] = lax.dot_general(
            ref[...], grads_ref[...], (((0,), (0,)), ((), ())), preferred_element_type=F32
        )


def affine_gradient(shares, width):
    return pl.pallas_call(
        affine_kernel,
        out_shape=(jax.ShapeDtypeStruct((width, C), F32), jax.ShapeDtypeStruct((1, C), F32)),
        in_specs=[vmem_spec()],
        out_specs=(vmem_spec(), vmem_spec()),
        scratch_shapes=[pltpu.VMEM((2 * PEERS * STAT, C), BF)] * 3,
        compiler_params=params(),
        name="affine",
    )(shares)


def body(images, latent, weight, affine, biases, cotangent):
    width = latent.shape[1]
    replicas = lax.axis_size("dp")
    segments = lax.axis_size("segment")
    core = lax.axis_index("dp") % 2
    planes = [list(range(k, k + DEPTH)) for k in range(0, segments, DEPTH)]
    across = [(i, (i + DEPTH) % segments) for i in range(segments)]
    sibling = [(i, i ^ 1) for i in range(replicas)]
    cores = [list(range(k, replicas, 2)) for k in range(2)]

    w = weight.reshape(ROWS, C)
    images = images.reshape(DEPTH, PX, C)
    cotangent = cotangent.reshape(DEPTH, PX, C)

    send, styles, demod, energy = prepare(latent, affine[0], w, biases)
    a = lax.all_to_all(send, "segment", 0, 0, axis_index_groups=planes)
    b = near(lax.ppermute(a, "dp", sibling))
    a = near(a)

    act = first(images, a, b)
    arrived = near(lax.ppermute(act, "segment", across))
    dx, xs, conv, _ = middle(images, cotangent, arrived, a, b)
    returned = near(lax.ppermute(dx, "segment", across))
    sent = last(cotangent, returned, xs, conv, a, b)

    r = near(lax.all_to_all(sent, "segment", 0, 0, axis_index_groups=planes))
    keep, give, extra, latent_part = gradients(r, w, styles, demod, energy, affine[0], latent)

    got = near(lax.ppermute(give, "dp", sibling))
    part = latent_part[:DEPTH]
    part = part + lax.ppermute(part, "segment", across)
    shared = pair(keep, extra, got)
    shared, part = lax.optimization_barrier((shared, part))
    shares = near(lax.all_to_all(shared, "dp", 0, 0, axis_index_groups=cores))
    part = part + lax.ppermute(part, "segment", [(i, i ^ 1) for i in range(segments)])
    spread_share = share(shares)
    spread_share, part = lax.optimization_barrier((spread_share, part))
    mine = lax.all_to_all(spread_share, "dp", 0, 0, axis_index_groups=cores).reshape(HALF, C)
    grad_latent = part + lax.ppermute(part, "segment", [(i, i ^ 2) for i in range(segments)])
    grad_affine, grad_bias = affine_gradient(shares, width)
    other = lax.ppermute(mine, "dp", sibling)
    low = jnp.where(core == 0, mine, other)
    high = jnp.where(core == 0, other, mine)
    grad_weight = jnp.concatenate([low, high], axis=0).astype(F32).reshape(weight.shape)
    return (grad_weight, grad_affine[None], grad_bias, grad_latent)


def solution(mesh):
    placed = (
        P("dp", None, None, None),
        P("dp", None),
        P("segment", None, None, None, None),
        P("segment", None, None),
        P("segment", None),
        P("dp", None, None, None),
    )
    return jax.shard_map(
        body,
        mesh=mesh,
        in_specs=placed,
        out_specs=(
            P("segment", None, None, None, None),
            P("segment", None, None),
            P("segment", None),
            P("dp", None),
        ),
        check_vma=False,
    )
```

```python
import functools
import math

import jax
import jax.numpy as jnp
from jax import lax
from jax.experimental import pallas as pl
from jax.experimental.pallas import tpu as pltpu
from jax.sharding import PartitionSpec as P

GAIN = math.sqrt(2.0)
EPS = 1e-08
BF = jnp.bfloat16
F32 = jnp.float32
C = 256
PX = 256
TAPS = 9
ROWS = TAPS * C
HALF = ROWS // 2
STAT = 16
DEPTH = 4
PEERS = 8
SHARE = HALF // PEERS
ROW = 16
PAD = PX + 2 * ROW
HI = lax.Precision.HIGHEST


def any_spec():
    return pl.BlockSpec(memory_space=pl.ANY)


def vmem_spec():
    return pl.BlockSpec(memory_space=pltpu.VMEM)


def params():
    return pltpu.CompilerParams(vmem_limit_bytes=28 << 20)


def near(value):
    return pltpu.with_memory_space_constraint(value, pltpu.VMEM)


def place():
    seg = lax.axis_index("segment")
    return seg // DEPTH, seg % DEPTH, lax.axis_index("dp") % 2


def split3(value):
    hi = value.astype(BF).astype(F32)
    rest = value - hi
    mid = rest.astype(BF).astype(F32)
    return hi, mid, rest - mid


def pack_rows(values):
    row = lax.broadcasted_iota(jnp.int32, (STAT, C), 0)
    out = jnp.zeros((STAT, C), F32)
    k = 0
    for value in values:
        for part in split3(value):
            out = jnp.where(row == k, jnp.broadcast_to(part, (STAT, C)), out)
            k += 1
    return out.astype(BF)


def unpack_rows(tile):
    t = tile.astype(F32)
    return [t[3 * k : 3 * k + 1] + t[3 * k + 1 : 3 * k + 2] + t[3 * k + 2 : 3 * k + 3] for k in range(3)]


def stack_rows(rows):
    index = lax.broadcasted_iota(jnp.int32, (8, C), 0)
    out = jnp.zeros((8, C), F32)
    for k, row in enumerate(rows):
        out = jnp.where(index == k, jnp.broadcast_to(row, (8, C)), out)
    return out


def prepare_kernel(
    latent_hbm, affine_hbm, w_hbm, bias_hbm, send_ref, styles_ref, demod_ref, energy_ref,
    rows_ref, affine_ref, w_ref, bias_ref, sem,
):
    _, _, core = place()
    mine = pl.ds(pl.multiple_of(core * HALF, HALF), HALF)
    rows_ref[...] = jnp.zeros_like(rows_ref)
    third = ROWS // 3
    loads = [
        pltpu.make_async_copy(affine_hbm, affine_ref, sem.at[0]),
        pltpu.make_async_copy(latent_hbm, rows_ref.at[pl.ds(0, DEPTH)], sem.at[1]),
        pltpu.make_async_copy(bias_hbm, bias_ref, sem.at[2]),
    ] + [
        pltpu.make_async_copy(w_hbm.at[pl.ds(k * third, third)], w_ref.at[pl.ds(k * third, third)], sem.at[3 + k])
        for k in range(3)
    ]
    sends = [
        pltpu.make_async_copy(w_hbm.at[mine], send_ref.at[k, pl.ds(0, HALF)], sem.at[6 + k]) for k in range(DEPTH)
    ]
    for copy in loads + sends:
        copy.start()
    for copy in loads[:3]:
        copy.wait()
    styles = jnp.dot(rows_ref[...], affine_ref[...], precision=HI, preferred_element_type=F32) + 1.0
    energy = jnp.zeros((C, C), F32)
    for tap in range(TAPS):
        if tap % 3 == 0:
            loads[3 + tap // 3].wait()
        part = w_ref[tap * C : (tap + 1) * C, :].astype(F32)
        energy += part * part
    energy_ref[...] = energy
    demod = lax.rsqrt(jnp.dot(styles * styles, energy, precision=HI, preferred_element_type=F32) + EPS)
    styles_ref[...] = styles
    demod_ref[...] = demod
    for k in range(DEPTH):
        send_ref[k, HALF : HALF + STAT, :] = pack_rows([styles[k : k + 1], demod[k : k + 1], bias_ref[...]])
    for copy in sends:
        copy.wait()


def prepare(latent, affine, w, bias):
    far = [pltpu.with_memory_space_constraint(value, pltpu.HBM) for value in (latent, affine, w, bias)]
    return pl.pallas_call(
        prepare_kernel,
        out_shape=(
            jax.ShapeDtypeStruct((DEPTH, HALF + STAT, C), BF),
            jax.ShapeDtypeStruct((8, C), F32),
            jax.ShapeDtypeStruct((8, C), F32),
            jax.ShapeDtypeStruct((C, C), F32),
        ),
        in_specs=[pl.BlockSpec(memory_space=pltpu.HBM)] * 4,
        out_specs=(vmem_spec(),) * 4,
        scratch_shapes=[
            pltpu.VMEM((8, latent.shape[1]), F32),
            pltpu.VMEM(affine.shape, F32),
            pltpu.VMEM((ROWS, C), BF),
            pltpu.VMEM((1, C), F32),
            pltpu.SemaphoreType.DMA((6 + DEPTH,)),
        ],
        compiler_params=params(),
        name="prepare",
    )(*far)


def weight_copies(a_any, b_any, w_buf, stat_buf, sem):
    _, _, core = place()
    mine = pl.ds(pl.multiple_of(core * HALF, HALF), HALF)
    other = pl.ds(pl.multiple_of((1 - core) * HALF, HALF), HALF)
    return [
        (
            pltpu.make_async_copy(a_any.at[l, pl.ds(HALF, STAT)], stat_buf.at[l], sem.at[0, l]),
            pltpu.make_async_copy(a_any.at[l, pl.ds(0, HALF)], w_buf.at[l, mine], sem.at[1, l]),
            pltpu.make_async_copy(b_any.at[l, pl.ds(0, HALF)], w_buf.at[l, other], sem.at[2, l]),
        )
        for l in range(DEPTH)
    ]


def clear_pads(pad_ref):
    for k in range(3):
        pad_ref[k, 0:ROW, :] = jnp.zeros((ROW, C), BF)
        pad_ref[k, ROW + PX : PAD, :] = jnp.zeros((ROW, C), BF)


def spread(pad_ref, value):
    column = lax.broadcasted_iota(jnp.int32, (PX, C), 0) % ROW
    pad_ref[1, ROW : ROW + PX, :] = value.astype(BF)
    pad_ref[0, ROW : ROW + PX, :] = jnp.where(column == 0, 0.0, pltpu.roll(value, 1, 0)).astype(BF)
    pad_ref[2, ROW : ROW + PX, :] = jnp.where(column == ROW - 1, 0.0, pltpu.roll(value, PX - 1, 0)).astype(BF)


def forward_layer(x, l, w_ref, stat, pad_ref):
    styles, demod, bias = stat
    spread(pad_ref, (x.astype(F32) * styles).astype(BF).astype(F32))
    lhs = jnp.concatenate(
        [pad_ref[kx, ky * ROW : ky * ROW + PX, :] for ky in range(3) for kx in range(3)], axis=1
    )
    return jnp.dot(lhs, w_ref[l], preferred_element_type=F32)


def activate(conv, stat):
    _, demod, bias = stat
    hidden = conv * demod + bias
    return (GAIN * hidden * (0.6 + 0.4 * jnp.tanh(hidden))).astype(BF)


def backward_layer(upstream, x, conv, l, flip_ref, stat, pad_ref, send_ref):
    styles, demod, bias = stat
    hidden = conv * demod + bias
    t = jnp.tanh(hidden)
    dh = upstream.astype(F32) * (GAIN * (0.6 + 0.4 * t + 0.4 * hidden * (1.0 - t * t)))
    grad_bias = jnp.sum(dh, axis=0, keepdims=True)
    grad_demod = jnp.sum(dh * conv, axis=0, keepdims=True)
    grad_conv = (dh * demod).astype(BF).astype(F32)
    spread(pad_ref, grad_conv)
    send_ref[l, PX : 2 * PX, :] = pad_ref[1, ROW : ROW + PX, :]
    lhs = jnp.concatenate(
        [pad_ref[2 - kx, (2 - ky) * ROW : (2 - ky) * ROW + PX, :] for ky in range(3) for kx in range(3)], axis=1
    )
    total = jnp.dot(lhs, flip_ref[l], preferred_element_type=F32)
    grad_scaled = total.astype(BF).astype(F32)
    xf = x.astype(F32)
    grad_styles = jnp.sum(grad_scaled * xf, axis=0, keepdims=True)
    send_ref[l, 0:PX, :] = (xf * styles).astype(BF)
    send_ref[l, 2 * PX : 2 * PX + STAT, :] = pack_rows([grad_styles, grad_demod, grad_bias])
    return (grad_scaled * styles).astype(BF)


def first_kernel(images_any, a_ref, b_ref, out_ref, w_ref, stat_ref, x_buf, pad_ref, sem, x_sem):
    _, z, _ = place()
    x_copy = pltpu.make_async_copy(images_any.at[z], x_buf, x_sem)
    x_copy.start()
    copies = weight_copies(a_ref, b_ref, w_ref, stat_ref, sem)
    for group in copies:
        for copy in group:
            copy.start()
    clear_pads(pad_ref)
    x_copy.wait()
    x = x_buf[...]
    for l in range(DEPTH):
        for copy in copies[l]:
            copy.wait()
        stat = unpack_rows(stat_ref[l])
        x = activate(forward_layer(x, l, w_ref, stat, pad_ref), stat)
    out_ref[...] = x


def flip_kernel(w_ref, flip_ref):
    for l in range(DEPTH):
        for tap in range(TAPS):
            at = slice(tap * C, (tap + 1) * C)
            flip_ref[l, at, :] = w_ref[l, at, :].T


def middle_kernel(
    images_any, cot_any, recv_ref, w_ref, flip_ref, stat_ref, dx_ref, xs_ref, conv_ref, send_ref,
    x_buf, u_buf, pad_ref, x_sem,
):
    half, z, _ = place()
    x_copy = pltpu.make_async_copy(images_any.at[z], x_buf, x_sem.at[0])
    u_copy = pltpu.make_async_copy(cot_any.at[z], u_buf, x_sem.at[1])
    x_copy.start()
    u_copy.start()
    clear_pads(pad_ref)
    x_copy.wait()
    x = jnp.where(half == 1, recv_ref[...], x_buf[...])
    stats = []
    for l in range(DEPTH):
        stats.append(unpack_rows(stat_ref[l]))
        xs_ref[l] = x
        conv = forward_layer(x, l, w_ref, stats[l], pad_ref)
        conv_ref[l] = conv
        if l < DEPTH - 1:
            x = activate(conv, stats[l])
    u_copy.wait()
    upstream = u_buf[...]
    for l in reversed(range(DEPTH)):
        upstream = backward_layer(upstream, xs_ref[l], conv_ref[l], l, flip_ref, stats[l], pad_ref, send_ref)
    dx_ref[...] = upstream


def last_kernel(cot_any, recv_ref, xs_ref, conv_ref, flip_ref, stat_ref, send_ref, u_buf, pad_ref, u_sem):
    half, z, _ = place()
    u_copy = pltpu.make_async_copy(cot_any.at[z], u_buf, u_sem)
    u_copy.start()
    clear_pads(pad_ref)
    u_copy.wait()
    upstream = jnp.where(half == 1, u_buf[...], recv_ref[...])
    for l in reversed(range(DEPTH)):
        stat = unpack_rows(stat_ref[l])
        upstream = backward_layer(upstream, xs_ref[l], conv_ref[l], l, flip_ref, stat, pad_ref, send_ref)


MAP = jax.ShapeDtypeStruct((PX, C), BF)
KERNELS = jax.ShapeDtypeStruct((DEPTH, ROWS, C), BF)
SENT = jax.ShapeDtypeStruct((DEPTH, 2 * PX + STAT, C), BF)


def first(images, a, b):
    return pl.pallas_call(
        first_kernel,
        out_shape=(MAP, KERNELS, jax.ShapeDtypeStruct((DEPTH, STAT, C), BF)),
        in_specs=[any_spec(), vmem_spec(), vmem_spec()],
        out_specs=(vmem_spec(),) * 3,
        scratch_shapes=[
            pltpu.VMEM((PX, C), BF),
            pltpu.VMEM((3, PAD, C), BF),
            pltpu.SemaphoreType.DMA((3, DEPTH)),
            pltpu.SemaphoreType.DMA,
        ],
        compiler_params=params(),
        name="first",
    )(images, a, b)


def flip(w):
    return pl.pallas_call(
        flip_kernel,
        out_shape=KERNELS,
        in_specs=[vmem_spec()],
        out_specs=vmem_spec(),
        compiler_params=params(),
        name="flip",
    )(w)


def middle(images, cot, recv, w, flipped, stat):
    return pl.pallas_call(
        middle_kernel,
        out_shape=(
            MAP,
            jax.ShapeDtypeStruct((DEPTH, PX, C), BF),
            jax.ShapeDtypeStruct((DEPTH, PX, C), F32),
            SENT,
        ),
        in_specs=[any_spec(), any_spec()] + [vmem_spec()] * 4,
        out_specs=(vmem_spec(),) * 4,
        scratch_shapes=[
            pltpu.VMEM((PX, C), BF),
            pltpu.VMEM((PX, C), BF),
            pltpu.VMEM((3, PAD, C), BF),
            pltpu.SemaphoreType.DMA((2,)),
        ],
        compiler_params=params(),
        name="middle",
    )(images, cot, recv, w, flipped, stat)


def last(cot, recv, xs, conv, flipped, stat):
    return pl.pallas_call(
        last_kernel,
        out_shape=SENT,
        in_specs=[any_spec()] + [vmem_spec()] * 5,
        out_specs=vmem_spec(),
        scratch_shapes=[
            pltpu.VMEM((PX, C), BF),
            pltpu.VMEM((3, PAD, C), BF),
            pltpu.SemaphoreType.DMA,
        ],
        compiler_params=params(),
        name="last",
    )(cot, recv, xs, conv, flipped, stat)


def gradient_kernel(
    r_ref, w_ref, styles_ref, demod_ref, energy_ref, affine_ref, latent_ref,
    keep_ref, give_ref, extra_ref, grad_latent_ref, flip_ref, pad_ref, total_ref, rows_ref,
):
    _, _, core = place()
    parts = [unpack_rows(r_ref[n, 2 * PX : 2 * PX + STAT, :]) for n in range(DEPTH)]
    styles = styles_ref[...]
    demod = demod_ref[...]
    grad_sum = stack_rows([p[1] for p in parts]) * (-0.5) * demod * demod * demod
    squares = styles * styles
    grad_squares = lax.dot_general(
        grad_sum, energy_ref[...], (((1,), (1,)), ((), ())), precision=HI, preferred_element_type=F32
    )
    grad_styles = stack_rows([p[0] for p in parts]) + 2.0 * styles * grad_squares
    grad_bias = parts[0][2] + parts[1][2] + parts[2][2] + parts[3][2]
    rows_ref[...] = jnp.zeros_like(rows_ref)
    rows_ref[0:DEPTH, :] = grad_styles[0:DEPTH]
    rows_ref[DEPTH : DEPTH + 1, :] = grad_bias
    rows_ref[8 : 8 + DEPTH, :] = latent_ref[:, 0:C]
    rows_ref[8 + DEPTH : 8 + 2 * DEPTH, :] = latent_ref[:, C : 2 * C]
    extra = rows_ref[...].astype(BF)
    extra_ref[...] = extra
    give_ref[HALF : HALF + STAT, :] = extra
    grad_latent_ref[...] = lax.dot_general(
        grad_styles, affine_ref[...], (((1,), (1,)), ((), ())), precision=HI, preferred_element_type=F32
    )
    grad_energy = 2.0 * lax.dot_general(
        squares, grad_sum, (((0,), (0,)), ((), ())), precision=HI, preferred_element_type=F32
    )
    for n in range(DEPTH):
        clear_pads(pad_ref.at[n])
        spread(pad_ref.at[n], r_ref[n, PX : 2 * PX, :].astype(F32))
        flip_ref[:, n * PX : (n + 1) * PX] = r_ref[n, 0:PX, :].astype(F32).T.astype(BF)
    for ky in range(3):
        for kx in range(3):
            tap = ky * 3 + kx
            rhs = jnp.concatenate(
                [pad_ref[n, 2 - kx, (2 - ky) * ROW : (2 - ky) * ROW + PX, :] for n in range(DEPTH)], axis=0
            )
            part = jnp.dot(flip_ref[...], rhs, preferred_element_type=F32)
            at = slice(tap * C, (tap + 1) * C)
            total_ref[at, :] = (part + w_ref[at, :].astype(F32) * grad_energy).astype(BF)
    keep_ref[...] = total_ref[pl.ds(pl.multiple_of(core * HALF, HALF), HALF), :]
    give_ref[0:HALF, :] = total_ref[pl.ds(pl.multiple_of((1 - core) * HALF, HALF), HALF), :]


def gradients(r, w, styles, demod, energy, affine, latent):
    return pl.pallas_call(
        gradient_kernel,
        out_shape=(
            jax.ShapeDtypeStruct((HALF, C), BF),
            jax.ShapeDtypeStruct((HALF + STAT, C), BF),
            jax.ShapeDtypeStruct((STAT, C), BF),
            jax.ShapeDtypeStruct((8, affine.shape[0]), F32),
        ),
        in_specs=[vmem_spec()] * 7,
        out_specs=(vmem_spec(),) * 4,
        scratch_shapes=[
            pltpu.VMEM((C, DEPTH * PX), BF),
            pltpu.VMEM((DEPTH, 3, PAD, C), BF),
            pltpu.VMEM((ROWS, C), BF),
            pltpu.VMEM((STAT, C), F32),
        ],
        compiler_params=params(),
        name="gradients",
    )(r, w, styles, demod, energy, affine, latent)


def pair_kernel(keep_ref, extra_ref, got_ref, out_ref):
    for k in range(PEERS):
        at = slice(k * SHARE, (k + 1) * SHARE)
        out_ref[k, 0:SHARE, :] = (keep_ref[at, :].astype(F32) + got_ref[at, :].astype(F32)).astype(BF)
        out_ref[k, SHARE : SHARE + STAT, :] = extra_ref[...]
        out_ref[k, SHARE + STAT : SHARE + 2 * STAT, :] = got_ref[HALF : HALF + STAT, :]


def pair(keep, extra, got):
    return pl.pallas_call(
        pair_kernel,
        out_shape=jax.ShapeDtypeStruct((PEERS, SHARE + 2 * STAT, C), BF),
        in_specs=[vmem_spec()] * 3,
        out_specs=vmem_spec(),
        compiler_params=params(),
        name="pair",
    )(keep, extra, got)


def share_kernel(shares_ref, out_ref):
    total = shares_ref[0, 0:SHARE, :].astype(F32)
    for k in range(1, PEERS):
        total += shares_ref[k, 0:SHARE, :].astype(F32)
    total = total.astype(BF)
    for k in range(PEERS):
        out_ref[k] = total


def share(shares):
    return pl.pallas_call(
        share_kernel,
        out_shape=jax.ShapeDtypeStruct((PEERS, SHARE, C), BF),
        in_specs=[vmem_spec()],
        out_specs=vmem_spec(),
        compiler_params=params(),
        name="share",
    )(shares)


def affine_kernel(shares_ref, affine_ref, bias_ref, grads_ref, low_ref, high_ref):
    row = lax.broadcasted_iota(jnp.int32, (STAT, C), 0)
    bias = jnp.zeros((1, C), F32)
    for k in range(2 * PEERS):
        start = SHARE + (k % 2) * STAT
        tile = shares_ref[k // 2, start : start + STAT, :].astype(F32)
        bias += tile[DEPTH : DEPTH + 1]
        at = slice(k * STAT, (k + 1) * STAT)
        grads_ref[at, :] = jnp.where(row < DEPTH, tile, 0.0).astype(BF)
        low_ref[at, :] = pltpu.roll(tile, 8, 0).astype(BF)
        high_ref[at, :] = pltpu.roll(tile, 4, 0).astype(BF)
    bias_ref[...] = bias
    for k, ref in enumerate((low_ref, high_ref)):
        affine_ref[k * C : (k + 1) * C, :] = lax.dot_general(
            ref[...], grads_ref[...], (((0,), (0,)), ((), ())), preferred_element_type=F32
        )


def affine_gradient(shares, width):
    return pl.pallas_call(
        affine_kernel,
        out_shape=(jax.ShapeDtypeStruct((width, C), F32), jax.ShapeDtypeStruct((1, C), F32)),
        in_specs=[vmem_spec()],
        out_specs=(vmem_spec(), vmem_spec()),
        scratch_shapes=[pltpu.VMEM((2 * PEERS * STAT, C), BF)] * 3,
        compiler_params=params(),
        name="affine",
    )(shares)


def own_kernel(mine_ref, out_any, wide_ref, sem):
    _, _, core = place()
    wide_ref[...] = mine_ref[...].astype(F32)
    copy = pltpu.make_async_copy(wide_ref, out_any.at[pl.ds(pl.multiple_of(core * HALF, HALF), HALF)], sem)
    copy.start()
    copy.wait()


def rest_kernel(other_ref, _, out_any, wide_ref, sem):
    _, _, core = place()
    wide_ref[...] = other_ref[...].astype(F32)
    copy = pltpu.make_async_copy(wide_ref, out_any.at[pl.ds(pl.multiple_of((1 - core) * HALF, HALF), HALF)], sem)
    copy.start()
    copy.wait()


def widen(kernel, name, *args):
    return pl.pallas_call(
        kernel,
        out_shape=jax.ShapeDtypeStruct((ROWS, C), F32),
        in_specs=[vmem_spec(), pl.BlockSpec(memory_space=pltpu.HBM)][: len(args)],
        out_specs=pl.BlockSpec(memory_space=pltpu.HBM),
        input_output_aliases={1: 0} if len(args) == 2 else {},
        scratch_shapes=[pltpu.VMEM((HALF, C), F32), pltpu.SemaphoreType.DMA],
        compiler_params=params(),
        name=name,
    )(*args)


def body(images, latent, weight, affine, biases, cotangent):
    width = latent.shape[1]
    replicas = lax.axis_size("dp")
    segments = lax.axis_size("segment")
    planes = [list(range(k, k + DEPTH)) for k in range(0, segments, DEPTH)]
    across = [(i, (i + DEPTH) % segments) for i in range(segments)]
    sibling = [(i, i ^ 1) for i in range(replicas)]
    cores = [list(range(k, replicas, 2)) for k in range(2)]

    w = weight.reshape(ROWS, C)
    images = images.reshape(DEPTH, PX, C)
    cotangent = cotangent.reshape(DEPTH, PX, C)

    send, styles, demod, energy = prepare(latent, affine[0], w, biases)
    a = lax.all_to_all(send, "segment", 0, 0, axis_index_groups=planes)
    b = near(lax.ppermute(a, "dp", sibling))
    a = near(a)

    act, kernels, stat = first(images, a, b)
    flipped = flip(kernels)
    arrived = near(lax.ppermute(act, "segment", across))
    dx, xs, conv, _ = middle(images, cotangent, arrived, kernels, flipped, stat)
    returned = near(lax.ppermute(dx, "segment", across))
    sent = last(cotangent, returned, xs, conv, flipped, stat)

    r = near(lax.all_to_all(sent, "segment", 0, 0, axis_index_groups=planes))
    keep, give, extra, latent_part = gradients(r, w, styles, demod, energy, affine[0], latent)

    got = near(lax.ppermute(give, "dp", sibling))
    shared, part = lax.optimization_barrier((pair(keep, extra, got), latent_part[:DEPTH]))
    shares = near(lax.all_to_all(shared, "dp", 0, 0, axis_index_groups=cores))
    part = part + lax.ppermute(part, "segment", across)
    part = part + lax.ppermute(part, "segment", [(i, i ^ 1) for i in range(segments)])
    spread_share, part = lax.optimization_barrier((share(shares), part))
    mine = lax.all_to_all(spread_share, "dp", 0, 0, axis_index_groups=cores).reshape(HALF, C)
    grad_latent = part + lax.ppermute(part, "segment", [(i, i ^ 2) for i in range(segments)])
    mine, grad_latent = lax.optimization_barrier((mine, grad_latent))
    other = near(lax.ppermute(mine, "dp", sibling))
    grad_affine, grad_bias = affine_gradient(shares, width)
    grad_weight = widen(rest_kernel, "rest", other, widen(own_kernel, "own", near(mine))).reshape(weight.shape)
    return (grad_weight, grad_affine[None], grad_bias, grad_latent)


def solution(mesh):
    placed = (
        P("dp", None, None, None),
        P("dp", None),
        P("segment", None, None, None, None),
        P("segment", None, None),
        P("segment", None),
        P("dp", None, None, None),
    )
    return jax.shard_map(
        body,
        mesh=mesh,
        in_specs=placed,
        out_specs=(
            P("segment", None, None, None, None),
            P("segment", None, None),
            P("segment", None),
            P("dp", None),
        ),
        check_vma=False,
    )
```

```python
import functools
import math

import jax
import jax.numpy as jnp
from jax import lax
from jax.experimental import pallas as pl
from jax.experimental.pallas import tpu as pltpu
from jax.sharding import PartitionSpec as P

GAIN = math.sqrt(2.0)
EPS = 1e-08
BF = jnp.bfloat16
F32 = jnp.float32
C = 256
PX = 256
TAPS = 9
ROWS = TAPS * C
HALF = ROWS // 2
STAT = 16
DEPTH = 4
PEERS = 8
SHARE = HALF // PEERS
ROW = 16
BLOCK = 128
PAD = PX + 2 * ROW
HI = lax.Precision.HIGHEST


def any_spec():
    return pl.BlockSpec(memory_space=pl.ANY)


def vmem_spec():
    return pl.BlockSpec(memory_space=pltpu.VMEM)


def params():
    return pltpu.CompilerParams(vmem_limit_bytes=28 << 20)


def near(value):
    return pltpu.with_memory_space_constraint(value, pltpu.VMEM)


def place():
    seg = lax.axis_index("segment")
    return seg // DEPTH, seg % DEPTH, lax.axis_index("dp") % 2


def split3(value):
    hi = value.astype(BF).astype(F32)
    rest = value - hi
    mid = rest.astype(BF).astype(F32)
    return hi, mid, rest - mid


def pack_rows(values):
    row = lax.broadcasted_iota(jnp.int32, (STAT, C), 0)
    out = jnp.zeros((STAT, C), F32)
    k = 0
    for value in values:
        for part in split3(value):
            out = jnp.where(row == k, jnp.broadcast_to(part, (STAT, C)), out)
            k += 1
    return out.astype(BF)


def unpack_rows(tile):
    t = tile.astype(F32)
    return [t[3 * k : 3 * k + 1] + t[3 * k + 1 : 3 * k + 2] + t[3 * k + 2 : 3 * k + 3] for k in range(3)]


def stack_rows(rows):
    index = lax.broadcasted_iota(jnp.int32, (8, C), 0)
    out = jnp.zeros((8, C), F32)
    for k, row in enumerate(rows):
        out = jnp.where(index == k, jnp.broadcast_to(row, (8, C)), out)
    return out


def prepare_kernel(
    latent_hbm, affine_hbm, w_hbm, bias_hbm, send_ref, styles_ref, demod_ref, energy_ref,
    rows_ref, affine_ref, w_ref, bias_ref, sem,
):
    _, _, core = place()
    mine = pl.ds(pl.multiple_of(core * HALF, HALF), HALF)
    rows_ref[...] = jnp.zeros_like(rows_ref)
    third = ROWS // 3
    loads = [
        pltpu.make_async_copy(affine_hbm, affine_ref, sem.at[0]),
        pltpu.make_async_copy(latent_hbm, rows_ref.at[pl.ds(0, DEPTH)], sem.at[1]),
        pltpu.make_async_copy(bias_hbm, bias_ref, sem.at[2]),
    ] + [
        pltpu.make_async_copy(w_hbm.at[pl.ds(k * third, third)], w_ref.at[pl.ds(k * third, third)], sem.at[3 + k])
        for k in range(3)
    ]
    sends = [
        pltpu.make_async_copy(w_hbm.at[mine], send_ref.at[k, pl.ds(0, HALF)], sem.at[6 + k]) for k in range(DEPTH)
    ]
    for copy in loads + sends:
        copy.start()
    for copy in loads[:3]:
        copy.wait()
    styles = jnp.dot(rows_ref[...], affine_ref[...], precision=HI, preferred_element_type=F32) + 1.0
    energy = jnp.zeros((C, C), F32)
    for tap in range(TAPS):
        if tap % 3 == 0:
            loads[3 + tap // 3].wait()
        part = w_ref[tap * C : (tap + 1) * C, :].astype(F32)
        energy += part * part
    energy_ref[...] = energy
    demod = lax.rsqrt(jnp.dot(styles * styles, energy, precision=HI, preferred_element_type=F32) + EPS)
    styles_ref[...] = styles
    demod_ref[...] = demod
    for k in range(DEPTH):
        send_ref[k, HALF : HALF + STAT, :] = pack_rows([styles[k : k + 1], demod[k : k + 1], bias_ref[...]])
    for copy in sends:
        copy.wait()


def prepare(latent, affine, w, bias):
    far = [pltpu.with_memory_space_constraint(value, pltpu.HBM) for value in (latent, affine, w, bias)]
    return pl.pallas_call(
        prepare_kernel,
        out_shape=(
            jax.ShapeDtypeStruct((DEPTH, HALF + STAT, C), BF),
            jax.ShapeDtypeStruct((8, C), F32),
            jax.ShapeDtypeStruct((8, C), F32),
            jax.ShapeDtypeStruct((C, C), F32),
        ),
        in_specs=[pl.BlockSpec(memory_space=pltpu.HBM)] * 4,
        out_specs=(vmem_spec(),) * 4,
        scratch_shapes=[
            pltpu.VMEM((8, latent.shape[1]), F32),
            pltpu.VMEM(affine.shape, F32),
            pltpu.VMEM((ROWS, C), BF),
            pltpu.VMEM((1, C), F32),
            pltpu.SemaphoreType.DMA((6 + DEPTH,)),
        ],
        compiler_params=params(),
        name="prepare",
    )(*far)


def weight_copies(a_any, b_any, w_buf, stat_buf, sem):
    _, _, core = place()
    mine = pl.ds(pl.multiple_of(core * HALF, HALF), HALF)
    other = pl.ds(pl.multiple_of((1 - core) * HALF, HALF), HALF)
    return [
        (
            pltpu.make_async_copy(a_any.at[l, pl.ds(HALF, STAT)], stat_buf.at[l], sem.at[0, l]),
            pltpu.make_async_copy(a_any.at[l, pl.ds(0, HALF)], w_buf.at[l, mine], sem.at[1, l]),
            pltpu.make_async_copy(b_any.at[l, pl.ds(0, HALF)], w_buf.at[l, other], sem.at[2, l]),
        )
        for l in range(DEPTH)
    ]


def clear_pads(pad_ref):
    for k in range(3):
        pad_ref[k, 0:ROW, :] = jnp.zeros((ROW, C), BF)
        pad_ref[k, ROW + PX : PAD, :] = jnp.zeros((ROW, C), BF)


def spread(pad_ref, value):
    column = lax.broadcasted_iota(jnp.int32, (PX, C), 0) % ROW
    pad_ref[1, ROW : ROW + PX, :] = value.astype(BF)
    pad_ref[0, ROW : ROW + PX, :] = jnp.where(column == 0, 0.0, pltpu.roll(value, 1, 0)).astype(BF)
    pad_ref[2, ROW : ROW + PX, :] = jnp.where(column == ROW - 1, 0.0, pltpu.roll(value, PX - 1, 0)).astype(BF)


def taps_matmul(pad_ref, w, mirrored):
    out = []
    for start in range(0, PX, BLOCK):
        pieces = []
        for ky in range(3):
            for kx in range(3):
                plane, shift = (2 - kx, 2 - ky) if mirrored else (kx, ky)
                first_row = start + shift * ROW
                pieces.append(pad_ref[plane, first_row : first_row + BLOCK, :])
        out.append(jnp.dot(jnp.concatenate(pieces, axis=1), w, preferred_element_type=F32))
    return jnp.concatenate(out, axis=0)


def forward_layer(x, l, w_ref, stat, pad_ref):
    styles, demod, bias = stat
    spread(pad_ref, (x.astype(F32) * styles).astype(BF).astype(F32))
    return taps_matmul(pad_ref, w_ref[l], False)


def activate(conv, stat):
    _, demod, bias = stat
    hidden = conv * demod + bias
    return (GAIN * hidden * (0.6 + 0.4 * jnp.tanh(hidden))).astype(BF)


def backward_layer(upstream, x, conv, l, flip_ref, stat, pad_ref, send_ref):
    styles, demod, bias = stat
    hidden = conv * demod + bias
    t = jnp.tanh(hidden)
    dh = upstream.astype(F32) * (GAIN * (0.6 + 0.4 * t + 0.4 * hidden * (1.0 - t * t)))
    grad_bias = jnp.sum(dh, axis=0, keepdims=True)
    grad_demod = jnp.sum(dh * conv, axis=0, keepdims=True)
    grad_conv = (dh * demod).astype(BF).astype(F32)
    spread(pad_ref, grad_conv)
    send_ref[l, PX : 2 * PX, :] = pad_ref[1, ROW : ROW + PX, :]
    total = taps_matmul(pad_ref, flip_ref[l], True)
    grad_scaled = total.astype(BF).astype(F32)
    xf = x.astype(F32)
    grad_styles = jnp.sum(grad_scaled * xf, axis=0, keepdims=True)
    send_ref[l, 0:PX, :] = (xf * styles).astype(BF)
    send_ref[l, 2 * PX : 2 * PX + STAT, :] = pack_rows([grad_styles, grad_demod, grad_bias])
    return (grad_scaled * styles).astype(BF)


def first_kernel(images_any, a_ref, b_ref, out_ref, w_ref, stat_ref, x_buf, pad_ref, sem, x_sem):
    _, z, _ = place()
    x_copy = pltpu.make_async_copy(images_any.at[z], x_buf, x_sem)
    x_copy.start()
    copies = weight_copies(a_ref, b_ref, w_ref, stat_ref, sem)
    for copy in copies[0]:
        copy.start()
    clear_pads(pad_ref)
    x_copy.wait()
    x = x_buf[...]
    for l in range(DEPTH):
        for copy in copies[l]:
            copy.wait()
        if l < DEPTH - 1:
            for copy in copies[l + 1]:
                copy.start()
        stat = unpack_rows(stat_ref[l])
        x = activate(forward_layer(x, l, w_ref, stat, pad_ref), stat)
    out_ref[...] = x


def flip_kernel(w_ref, flip_ref):
    for l in range(DEPTH):
        for tap in range(TAPS):
            at = slice(tap * C, (tap + 1) * C)
            flip_ref[l, at, :] = w_ref[l, at, :].T


def middle_kernel(
    images_any, cot_any, recv_ref, w_ref, flip_ref, stat_ref, dx_ref, xs_ref, conv_ref, send_ref,
    x_buf, u_buf, pad_ref, x_sem,
):
    half, z, _ = place()
    x_copy = pltpu.make_async_copy(images_any.at[z], x_buf, x_sem.at[0])
    u_copy = pltpu.make_async_copy(cot_any.at[z], u_buf, x_sem.at[1])
    x_copy.start()
    u_copy.start()
    clear_pads(pad_ref)
    x_copy.wait()
    x = jnp.where(half == 1, recv_ref[...], x_buf[...])
    stats = []
    for l in range(DEPTH):
        stats.append(unpack_rows(stat_ref[l]))
        xs_ref[l] = x
        conv = forward_layer(x, l, w_ref, stats[l], pad_ref)
        conv_ref[l] = conv
        if l < DEPTH - 1:
            x = activate(conv, stats[l])
    u_copy.wait()
    upstream = u_buf[...]
    for l in reversed(range(DEPTH)):
        upstream = backward_layer(upstream, xs_ref[l], conv_ref[l], l, flip_ref, stats[l], pad_ref, send_ref)
    dx_ref[...] = upstream


def last_kernel(cot_any, recv_ref, xs_ref, conv_ref, flip_ref, stat_ref, send_ref, u_buf, pad_ref, u_sem):
    half, z, _ = place()
    u_copy = pltpu.make_async_copy(cot_any.at[z], u_buf, u_sem)
    u_copy.start()
    clear_pads(pad_ref)
    u_copy.wait()
    upstream = jnp.where(half == 1, u_buf[...], recv_ref[...])
    for l in reversed(range(DEPTH)):
        stat = unpack_rows(stat_ref[l])
        upstream = backward_layer(upstream, xs_ref[l], conv_ref[l], l, flip_ref, stat, pad_ref, send_ref)


MAP = jax.ShapeDtypeStruct((PX, C), BF)
KERNELS = jax.ShapeDtypeStruct((DEPTH, ROWS, C), BF)
SENT = jax.ShapeDtypeStruct((DEPTH, 2 * PX + STAT, C), BF)


def first(images, a, b):
    return pl.pallas_call(
        first_kernel,
        out_shape=(MAP, KERNELS, jax.ShapeDtypeStruct((DEPTH, STAT, C), BF)),
        in_specs=[any_spec(), vmem_spec(), vmem_spec()],
        out_specs=(vmem_spec(),) * 3,
        scratch_shapes=[
            pltpu.VMEM((PX, C), BF),
            pltpu.VMEM((3, PAD, C), BF),
            pltpu.SemaphoreType.DMA((3, DEPTH)),
            pltpu.SemaphoreType.DMA,
        ],
        compiler_params=params(),
        name="first",
    )(images, a, b)


def flip(w):
    return pl.pallas_call(
        flip_kernel,
        out_shape=KERNELS,
        in_specs=[vmem_spec()],
        out_specs=vmem_spec(),
        compiler_params=params(),
        name="flip",
    )(w)


def middle(images, cot, recv, w, flipped, stat):
    return pl.pallas_call(
        middle_kernel,
        out_shape=(
            MAP,
            jax.ShapeDtypeStruct((DEPTH, PX, C), BF),
            jax.ShapeDtypeStruct((DEPTH, PX, C), F32),
            SENT,
        ),
        in_specs=[any_spec(), any_spec()] + [vmem_spec()] * 4,
        out_specs=(vmem_spec(),) * 4,
        scratch_shapes=[
            pltpu.VMEM((PX, C), BF),
            pltpu.VMEM((PX, C), BF),
            pltpu.VMEM((3, PAD, C), BF),
            pltpu.SemaphoreType.DMA((2,)),
        ],
        compiler_params=params(),
        name="middle",
    )(images, cot, recv, w, flipped, stat)


def last(cot, recv, xs, conv, flipped, stat):
    return pl.pallas_call(
        last_kernel,
        out_shape=SENT,
        in_specs=[any_spec()] + [vmem_spec()] * 5,
        out_specs=vmem_spec(),
        scratch_shapes=[
            pltpu.VMEM((PX, C), BF),
            pltpu.VMEM((3, PAD, C), BF),
            pltpu.SemaphoreType.DMA,
        ],
        compiler_params=params(),
        name="last",
    )(cot, recv, xs, conv, flipped, stat)


def half_gradient(flip_ref, pad_ref, w_ref, grad_energy_ref, half, out_ref):
    first_row = pl.multiple_of(half * BLOCK, BLOCK)
    lhs = flip_ref[pl.ds(first_row, BLOCK), :]
    grad_energy = grad_energy_ref[pl.ds(first_row, BLOCK), :]
    for ky in range(3):
        for kx in range(3):
            tap = ky * 3 + kx
            rhs = jnp.concatenate(
                [pad_ref[n, 2 - kx, (2 - ky) * ROW : (2 - ky) * ROW + PX, :] for n in range(DEPTH)], axis=0
            )
            part = jnp.dot(lhs, rhs, preferred_element_type=F32)
            w = w_ref[pl.ds(pl.multiple_of(tap * C + half * BLOCK, BLOCK), BLOCK), :].astype(F32)
            out_ref[tap * BLOCK : (tap + 1) * BLOCK, :] = (part + w * grad_energy).astype(BF)


def give_kernel(
    r_ref, w_ref, styles_ref, demod_ref, energy_ref, affine_ref, latent_ref,
    give_ref, extra_ref, grad_latent_ref, flip_ref, pad_ref, grad_energy_ref, rows_ref,
):
    _, _, core = place()
    parts = [unpack_rows(r_ref[n, 2 * PX : 2 * PX + STAT, :]) for n in range(DEPTH)]
    styles = styles_ref[...]
    demod = demod_ref[...]
    grad_sum = stack_rows([p[1] for p in parts]) * (-0.5) * demod * demod * demod
    squares = styles * styles
    grad_squares = lax.dot_general(
        grad_sum, energy_ref[...], (((1,), (1,)), ((), ())), precision=HI, preferred_element_type=F32
    )
    grad_styles = stack_rows([p[0] for p in parts]) + 2.0 * styles * grad_squares
    grad_bias = parts[0][2] + parts[1][2] + parts[2][2] + parts[3][2]
    rows_ref[...] = jnp.zeros_like(rows_ref)
    rows_ref[0:DEPTH, :] = grad_styles[0:DEPTH]
    rows_ref[DEPTH : DEPTH + 1, :] = grad_bias
    rows_ref[8 : 8 + DEPTH, :] = latent_ref[:, 0:C]
    rows_ref[8 + DEPTH : 8 + 2 * DEPTH, :] = latent_ref[:, C : 2 * C]
    extra = rows_ref[...].astype(BF)
    extra_ref[...] = extra
    give_ref[HALF : HALF + STAT, :] = extra
    grad_latent = lax.dot_general(
        grad_styles, affine_ref[...], (((1,), (1,)), ((), ())), precision=HI, preferred_element_type=F32
    )
    grad_latent_ref[...] = grad_latent[0:DEPTH]
    grad_energy_ref[...] = 2.0 * lax.dot_general(
        squares, grad_sum, (((0,), (0,)), ((), ())), precision=HI, preferred_element_type=F32
    )
    for n in range(DEPTH):
        clear_pads(pad_ref.at[n])
        spread(pad_ref.at[n], r_ref[n, PX : 2 * PX, :].astype(F32))
        flip_ref[:, n * PX : (n + 1) * PX] = r_ref[n, 0:PX, :].astype(F32).T.astype(BF)
    half_gradient(flip_ref, pad_ref, w_ref, grad_energy_ref, 1 - core, give_ref)


def give_half(r, w, styles, demod, energy, affine, latent):
    return pl.pallas_call(
        give_kernel,
        out_shape=(
            jax.ShapeDtypeStruct((HALF + STAT, C), BF),
            jax.ShapeDtypeStruct((STAT, C), BF),
            jax.ShapeDtypeStruct((DEPTH, affine.shape[0]), F32),
            jax.ShapeDtypeStruct((C, DEPTH * PX), BF),
            jax.ShapeDtypeStruct((DEPTH, 3, PAD, C), BF),
            jax.ShapeDtypeStruct((C, C), F32),
        ),
        in_specs=[vmem_spec()] * 7,
        out_specs=(vmem_spec(),) * 6,
        scratch_shapes=[pltpu.VMEM((STAT, C), F32)],
        compiler_params=params(),
        name="give",
    )(r, w, styles, demod, energy, affine, latent)


def keep_kernel(flip_ref, pad_ref, w_ref, grad_energy_ref, keep_ref):
    _, _, core = place()
    half_gradient(flip_ref, pad_ref, w_ref, grad_energy_ref, core, keep_ref)


def keep_half(flipped, padded, w, grad_energy):
    return pl.pallas_call(
        keep_kernel,
        out_shape=jax.ShapeDtypeStruct((HALF, C), BF),
        in_specs=[vmem_spec()] * 4,
        out_specs=vmem_spec(),
        compiler_params=params(),
        name="keep",
    )(flipped, padded, w, grad_energy)


def pair_kernel(keep_ref, extra_ref, got_ref, out_ref):
    for k in range(PEERS):
        at = slice(k * SHARE, (k + 1) * SHARE)
        out_ref[k, 0:SHARE, :] = (keep_ref[at, :].astype(F32) + got_ref[at, :].astype(F32)).astype(BF)
        out_ref[k, SHARE : SHARE + STAT, :] = extra_ref[...]
        out_ref[k, SHARE + STAT : SHARE + 2 * STAT, :] = got_ref[HALF : HALF + STAT, :]


def pair(keep, extra, got):
    return pl.pallas_call(
        pair_kernel,
        out_shape=jax.ShapeDtypeStruct((PEERS, SHARE + 2 * STAT, C), BF),
        in_specs=[vmem_spec()] * 3,
        out_specs=vmem_spec(),
        compiler_params=params(),
        name="pair",
    )(keep, extra, got)


def share_kernel(shares_ref, out_ref):
    total = shares_ref[0, 0:SHARE, :].astype(F32)
    for k in range(1, PEERS):
        total += shares_ref[k, 0:SHARE, :].astype(F32)
    total = total.astype(BF)
    for k in range(PEERS):
        out_ref[k] = total


def share(shares):
    return pl.pallas_call(
        share_kernel,
        out_shape=jax.ShapeDtypeStruct((PEERS, SHARE, C), BF),
        in_specs=[vmem_spec()],
        out_specs=vmem_spec(),
        compiler_params=params(),
        name="share",
    )(shares)


def affine_kernel(shares_ref, affine_ref, bias_ref, grads_ref, low_ref, high_ref):
    row = lax.broadcasted_iota(jnp.int32, (STAT, C), 0)
    bias = jnp.zeros((1, C), F32)
    for k in range(2 * PEERS):
        start = SHARE + (k % 2) * STAT
        tile = shares_ref[k // 2, start : start + STAT, :].astype(F32)
        bias += tile[DEPTH : DEPTH + 1]
        at = slice(k * STAT, (k + 1) * STAT)
        grads_ref[at, :] = jnp.where(row < DEPTH, tile, 0.0).astype(BF)
        low_ref[at, :] = pltpu.roll(tile, 8, 0).astype(BF)
        high_ref[at, :] = pltpu.roll(tile, 4, 0).astype(BF)
    bias_ref[...] = bias
    for k, ref in enumerate((low_ref, high_ref)):
        affine_ref[k * C : (k + 1) * C, :] = lax.dot_general(
            ref[...], grads_ref[...], (((0,), (0,)), ((), ())), preferred_element_type=F32
        )


def affine_gradient(shares, width):
    return pl.pallas_call(
        affine_kernel,
        out_shape=(jax.ShapeDtypeStruct((width, C), F32), jax.ShapeDtypeStruct((1, C), F32)),
        in_specs=[vmem_spec()],
        out_specs=(vmem_spec(), vmem_spec()),
        scratch_shapes=[pltpu.VMEM((2 * PEERS * STAT, C), BF)] * 3,
        compiler_params=params(),
        name="affine",
    )(shares)


def widen_kernel(own, value_ref, *refs):
    out_any, wide_ref, sem = refs[-3:]
    _, _, core = place()
    half = core if own else 1 - core
    wide_ref[...] = value_ref[...].reshape(TAPS, BLOCK, C).astype(F32)
    copy = pltpu.make_async_copy(wide_ref, out_any.at[:, pl.ds(pl.multiple_of(half * BLOCK, BLOCK), BLOCK)], sem)
    copy.start()
    copy.wait()


def widen(value, target=None):
    hbm = pl.BlockSpec(memory_space=pltpu.HBM)
    args = (value,) if target is None else (value, target)
    return pl.pallas_call(
        functools.partial(widen_kernel, target is None),
        out_shape=jax.ShapeDtypeStruct((TAPS, C, C), F32),
        in_specs=[vmem_spec(), hbm][: len(args)],
        out_specs=hbm,
        input_output_aliases={1: 0} if len(args) == 2 else {},
        scratch_shapes=[pltpu.VMEM((TAPS, BLOCK, C), F32), pltpu.SemaphoreType.DMA],
        compiler_params=params(),
        name="own" if target is None else "rest",
    )(*args)


def body(images, latent, weight, affine, biases, cotangent):
    width = latent.shape[1]
    replicas = lax.axis_size("dp")
    segments = lax.axis_size("segment")
    planes = [list(range(k, k + DEPTH)) for k in range(0, segments, DEPTH)]
    across = [(i, (i + DEPTH) % segments) for i in range(segments)]
    sibling = [(i, i ^ 1) for i in range(replicas)]
    cores = [list(range(k, replicas, 2)) for k in range(2)]

    w = weight.reshape(ROWS, C)
    images = images.reshape(DEPTH, PX, C)
    cotangent = cotangent.reshape(DEPTH, PX, C)

    send, styles, demod, energy = prepare(latent, affine[0], w, biases)
    a = lax.all_to_all(send, "segment", 0, 0, axis_index_groups=planes)
    b = near(lax.ppermute(a, "dp", sibling))
    a = near(a)

    act, kernels, stat = first(images, a, b)
    flipped = flip(kernels)
    arrived = near(lax.ppermute(act, "segment", across))
    dx, xs, conv, _ = middle(images, cotangent, arrived, kernels, flipped, stat)
    returned = near(lax.ppermute(dx, "segment", across))
    sent = last(cotangent, returned, xs, conv, flipped, stat)

    r = near(lax.all_to_all(sent, "segment", 0, 0, axis_index_groups=planes))
    give, extra, part, flipped_maps, padded, grad_energy = give_half(
        r, w, styles, demod, energy, affine[0], latent
    )
    got = near(lax.ppermute(give, "dp", sibling))
    part = part + lax.ppermute(part, "segment", across)
    keep = keep_half(flipped_maps, padded, w, grad_energy)
    shared, part = lax.optimization_barrier((pair(keep, extra, got), part))
    shares = near(lax.all_to_all(near(shared), "dp", 0, 0, axis_index_groups=cores))
    part = part + lax.ppermute(part, "segment", [(i, i ^ 1) for i in range(segments)])
    grad_latent = part + lax.ppermute(part, "segment", [(i, i ^ 2) for i in range(segments)])
    spread_share, grad_latent = lax.optimization_barrier((share(shares), grad_latent))
    mine = lax.all_to_all(near(spread_share), "dp", 0, 0, axis_index_groups=cores)
    grad_affine, grad_bias = affine_gradient(shares, width)
    mine, grad_affine, grad_bias = lax.optimization_barrier((mine, grad_affine, grad_bias))
    other = near(lax.ppermute(mine, "dp", sibling))
    grad_weight = widen(other, widen(near(mine))).reshape(weight.shape)
    return (grad_weight, grad_affine[None], grad_bias, grad_latent)


def solution(mesh):
    placed = (
        P("dp", None, None, None),
        P("dp", None),
        P("segment", None, None, None, None),
        P("segment", None, None),
        P("segment", None),
        P("dp", None, None, None),
    )
    return jax.shard_map(
        body,
        mesh=mesh,
        in_specs=placed,
        out_specs=(
            P("segment", None, None, None, None),
            P("segment", None, None),
            P("segment", None),
            P("dp", None),
        ),
        check_vma=False,
    )
```

```python
import functools
import math

import jax
import jax.numpy as jnp
from jax import lax
from jax.experimental import pallas as pl
from jax.experimental.pallas import tpu as pltpu
from jax.sharding import PartitionSpec as P

GAIN = math.sqrt(2.0)
EPS = 1e-08
BF = jnp.bfloat16
F32 = jnp.float32
C = 256
PX = 256
TAPS = 9
ROWS = TAPS * C
HALF = ROWS // 2
STAT = 16
DEPTH = 4
PEERS = 8
SHARE = HALF // PEERS
ROW = 16
BLOCK = 128
LANES = 128
PAD = PX + 2 * ROW
HI = lax.Precision.HIGHEST


def any_spec():
    return pl.BlockSpec(memory_space=pl.ANY)


def vmem_spec():
    return pl.BlockSpec(memory_space=pltpu.VMEM)


def params():
    return pltpu.CompilerParams(vmem_limit_bytes=28 << 20)


def near(value):
    return pltpu.with_memory_space_constraint(value, pltpu.VMEM)


def place():
    seg = lax.axis_index("segment")
    return seg // DEPTH, seg % DEPTH, lax.axis_index("dp") % 2


def split3(value):
    hi = value.astype(BF).astype(F32)
    rest = value - hi
    mid = rest.astype(BF).astype(F32)
    return hi, mid, rest - mid


def pack_rows(values):
    row = lax.broadcasted_iota(jnp.int32, (STAT, C), 0)
    out = jnp.zeros((STAT, C), F32)
    k = 0
    for value in values:
        for part in split3(value):
            out = jnp.where(row == k, jnp.broadcast_to(part, (STAT, C)), out)
            k += 1
    return out.astype(BF)


def unpack_rows(tile):
    t = tile.astype(F32)
    return [t[3 * k : 3 * k + 1] + t[3 * k + 1 : 3 * k + 2] + t[3 * k + 2 : 3 * k + 3] for k in range(3)]


def stack_rows(rows):
    index = lax.broadcasted_iota(jnp.int32, (8, C), 0)
    out = jnp.zeros((8, C), F32)
    for k, row in enumerate(rows):
        out = jnp.where(index == k, jnp.broadcast_to(row, (8, C)), out)
    return out


def prepare_kernel(
    latent_hbm, affine_hbm, w_hbm, bias_hbm, send_ref, styles_ref, demod_ref, energy_ref,
    rows_ref, affine_ref, w_ref, bias_ref, sem,
):
    _, _, core = place()
    mine = pl.ds(pl.multiple_of(core * LANES, LANES), LANES)
    rows_ref[...] = jnp.zeros_like(rows_ref)
    third = ROWS // 3
    loads = [
        pltpu.make_async_copy(affine_hbm, affine_ref, sem.at[0]),
        pltpu.make_async_copy(latent_hbm, rows_ref.at[pl.ds(0, DEPTH)], sem.at[1]),
        pltpu.make_async_copy(bias_hbm, bias_ref, sem.at[2]),
    ] + [
        pltpu.make_async_copy(w_hbm.at[pl.ds(k * third, third)], w_ref.at[pl.ds(k * third, third)], sem.at[3 + k])
        for k in range(3)
    ]
    sends = [
        pltpu.make_async_copy(w_hbm.at[:, mine], send_ref.at[k, pl.ds(0, ROWS)], sem.at[6 + k]) for k in range(DEPTH)
    ]
    for copy in loads + sends:
        copy.start()
    for copy in loads[:3]:
        copy.wait()
    styles = jnp.dot(rows_ref[...], affine_ref[...], precision=HI, preferred_element_type=F32) + 1.0
    energy = jnp.zeros((C, C), F32)
    for tap in range(TAPS):
        if tap % 3 == 0:
            loads[3 + tap // 3].wait()
        part = w_ref[tap * C : (tap + 1) * C, :].astype(F32)
        energy += part * part
    energy_ref[...] = energy
    demod = lax.rsqrt(jnp.dot(styles * styles, energy, precision=HI, preferred_element_type=F32) + EPS)
    styles_ref[...] = styles
    demod_ref[...] = demod
    for k in range(DEPTH):
        tile = pack_rows([styles[k : k + 1], demod[k : k + 1], bias_ref[...]])
        send_ref[k, ROWS : ROWS + STAT, :] = tile[:, :LANES]
        send_ref[k, ROWS + STAT : ROWS + 2 * STAT, :] = tile[:, LANES:]
    for copy in sends:
        copy.wait()


def prepare(latent, affine, w, bias):
    far = [pltpu.with_memory_space_constraint(value, pltpu.HBM) for value in (latent, affine, w, bias)]
    return pl.pallas_call(
        prepare_kernel,
        out_shape=(
            jax.ShapeDtypeStruct((DEPTH, ROWS + 2 * STAT, LANES), BF),
            jax.ShapeDtypeStruct((8, C), F32),
            jax.ShapeDtypeStruct((8, C), F32),
            jax.ShapeDtypeStruct((C, C), F32),
        ),
        in_specs=[pl.BlockSpec(memory_space=pltpu.HBM)] * 4,
        out_specs=(vmem_spec(),) * 4,
        scratch_shapes=[
            pltpu.VMEM((8, latent.shape[1]), F32),
            pltpu.VMEM(affine.shape, F32),
            pltpu.VMEM((ROWS, C), BF),
            pltpu.VMEM((1, C), F32),
            pltpu.SemaphoreType.DMA((6 + DEPTH,)),
        ],
        compiler_params=params(),
        name="prepare",
    )(*far)


def read_stats(a_ref, l):
    return unpack_rows(
        jnp.concatenate(
            [a_ref[l, ROWS : ROWS + STAT, :], a_ref[l, ROWS + STAT : ROWS + 2 * STAT, :]], axis=1
        )
    )


def clear_pads(pad_ref):
    for k in range(3):
        pad_ref[k, 0:ROW, :] = jnp.zeros((ROW, C), BF)
        pad_ref[k, ROW + PX : PAD, :] = jnp.zeros((ROW, C), BF)


def spread(pad_ref, value):
    column = lax.broadcasted_iota(jnp.int32, (PX, C), 0) % ROW
    pad_ref[1, ROW : ROW + PX, :] = value.astype(BF)
    pad_ref[0, ROW : ROW + PX, :] = jnp.where(column == 0, 0.0, pltpu.roll(value, 1, 0)).astype(BF)
    pad_ref[2, ROW : ROW + PX, :] = jnp.where(column == ROW - 1, 0.0, pltpu.roll(value, PX - 1, 0)).astype(BF)


def taps_matmul(pad_ref, w, mirrored):
    out = []
    for start in range(0, PX, BLOCK):
        pieces = []
        for ky in range(3):
            for kx in range(3):
                plane, shift = (2 - kx, 2 - ky) if mirrored else (kx, ky)
                first_row = start + shift * ROW
                pieces.append(pad_ref[plane, first_row : first_row + BLOCK, :])
        out.append(jnp.dot(jnp.concatenate(pieces, axis=1), w, preferred_element_type=F32))
    return jnp.concatenate(out, axis=0)


def forward_layer(x, l, a_ref, b_ref, stat, pad_ref):
    styles, demod, bias = stat
    spread(pad_ref, (x.astype(F32) * styles).astype(BF).astype(F32))
    _, _, core = place()
    w = jnp.concatenate([a_ref[l, 0:ROWS, :], b_ref[l, 0:ROWS, :]], axis=1)
    conv = taps_matmul(pad_ref, w, False)
    return jnp.where(core == 0, conv, jnp.concatenate([conv[:, LANES:], conv[:, :LANES]], axis=1))


def activate(conv, stat):
    _, demod, bias = stat
    hidden = conv * demod + bias
    return (GAIN * hidden * (0.6 + 0.4 * jnp.tanh(hidden))).astype(BF)


def backward_layer(upstream, x, conv, l, flip_ref, stat, pad_ref, send_ref):
    styles, demod, bias = stat
    hidden = conv * demod + bias
    t = jnp.tanh(hidden)
    dh = upstream.astype(F32) * (GAIN * (0.6 + 0.4 * t + 0.4 * hidden * (1.0 - t * t)))
    grad_bias = jnp.sum(dh, axis=0, keepdims=True)
    grad_demod = jnp.sum(dh * conv, axis=0, keepdims=True)
    grad_conv = (dh * demod).astype(BF).astype(F32)
    spread(pad_ref, grad_conv)
    send_ref[l, PX : 2 * PX, :] = pad_ref[1, ROW : ROW + PX, :]
    total = taps_matmul(pad_ref, flip_ref[l], True)
    grad_scaled = total.astype(BF).astype(F32)
    xf = x.astype(F32)
    grad_styles = jnp.sum(grad_scaled * xf, axis=0, keepdims=True)
    send_ref[l, 0:PX, :] = (xf * styles).astype(BF)
    send_ref[l, 2 * PX : 2 * PX + STAT, :] = pack_rows([grad_styles, grad_demod, grad_bias])
    return (grad_scaled * styles).astype(BF)


def first_kernel(images_any, a_ref, b_ref, out_ref, x_buf, pad_ref, x_sem):
    _, z, _ = place()
    x_copy = pltpu.make_async_copy(images_any.at[z], x_buf, x_sem)
    x_copy.start()
    clear_pads(pad_ref)
    x_copy.wait()
    x = x_buf[...]
    for l in range(DEPTH):
        stat = read_stats(a_ref, l)
        x = activate(forward_layer(x, l, a_ref, b_ref, stat, pad_ref), stat)
    out_ref[...] = x


def flip_kernel(a_ref, b_ref, flip_ref):
    _, _, core = place()
    for source, half in ((a_ref, core), (b_ref, 1 - core)):
        for l in range(DEPTH):
            for tap in range(TAPS):
                at = pl.ds(pl.multiple_of(tap * C + half * LANES, LANES), LANES)
                flip_ref[l, at, :] = source[l, tap * C : (tap + 1) * C, :].T


def middle_kernel(
    images_any, cot_any, recv_ref, a_ref, b_ref, flip_ref, dx_ref, xs_ref, conv_ref, send_ref,
    x_buf, u_buf, pad_ref, x_sem,
):
    half, z, _ = place()
    x_copy = pltpu.make_async_copy(images_any.at[z], x_buf, x_sem.at[0])
    u_copy = pltpu.make_async_copy(cot_any.at[z], u_buf, x_sem.at[1])
    x_copy.start()
    u_copy.start()
    clear_pads(pad_ref)
    x_copy.wait()
    x = jnp.where(half == 1, recv_ref[...], x_buf[...])
    stats = []
    for l in range(DEPTH):
        stats.append(read_stats(a_ref, l))
        xs_ref[l] = x
        conv = forward_layer(x, l, a_ref, b_ref, stats[l], pad_ref)
        conv_ref[l] = conv
        if l < DEPTH - 1:
            x = activate(conv, stats[l])
    u_copy.wait()
    upstream = u_buf[...]
    for l in reversed(range(DEPTH)):
        upstream = backward_layer(upstream, xs_ref[l], conv_ref[l], l, flip_ref, stats[l], pad_ref, send_ref)
    dx_ref[...] = upstream


def last_kernel(cot_any, recv_ref, xs_ref, conv_ref, flip_ref, a_ref, send_ref, u_buf, pad_ref, u_sem):
    half, z, _ = place()
    u_copy = pltpu.make_async_copy(cot_any.at[z], u_buf, u_sem)
    u_copy.start()
    clear_pads(pad_ref)
    u_copy.wait()
    upstream = jnp.where(half == 1, u_buf[...], recv_ref[...])
    for l in reversed(range(DEPTH)):
        stat = read_stats(a_ref, l)
        upstream = backward_layer(upstream, xs_ref[l], conv_ref[l], l, flip_ref, stat, pad_ref, send_ref)


MAP = jax.ShapeDtypeStruct((PX, C), BF)
KERNELS = jax.ShapeDtypeStruct((DEPTH, ROWS, C), BF)
SENT = jax.ShapeDtypeStruct((DEPTH, 2 * PX + STAT, C), BF)


def first(images, a, b):
    return pl.pallas_call(
        first_kernel,
        out_shape=MAP,
        in_specs=[any_spec(), vmem_spec(), vmem_spec()],
        out_specs=vmem_spec(),
        scratch_shapes=[
            pltpu.VMEM((PX, C), BF),
            pltpu.VMEM((3, PAD, C), BF),
            pltpu.SemaphoreType.DMA,
        ],
        compiler_params=params(),
        name="first",
    )(images, a, b)


def flip(a, b):
    return pl.pallas_call(
        flip_kernel,
        out_shape=KERNELS,
        in_specs=[vmem_spec()] * 2,
        out_specs=vmem_spec(),
        compiler_params=params(),
        name="flip",
    )(a, b)


def middle(images, cot, recv, a, b, flipped):
    return pl.pallas_call(
        middle_kernel,
        out_shape=(
            MAP,
            jax.ShapeDtypeStruct((DEPTH, PX, C), BF),
            jax.ShapeDtypeStruct((DEPTH, PX, C), F32),
            SENT,
        ),
        in_specs=[any_spec(), any_spec()] + [vmem_spec()] * 4,
        out_specs=(vmem_spec(),) * 4,
        scratch_shapes=[
            pltpu.VMEM((PX, C), BF),
            pltpu.VMEM((PX, C), BF),
            pltpu.VMEM((3, PAD, C), BF),
            pltpu.SemaphoreType.DMA((2,)),
        ],
        compiler_params=params(),
        name="middle",
    )(images, cot, recv, a, b, flipped)


def last(cot, recv, xs, conv, flipped, a):
    return pl.pallas_call(
        last_kernel,
        out_shape=SENT,
        in_specs=[any_spec()] + [vmem_spec()] * 5,
        out_specs=vmem_spec(),
        scratch_shapes=[
            pltpu.VMEM((PX, C), BF),
            pltpu.VMEM((3, PAD, C), BF),
            pltpu.SemaphoreType.DMA,
        ],
        compiler_params=params(),
        name="last",
    )(cot, recv, xs, conv, flipped, a)


def half_gradient(flip_ref, pad_ref, w_ref, grad_energy_ref, half, out_ref):
    first_row = pl.multiple_of(half * BLOCK, BLOCK)
    lhs = flip_ref[pl.ds(first_row, BLOCK), :]
    grad_energy = grad_energy_ref[pl.ds(first_row, BLOCK), :]
    for ky in range(3):
        for kx in range(3):
            tap = ky * 3 + kx
            rhs = jnp.concatenate(
                [pad_ref[n, 2 - kx, (2 - ky) * ROW : (2 - ky) * ROW + PX, :] for n in range(DEPTH)], axis=0
            )
            part = jnp.dot(lhs, rhs, preferred_element_type=F32)
            w = w_ref[pl.ds(pl.multiple_of(tap * C + half * BLOCK, BLOCK), BLOCK), :].astype(F32)
            out_ref[tap * BLOCK : (tap + 1) * BLOCK, :] = (part + w * grad_energy).astype(BF)


def give_kernel(
    r_ref, w_ref, styles_ref, demod_ref, energy_ref, affine_ref, latent_ref,
    give_ref, extra_ref, grad_latent_ref, flip_ref, pad_ref, grad_energy_ref, rows_ref,
):
    _, _, core = place()
    parts = [unpack_rows(r_ref[n, 2 * PX : 2 * PX + STAT, :]) for n in range(DEPTH)]
    styles = styles_ref[...]
    demod = demod_ref[...]
    grad_sum = stack_rows([p[1] for p in parts]) * (-0.5) * demod * demod * demod
    squares = styles * styles
    grad_squares = lax.dot_general(
        grad_sum, energy_ref[...], (((1,), (1,)), ((), ())), precision=HI, preferred_element_type=F32
    )
    grad_styles = stack_rows([p[0] for p in parts]) + 2.0 * styles * grad_squares
    grad_bias = parts[0][2] + parts[1][2] + parts[2][2] + parts[3][2]
    rows_ref[...] = jnp.zeros_like(rows_ref)
    rows_ref[0:DEPTH, :] = grad_styles[0:DEPTH]
    rows_ref[DEPTH : DEPTH + 1, :] = grad_bias
    rows_ref[8 : 8 + DEPTH, :] = latent_ref[:, 0:C]
    rows_ref[8 + DEPTH : 8 + 2 * DEPTH, :] = latent_ref[:, C : 2 * C]
    extra = rows_ref[...].astype(BF)
    extra_ref[...] = extra
    give_ref[HALF : HALF + STAT, :] = extra
    grad_latent = lax.dot_general(
        grad_styles, affine_ref[...], (((1,), (1,)), ((), ())), precision=HI, preferred_element_type=F32
    )
    grad_latent_ref[...] = grad_latent[0:DEPTH]
    grad_energy_ref[...] = 2.0 * lax.dot_general(
        squares, grad_sum, (((0,), (0,)), ((), ())), precision=HI, preferred_element_type=F32
    )
    for n in range(DEPTH):
        clear_pads(pad_ref.at[n])
        spread(pad_ref.at[n], r_ref[n, PX : 2 * PX, :].astype(F32))
        flip_ref[:, n * PX : (n + 1) * PX] = r_ref[n, 0:PX, :].astype(F32).T.astype(BF)
    half_gradient(flip_ref, pad_ref, w_ref, grad_energy_ref, 1 - core, give_ref)


def give_half(r, w, styles, demod, energy, affine, latent):
    return pl.pallas_call(
        give_kernel,
        out_shape=(
            jax.ShapeDtypeStruct((HALF + STAT, C), BF),
            jax.ShapeDtypeStruct((STAT, C), BF),
            jax.ShapeDtypeStruct((DEPTH, affine.shape[0]), F32),
            jax.ShapeDtypeStruct((C, DEPTH * PX), BF),
            jax.ShapeDtypeStruct((DEPTH, 3, PAD, C), BF),
            jax.ShapeDtypeStruct((C, C), F32),
        ),
        in_specs=[vmem_spec()] * 7,
        out_specs=(vmem_spec(),) * 6,
        scratch_shapes=[pltpu.VMEM((STAT, C), F32)],
        compiler_params=params(),
        name="give",
    )(r, w, styles, demod, energy, affine, latent)


def keep_kernel(flip_ref, pad_ref, w_ref, grad_energy_ref, keep_ref):
    _, _, core = place()
    half_gradient(flip_ref, pad_ref, w_ref, grad_energy_ref, core, keep_ref)


def keep_half(flipped, padded, w, grad_energy):
    return pl.pallas_call(
        keep_kernel,
        out_shape=jax.ShapeDtypeStruct((HALF, C), BF),
        in_specs=[vmem_spec()] * 4,
        out_specs=vmem_spec(),
        compiler_params=params(),
        name="keep",
    )(flipped, padded, w, grad_energy)


def pair_kernel(keep_ref, extra_ref, got_ref, out_ref):
    for k in range(PEERS):
        at = slice(k * SHARE, (k + 1) * SHARE)
        out_ref[k, 0:SHARE, :] = (keep_ref[at, :].astype(F32) + got_ref[at, :].astype(F32)).astype(BF)
        out_ref[k, SHARE : SHARE + STAT, :] = extra_ref[...]
        out_ref[k, SHARE + STAT : SHARE + 2 * STAT, :] = got_ref[HALF : HALF + STAT, :]


def pair(keep, extra, got):
    return pl.pallas_call(
        pair_kernel,
        out_shape=jax.ShapeDtypeStruct((PEERS, SHARE + 2 * STAT, C), BF),
        in_specs=[vmem_spec()] * 3,
        out_specs=vmem_spec(),
        compiler_params=params(),
        name="pair",
    )(keep, extra, got)


def share_kernel(shares_ref, out_ref):
    total = shares_ref[0, 0:SHARE, :].astype(F32)
    for k in range(1, PEERS):
        total += shares_ref[k, 0:SHARE, :].astype(F32)
    total = total.astype(BF)
    for k in range(PEERS):
        out_ref[k] = total


def share(shares):
    return pl.pallas_call(
        share_kernel,
        out_shape=jax.ShapeDtypeStruct((PEERS, SHARE, C), BF),
        in_specs=[vmem_spec()],
        out_specs=vmem_spec(),
        compiler_params=params(),
        name="share",
    )(shares)


def affine_kernel(shares_ref, affine_ref, bias_ref, grads_ref, low_ref, high_ref):
    row = lax.broadcasted_iota(jnp.int32, (STAT, C), 0)
    bias = jnp.zeros((1, C), F32)
    for k in range(2 * PEERS):
        start = SHARE + (k % 2) * STAT
        tile = shares_ref[k // 2, start : start + STAT, :].astype(F32)
        bias += tile[DEPTH : DEPTH + 1]
        at = slice(k * STAT, (k + 1) * STAT)
        grads_ref[at, :] = jnp.where(row < DEPTH, tile, 0.0).astype(BF)
        low_ref[at, :] = pltpu.roll(tile, 8, 0).astype(BF)
        high_ref[at, :] = pltpu.roll(tile, 4, 0).astype(BF)
    bias_ref[...] = bias
    for k, ref in enumerate((low_ref, high_ref)):
        affine_ref[k * C : (k + 1) * C, :] = lax.dot_general(
            ref[...], grads_ref[...], (((0,), (0,)), ((), ())), preferred_element_type=F32
        )


def affine_gradient(shares, width):
    return pl.pallas_call(
        affine_kernel,
        out_shape=(jax.ShapeDtypeStruct((width, C), F32), jax.ShapeDtypeStruct((1, C), F32)),
        in_specs=[vmem_spec()],
        out_specs=(vmem_spec(), vmem_spec()),
        scratch_shapes=[pltpu.VMEM((2 * PEERS * STAT, C), BF)] * 3,
        compiler_params=params(),
        name="affine",
    )(shares)


def widen_kernel(own, value_ref, *refs):
    out_any, wide_ref, sem = refs[-3:]
    _, _, core = place()
    half = core if own else 1 - core
    value = value_ref[...].reshape(TAPS, BLOCK, C)
    rows = pl.ds(pl.multiple_of(half * BLOCK, BLOCK), BLOCK)
    copies = []
    for k in range(3):
        taps = slice(3 * k, 3 * k + 3)
        wide_ref[taps] = value[taps].astype(F32)
        copies.append(pltpu.make_async_copy(wide_ref.at[taps], out_any.at[taps, rows], sem.at[k]))
        copies[k].start()
    for copy in copies:
        copy.wait()


def widen(value, target=None):
    hbm = pl.BlockSpec(memory_space=pltpu.HBM)
    args = (value,) if target is None else (value, target)
    return pl.pallas_call(
        functools.partial(widen_kernel, target is None),
        out_shape=jax.ShapeDtypeStruct((TAPS, C, C), F32),
        in_specs=[vmem_spec(), hbm][: len(args)],
        out_specs=hbm,
        input_output_aliases={1: 0} if len(args) == 2 else {},
        scratch_shapes=[pltpu.VMEM((TAPS, BLOCK, C), F32), pltpu.SemaphoreType.DMA((3,))],
        compiler_params=params(),
        name="own" if target is None else "rest",
    )(*args)


def body(images, latent, weight, affine, biases, cotangent):
    width = latent.shape[1]
    replicas = lax.axis_size("dp")
    segments = lax.axis_size("segment")
    planes = [list(range(k, k + DEPTH)) for k in range(0, segments, DEPTH)]
    across = [(i, (i + DEPTH) % segments) for i in range(segments)]
    sibling = [(i, i ^ 1) for i in range(replicas)]
    cores = [list(range(k, replicas, 2)) for k in range(2)]

    w = weight.reshape(ROWS, C)
    images = images.reshape(DEPTH, PX, C)
    cotangent = cotangent.reshape(DEPTH, PX, C)

    send, styles, demod, energy = prepare(latent, affine[0], w, biases)
    a = lax.all_to_all(send, "segment", 0, 0, axis_index_groups=planes)
    b = near(lax.ppermute(a, "dp", sibling))
    a = near(a)

    act = first(images, a, b)
    flipped = flip(a, b)
    arrived = near(lax.ppermute(act, "segment", across))
    dx, xs, conv, _ = middle(images, cotangent, arrived, a, b, flipped)
    returned = near(lax.ppermute(dx, "segment", across))
    sent = last(cotangent, returned, xs, conv, flipped, a)

    r = near(lax.all_to_all(sent, "segment", 0, 0, axis_index_groups=planes))
    give, extra, part, flipped_maps, padded, grad_energy = give_half(
        r, w, styles, demod, energy, affine[0], latent
    )
    got = near(lax.ppermute(give, "dp", sibling))
    part = part + lax.ppermute(part, "segment", across)
    keep = keep_half(flipped_maps, padded, w, grad_energy)
    shared, part = lax.optimization_barrier((pair(keep, extra, got), part))
    shares = near(lax.all_to_all(near(shared), "dp", 0, 0, axis_index_groups=cores))
    part = part + lax.ppermute(part, "segment", [(i, i ^ 1) for i in range(segments)])
    grad_latent = part + lax.ppermute(part, "segment", [(i, i ^ 2) for i in range(segments)])
    spread_share, grad_latent = lax.optimization_barrier((share(shares), grad_latent))
    mine = lax.all_to_all(near(spread_share), "dp", 0, 0, axis_index_groups=cores)
    other = near(lax.ppermute(mine, "dp", sibling))
    mine, shares = lax.optimization_barrier((mine, shares))
    grad_affine, grad_bias = affine_gradient(shares, width)
    grad_weight = widen(other, widen(near(mine))).reshape(weight.shape)
    return (grad_weight, grad_affine[None], grad_bias, grad_latent)


def solution(mesh):
    placed = (
        P("dp", None, None, None),
        P("dp", None),
        P("segment", None, None, None, None),
        P("segment", None, None),
        P("segment", None),
        P("dp", None, None, None),
    )
    return jax.shard_map(
        body,
        mesh=mesh,
        in_specs=placed,
        out_specs=(
            P("segment", None, None, None, None),
            P("segment", None, None),
            P("segment", None),
            P("dp", None),
        ),
        check_vma=False,
    )
```

```python
import functools
import math

import jax
import jax.numpy as jnp
from jax import lax
from jax.experimental import pallas as pl
from jax.experimental.pallas import tpu as pltpu
from jax.sharding import PartitionSpec as P

GAIN = math.sqrt(2.0)
EPS = 1e-08
BF = jnp.bfloat16
F32 = jnp.float32
C = 256
PX = 256
TAPS = 9
ROWS = TAPS * C
HALF = ROWS // 2
STAT = 16
DEPTH = 4
PEERS = 8
SHARE = HALF // PEERS
ROW = 16
BLOCK = 128
LANES = 128
PAD = PX + 2 * ROW
HI = lax.Precision.HIGHEST


def any_spec():
    return pl.BlockSpec(memory_space=pl.ANY)


def vmem_spec():
    return pl.BlockSpec(memory_space=pltpu.VMEM)


def params():
    return pltpu.CompilerParams(vmem_limit_bytes=28 << 20)


def near(value):
    return pltpu.with_memory_space_constraint(value, pltpu.VMEM)


def place():
    seg = lax.axis_index("segment")
    return seg // DEPTH, seg % DEPTH, lax.axis_index("dp") % 2


def split3(value):
    hi = value.astype(BF).astype(F32)
    rest = value - hi
    mid = rest.astype(BF).astype(F32)
    return hi, mid, rest - mid


def pack_rows(values):
    row = lax.broadcasted_iota(jnp.int32, (STAT, C), 0)
    out = jnp.zeros((STAT, C), F32)
    k = 0
    for value in values:
        for part in split3(value):
            out = jnp.where(row == k, jnp.broadcast_to(part, (STAT, C)), out)
            k += 1
    return out.astype(BF)


def unpack_rows(tile):
    t = tile.astype(F32)
    return [t[3 * k : 3 * k + 1] + t[3 * k + 1 : 3 * k + 2] + t[3 * k + 2 : 3 * k + 3] for k in range(3)]


def stack_rows(rows):
    index = lax.broadcasted_iota(jnp.int32, (8, C), 0)
    out = jnp.zeros((8, C), F32)
    for k, row in enumerate(rows):
        out = jnp.where(index == k, jnp.broadcast_to(row, (8, C)), out)
    return out


def prepare_kernel(
    latent_hbm, affine_hbm, w_hbm, bias_hbm, send_ref, styles_ref, demod_ref, energy_ref,
    rows_ref, affine_ref, w_ref, bias_ref, sem,
):
    _, _, core = place()
    mine = pl.ds(pl.multiple_of(core * LANES, LANES), LANES)
    rows_ref[...] = jnp.zeros_like(rows_ref)
    third = ROWS // 3
    loads = [
        pltpu.make_async_copy(affine_hbm, affine_ref, sem.at[0]),
        pltpu.make_async_copy(latent_hbm, rows_ref.at[pl.ds(0, DEPTH)], sem.at[1]),
        pltpu.make_async_copy(bias_hbm, bias_ref, sem.at[2]),
    ] + [
        pltpu.make_async_copy(w_hbm.at[pl.ds(k * third, third)], w_ref.at[pl.ds(k * third, third)], sem.at[3 + k])
        for k in range(3)
    ]
    sends = [
        pltpu.make_async_copy(w_hbm.at[:, mine], send_ref.at[k, pl.ds(0, ROWS)], sem.at[6 + k]) for k in range(DEPTH)
    ]
    for copy in loads + sends:
        copy.start()
    for copy in loads[:3]:
        copy.wait()
    styles = jnp.dot(rows_ref[...], affine_ref[...], precision=HI, preferred_element_type=F32) + 1.0
    energy = jnp.zeros((C, C), F32)
    for tap in range(TAPS):
        if tap % 3 == 0:
            loads[3 + tap // 3].wait()
        part = w_ref[tap * C : (tap + 1) * C, :].astype(F32)
        energy += part * part
    energy_ref[...] = energy
    demod = lax.rsqrt(jnp.dot(styles * styles, energy, precision=HI, preferred_element_type=F32) + EPS)
    styles_ref[...] = styles
    demod_ref[...] = demod
    for k in range(DEPTH):
        tile = pack_rows([styles[k : k + 1], demod[k : k + 1], bias_ref[...]])
        send_ref[k, ROWS : ROWS + STAT, :] = tile[:, :LANES]
        send_ref[k, ROWS + STAT : ROWS + 2 * STAT, :] = tile[:, LANES:]
    for copy in sends:
        copy.wait()


def prepare(latent, affine, w, bias):
    far = [pltpu.with_memory_space_constraint(value, pltpu.HBM) for value in (latent, affine, w, bias)]
    return pl.pallas_call(
        prepare_kernel,
        out_shape=(
            jax.ShapeDtypeStruct((DEPTH, ROWS + 2 * STAT, LANES), BF),
            jax.ShapeDtypeStruct((8, C), F32),
            jax.ShapeDtypeStruct((8, C), F32),
            jax.ShapeDtypeStruct((C, C), F32),
        ),
        in_specs=[pl.BlockSpec(memory_space=pltpu.HBM)] * 4,
        out_specs=(vmem_spec(),) * 4,
        scratch_shapes=[
            pltpu.VMEM((8, latent.shape[1]), F32),
            pltpu.VMEM(affine.shape, F32),
            pltpu.VMEM((ROWS, C), BF),
            pltpu.VMEM((1, C), F32),
            pltpu.SemaphoreType.DMA((6 + DEPTH,)),
        ],
        compiler_params=params(),
        name="prepare",
    )(*far)


def read_stats(a_ref, l):
    return unpack_rows(
        jnp.concatenate(
            [a_ref[l, ROWS : ROWS + STAT, :], a_ref[l, ROWS + STAT : ROWS + 2 * STAT, :]], axis=1
        )
    )


def clear_pads(pad_ref):
    for k in range(3):
        pad_ref[k, 0:ROW, :] = jnp.zeros((ROW, C), BF)
        pad_ref[k, ROW + PX : PAD, :] = jnp.zeros((ROW, C), BF)


def spread(pad_ref, value):
    column = lax.broadcasted_iota(jnp.int32, (PX, C), 0) % ROW
    pad_ref[1, ROW : ROW + PX, :] = value.astype(BF)
    pad_ref[0, ROW : ROW + PX, :] = jnp.where(column == 0, 0.0, pltpu.roll(value, 1, 0)).astype(BF)
    pad_ref[2, ROW : ROW + PX, :] = jnp.where(column == ROW - 1, 0.0, pltpu.roll(value, PX - 1, 0)).astype(BF)


def taps_matmul(pad_ref, w, mirrored):
    out = []
    for start in range(0, PX, BLOCK):
        pieces = []
        for ky in range(3):
            for kx in range(3):
                plane, shift = (2 - kx, 2 - ky) if mirrored else (kx, ky)
                first_row = start + shift * ROW
                pieces.append(pad_ref[plane, first_row : first_row + BLOCK, :])
        out.append(jnp.dot(jnp.concatenate(pieces, axis=1), w, preferred_element_type=F32))
    return jnp.concatenate(out, axis=0)


def forward_layer(x, l, a_ref, b_ref, stat, pad_ref):
    styles, demod, bias = stat
    spread(pad_ref, (x.astype(F32) * styles).astype(BF).astype(F32))
    _, _, core = place()
    w = jnp.concatenate([a_ref[l, 0:ROWS, :], b_ref[l, 0:ROWS, :]], axis=1)
    conv = taps_matmul(pad_ref, w, False)
    return jnp.where(core == 0, conv, jnp.concatenate([conv[:, LANES:], conv[:, :LANES]], axis=1))


def activate(conv, stat):
    _, demod, bias = stat
    hidden = conv * demod + bias
    return (GAIN * hidden * (0.6 + 0.4 * jnp.tanh(hidden))).astype(BF)


def backward_layer(upstream, x, conv, l, flip_ref, stat, pad_ref, send_ref=None):
    styles, demod, bias = stat
    hidden = conv * demod + bias
    t = jnp.tanh(hidden)
    dh = upstream.astype(F32) * (GAIN * (0.6 + 0.4 * t + 0.4 * hidden * (1.0 - t * t)))
    spread(pad_ref, (dh * demod).astype(BF).astype(F32))
    grad_scaled = taps_matmul(pad_ref, flip_ref[l], True).astype(BF).astype(F32)
    if send_ref is not None:
        grad_bias = jnp.sum(dh, axis=0, keepdims=True)
        grad_demod = jnp.sum(dh * conv, axis=0, keepdims=True)
        grad_styles = jnp.sum(grad_scaled * x.astype(F32), axis=0, keepdims=True)
        send_ref[l, 0:PX, :] = pad_ref[1, ROW : ROW + PX, :]
        send_ref[l, PX : PX + STAT, :] = pack_rows([grad_styles, grad_demod, grad_bias])
    return (grad_scaled * styles).astype(BF)


def first_kernel(images_any, a_ref, b_ref, out_ref, x_buf, pad_ref, x_sem):
    _, z, _ = place()
    x_copy = pltpu.make_async_copy(images_any.at[z], x_buf, x_sem)
    x_copy.start()
    clear_pads(pad_ref)
    x_copy.wait()
    x = x_buf[...]
    for l in range(DEPTH):
        stat = read_stats(a_ref, l)
        x = activate(forward_layer(x, l, a_ref, b_ref, stat, pad_ref), stat)
    out_ref[...] = x


def flip_kernel(a_ref, b_ref, flip_ref):
    _, _, core = place()
    for source, half in ((a_ref, core), (b_ref, 1 - core)):
        for l in range(DEPTH):
            for tap in range(TAPS):
                at = pl.ds(pl.multiple_of(tap * C + half * LANES, LANES), LANES)
                flip_ref[l, at, :] = source[l, tap * C : (tap + 1) * C, :].T


def middle_kernel(
    images_any, cot_any, recv_ref, a_ref, b_ref, flip_ref, dx_ref, xs_ref, conv_ref, scaled_ref,
    x_buf, u_buf, pad_ref, x_sem,
):
    half, z, _ = place()
    x_copy = pltpu.make_async_copy(images_any.at[z], x_buf, x_sem.at[0])
    u_copy = pltpu.make_async_copy(cot_any.at[z], u_buf, x_sem.at[1])
    x_copy.start()
    u_copy.start()
    clear_pads(pad_ref)
    x_copy.wait()
    x = jnp.where(half == 1, recv_ref[...], x_buf[...])
    stats = []
    for l in range(DEPTH):
        stats.append(read_stats(a_ref, l))
        xs_ref[l] = x
        conv = forward_layer(x, l, a_ref, b_ref, stats[l], pad_ref)
        conv_ref[l] = conv
        scaled_ref[lax.rem(l - z + DEPTH, DEPTH)] = pad_ref[1, ROW : ROW + PX, :]
        if l < DEPTH - 1:
            x = activate(conv, stats[l])
    u_copy.wait()
    upstream = u_buf[...]
    for l in reversed(range(DEPTH)):
        upstream = backward_layer(upstream, xs_ref[l], conv_ref[l], l, flip_ref, stats[l], pad_ref)
    dx_ref[...] = upstream


def last_kernel(cot_any, recv_ref, xs_ref, conv_ref, flip_ref, a_ref, send_ref, u_buf, pad_ref, u_sem):
    half, z, _ = place()
    u_copy = pltpu.make_async_copy(cot_any.at[z], u_buf, u_sem)
    u_copy.start()
    clear_pads(pad_ref)
    u_copy.wait()
    upstream = jnp.where(half == 1, u_buf[...], recv_ref[...])
    for l in reversed(range(DEPTH)):
        stat = read_stats(a_ref, l)
        upstream = backward_layer(upstream, xs_ref[l], conv_ref[l], l, flip_ref, stat, pad_ref, send_ref)


MAP = jax.ShapeDtypeStruct((PX, C), BF)
KERNELS = jax.ShapeDtypeStruct((DEPTH, ROWS, C), BF)
SENT = jax.ShapeDtypeStruct((DEPTH, PX + STAT, C), BF)


def first(images, a, b):
    return pl.pallas_call(
        first_kernel,
        out_shape=MAP,
        in_specs=[any_spec(), vmem_spec(), vmem_spec()],
        out_specs=vmem_spec(),
        scratch_shapes=[
            pltpu.VMEM((PX, C), BF),
            pltpu.VMEM((3, PAD, C), BF),
            pltpu.SemaphoreType.DMA,
        ],
        compiler_params=params(),
        name="first",
    )(images, a, b)


def flip(a, b):
    return pl.pallas_call(
        flip_kernel,
        out_shape=KERNELS,
        in_specs=[vmem_spec()] * 2,
        out_specs=vmem_spec(),
        compiler_params=params(),
        name="flip",
    )(a, b)


def middle(images, cot, recv, a, b, flipped):
    return pl.pallas_call(
        middle_kernel,
        out_shape=(
            MAP,
            jax.ShapeDtypeStruct((DEPTH, PX, C), BF),
            jax.ShapeDtypeStruct((DEPTH, PX, C), F32),
            jax.ShapeDtypeStruct((DEPTH, PX, C), BF),
        ),
        in_specs=[any_spec(), any_spec()] + [vmem_spec()] * 4,
        out_specs=(vmem_spec(),) * 4,
        scratch_shapes=[
            pltpu.VMEM((PX, C), BF),
            pltpu.VMEM((PX, C), BF),
            pltpu.VMEM((3, PAD, C), BF),
            pltpu.SemaphoreType.DMA((2,)),
        ],
        compiler_params=params(),
        name="middle",
    )(images, cot, recv, a, b, flipped)


def last(cot, recv, xs, conv, flipped, a):
    return pl.pallas_call(
        last_kernel,
        out_shape=SENT,
        in_specs=[any_spec()] + [vmem_spec()] * 5,
        out_specs=vmem_spec(),
        scratch_shapes=[
            pltpu.VMEM((PX, C), BF),
            pltpu.VMEM((3, PAD, C), BF),
            pltpu.SemaphoreType.DMA,
        ],
        compiler_params=params(),
        name="last",
    )(cot, recv, xs, conv, flipped, a)


def half_gradient(flip_ref, pad_ref, w_ref, grad_energy_ref, half, out_ref):
    first_row = pl.multiple_of(half * BLOCK, BLOCK)
    lhs = flip_ref[pl.ds(first_row, BLOCK), :]
    grad_energy = grad_energy_ref[pl.ds(first_row, BLOCK), :]
    for ky in range(3):
        for kx in range(3):
            tap = ky * 3 + kx
            rhs = jnp.concatenate(
                [pad_ref[n, 2 - kx, (2 - ky) * ROW : (2 - ky) * ROW + PX, :] for n in range(DEPTH)], axis=0
            )
            part = jnp.dot(lhs, rhs, preferred_element_type=F32)
            w = w_ref[pl.ds(pl.multiple_of(tap * C + half * BLOCK, BLOCK), BLOCK), :].astype(F32)
            out_ref[tap * BLOCK : (tap + 1) * BLOCK, :] = (part + w * grad_energy).astype(BF)


def turn_kernel(s0_ref, s1_ref, s2_ref, s3_ref, flip_ref):
    for k, ref in enumerate((s0_ref, s1_ref, s2_ref, s3_ref)):
        flip_ref[:, k * PX : (k + 1) * PX] = ref[...].T


def turn(*maps):
    return pl.pallas_call(
        turn_kernel,
        out_shape=jax.ShapeDtypeStruct((C, DEPTH * PX), BF),
        in_specs=[vmem_spec()] * DEPTH,
        out_specs=vmem_spec(),
        compiler_params=params(),
        name="turn",
    )(*maps)


def give_kernel(
    r_ref, flip_ref, w_ref, styles_ref, demod_ref, energy_ref, affine_ref, latent_ref,
    give_ref, extra_ref, grad_latent_ref, pad_ref, grad_energy_ref, rows_ref,
):
    _, z, core = place()
    parts = [unpack_rows(r_ref[n, PX : PX + STAT, :]) for n in range(DEPTH)]
    styles = styles_ref[...]
    demod = demod_ref[...]
    grad_sum = stack_rows([p[1] for p in parts]) * (-0.5) * demod * demod * demod
    squares = styles * styles
    grad_squares = lax.dot_general(
        grad_sum, energy_ref[...], (((1,), (1,)), ((), ())), precision=HI, preferred_element_type=F32
    )
    grad_styles = stack_rows([p[0] for p in parts]) + 2.0 * styles * grad_squares
    grad_bias = parts[0][2] + parts[1][2] + parts[2][2] + parts[3][2]
    rows_ref[...] = jnp.zeros_like(rows_ref)
    rows_ref[0:DEPTH, :] = grad_styles[0:DEPTH]
    rows_ref[DEPTH : DEPTH + 1, :] = grad_bias
    rows_ref[8 : 8 + DEPTH, :] = latent_ref[:, 0:C]
    rows_ref[8 + DEPTH : 8 + 2 * DEPTH, :] = latent_ref[:, C : 2 * C]
    extra = rows_ref[...].astype(BF)
    extra_ref[...] = extra
    give_ref[HALF : HALF + STAT, :] = extra
    grad_latent = lax.dot_general(
        grad_styles, affine_ref[...], (((1,), (1,)), ((), ())), precision=HI, preferred_element_type=F32
    )
    grad_latent_ref[...] = grad_latent[0:DEPTH]
    grad_energy_ref[...] = 2.0 * lax.dot_general(
        squares, grad_sum, (((0,), (0,)), ((), ())), precision=HI, preferred_element_type=F32
    )
    for k in range(DEPTH):
        clear_pads(pad_ref.at[k])
        spread(pad_ref.at[k], r_ref[lax.rem(z - k + DEPTH, DEPTH), 0:PX, :].astype(F32))
    half_gradient(flip_ref, pad_ref, w_ref, grad_energy_ref, 1 - core, give_ref)


def give_half(r, turned, w, styles, demod, energy, affine, latent):
    return pl.pallas_call(
        give_kernel,
        out_shape=(
            jax.ShapeDtypeStruct((HALF + STAT, C), BF),
            jax.ShapeDtypeStruct((STAT, C), BF),
            jax.ShapeDtypeStruct((DEPTH, affine.shape[0]), F32),
            jax.ShapeDtypeStruct((DEPTH, 3, PAD, C), BF),
            jax.ShapeDtypeStruct((C, C), F32),
        ),
        in_specs=[vmem_spec()] * 8,
        out_specs=(vmem_spec(),) * 5,
        scratch_shapes=[pltpu.VMEM((STAT, C), F32)],
        compiler_params=params(),
        name="give",
    )(r, turned, w, styles, demod, energy, affine, latent)


def keep_kernel(flip_ref, pad_ref, w_ref, grad_energy_ref, keep_ref):
    _, _, core = place()
    half_gradient(flip_ref, pad_ref, w_ref, grad_energy_ref, core, keep_ref)


def keep_half(flipped, padded, w, grad_energy):
    return pl.pallas_call(
        keep_kernel,
        out_shape=jax.ShapeDtypeStruct((HALF, C), BF),
        in_specs=[vmem_spec()] * 4,
        out_specs=vmem_spec(),
        compiler_params=params(),
        name="keep",
    )(flipped, padded, w, grad_energy)


def pair_kernel(keep_ref, extra_ref, got_ref, out_ref):
    for k in range(PEERS):
        at = slice(k * SHARE, (k + 1) * SHARE)
        out_ref[k, 0:SHARE, :] = (keep_ref[at, :].astype(F32) + got_ref[at, :].astype(F32)).astype(BF)
        out_ref[k, SHARE : SHARE + STAT, :] = extra_ref[...]
        out_ref[k, SHARE + STAT : SHARE + 2 * STAT, :] = got_ref[HALF : HALF + STAT, :]


def pair(keep, extra, got):
    return pl.pallas_call(
        pair_kernel,
        out_shape=jax.ShapeDtypeStruct((PEERS, SHARE + 2 * STAT, C), BF),
        in_specs=[vmem_spec()] * 3,
        out_specs=vmem_spec(),
        compiler_params=params(),
        name="pair",
    )(keep, extra, got)


def share_kernel(shares_ref, out_ref):
    total = shares_ref[0, 0:SHARE, :].astype(F32)
    for k in range(1, PEERS):
        total += shares_ref[k, 0:SHARE, :].astype(F32)
    total = total.astype(BF)
    for k in range(PEERS):
        out_ref[k] = total


def share(shares):
    return pl.pallas_call(
        share_kernel,
        out_shape=jax.ShapeDtypeStruct((PEERS, SHARE, C), BF),
        in_specs=[vmem_spec()],
        out_specs=vmem_spec(),
        compiler_params=params(),
        name="share",
    )(shares)


def affine_kernel(shares_ref, affine_ref, bias_ref, grads_ref, low_ref, high_ref):
    row = lax.broadcasted_iota(jnp.int32, (STAT, C), 0)
    bias = jnp.zeros((1, C), F32)
    for k in range(2 * PEERS):
        start = SHARE + (k % 2) * STAT
        tile = shares_ref[k // 2, start : start + STAT, :].astype(F32)
        bias += tile[DEPTH : DEPTH + 1]
        at = slice(k * STAT, (k + 1) * STAT)
        grads_ref[at, :] = jnp.where(row < DEPTH, tile, 0.0).astype(BF)
        low_ref[at, :] = pltpu.roll(tile, 8, 0).astype(BF)
        high_ref[at, :] = pltpu.roll(tile, 4, 0).astype(BF)
    bias_ref[...] = bias
    for k, ref in enumerate((low_ref, high_ref)):
        affine_ref[k * C : (k + 1) * C, :] = lax.dot_general(
            ref[...], grads_ref[...], (((0,), (0,)), ((), ())), preferred_element_type=F32
        )


def affine_gradient(shares, width):
    return pl.pallas_call(
        affine_kernel,
        out_shape=(jax.ShapeDtypeStruct((width, C), F32), jax.ShapeDtypeStruct((1, C), F32)),
        in_specs=[vmem_spec()],
        out_specs=(vmem_spec(), vmem_spec()),
        scratch_shapes=[pltpu.VMEM((2 * PEERS * STAT, C), BF)] * 3,
        compiler_params=params(),
        name="affine",
    )(shares)


def widen_kernel(own, value_ref, *refs):
    out_any, wide_ref, sem = refs[-3:]
    _, _, core = place()
    half = core if own else 1 - core
    value = value_ref[...].reshape(TAPS, BLOCK, C)
    rows = pl.ds(pl.multiple_of(half * BLOCK, BLOCK), BLOCK)
    copies = []
    for k in range(3):
        taps = slice(3 * k, 3 * k + 3)
        wide_ref[taps] = value[taps].astype(F32)
        copies.append(pltpu.make_async_copy(wide_ref.at[taps], out_any.at[taps, rows], sem.at[k]))
        copies[k].start()
    for copy in copies:
        copy.wait()


def widen(value, target=None):
    hbm = pl.BlockSpec(memory_space=pltpu.HBM)
    args = (value,) if target is None else (value, target)
    return pl.pallas_call(
        functools.partial(widen_kernel, target is None),
        out_shape=jax.ShapeDtypeStruct((TAPS, C, C), F32),
        in_specs=[vmem_spec(), hbm][: len(args)],
        out_specs=hbm,
        input_output_aliases={1: 0} if len(args) == 2 else {},
        scratch_shapes=[pltpu.VMEM((TAPS, BLOCK, C), F32), pltpu.SemaphoreType.DMA((3,))],
        compiler_params=params(),
        name="own" if target is None else "rest",
    )(*args)


def body(images, latent, weight, affine, biases, cotangent):
    width = latent.shape[1]
    replicas = lax.axis_size("dp")
    segments = lax.axis_size("segment")
    planes = [list(range(k, k + DEPTH)) for k in range(0, segments, DEPTH)]
    across = [(i, (i + DEPTH) % segments) for i in range(segments)]
    sibling = [(i, i ^ 1) for i in range(replicas)]
    cores = [list(range(k, replicas, 2)) for k in range(2)]

    w = weight.reshape(ROWS, C)
    images = images.reshape(DEPTH, PX, C)
    cotangent = cotangent.reshape(DEPTH, PX, C)

    send, styles, demod, energy = prepare(latent, affine[0], w, biases)
    a = lax.all_to_all(send, "segment", 0, 0, axis_index_groups=planes)
    b = near(lax.ppermute(a, "dp", sibling))
    a = near(a)

    act = first(images, a, b)
    flipped = flip(a, b)
    arrived = near(lax.ppermute(act, "segment", across))
    dx, xs, conv, scaled = middle(images, cotangent, arrived, a, b, flipped)
    returned = near(lax.ppermute(dx, "segment", across))
    maps = [scaled[0]] + [
        lax.ppermute(
            scaled[k], "segment", [(i, i - i % DEPTH + (i + k) % DEPTH) for i in range(segments)]
        )
        for k in range(1, DEPTH)
    ]
    sent, *maps = lax.optimization_barrier((last(cotangent, returned, xs, conv, flipped, a), *maps))
    turned = turn(*[near(value) for value in maps])

    r = near(lax.all_to_all(sent, "segment", 0, 0, axis_index_groups=planes))
    give, extra, part, padded, grad_energy = give_half(
        r, turned, w, styles, demod, energy, affine[0], latent
    )
    got = near(lax.ppermute(give, "dp", sibling))
    part = part + lax.ppermute(part, "segment", across)
    keep = keep_half(turned, padded, w, grad_energy)
    shared, part = lax.optimization_barrier((pair(keep, extra, got), part))
    shares = near(lax.all_to_all(near(shared), "dp", 0, 0, axis_index_groups=cores))
    part = part + lax.ppermute(part, "segment", [(i, i ^ 1) for i in range(segments)])
    grad_latent = part + lax.ppermute(part, "segment", [(i, i ^ 2) for i in range(segments)])
    spread_share, grad_latent = lax.optimization_barrier((share(shares), grad_latent))
    mine = lax.all_to_all(near(spread_share), "dp", 0, 0, axis_index_groups=cores)
    other = near(lax.ppermute(mine, "dp", sibling))
    mine, shares = lax.optimization_barrier((mine, shares))
    grad_affine, grad_bias = affine_gradient(shares, width)
    grad_weight = widen(other, widen(near(mine))).reshape(weight.shape)
    return (grad_weight, grad_affine[None], grad_bias, grad_latent)


def solution(mesh):
    placed = (
        P("dp", None, None, None),
        P("dp", None),
        P("segment", None, None, None, None),
        P("segment", None, None),
        P("segment", None),
        P("dp", None, None, None),
    )
    return jax.shard_map(
        body,
        mesh=mesh,
        in_specs=placed,
        out_specs=(
            P("segment", None, None, None, None),
            P("segment", None, None),
            P("segment", None),
            P("dp", None),
        ),
        check_vma=False,
    )
```

```python
import math

import jax
import jax.numpy as jnp
from jax import lax
from jax.experimental import pallas as pl
from jax.experimental.pallas import tpu as pltpu
from jax.sharding import PartitionSpec as P

GAIN = math.sqrt(2.0)
EPS = 1e-08
BF = jnp.bfloat16
F32 = jnp.float32
C = 256
PX = 256
TAPS = 9
ROWS = TAPS * C
HALF = ROWS // 2
STAT = 16
DEPTH = 4
PEERS = 8
SHARE = HALF // PEERS
ROW = 16
BLOCK = 128
LANES = 128
PAD = PX + 2 * ROW
HI = lax.Precision.HIGHEST


def any_spec():
    return pl.BlockSpec(memory_space=pl.ANY)


def vmem_spec():
    return pl.BlockSpec(memory_space=pltpu.VMEM)


def params():
    return pltpu.CompilerParams(vmem_limit_bytes=28 << 20)


def near(value):
    return pltpu.with_memory_space_constraint(value, pltpu.VMEM)


def place():
    seg = lax.axis_index("segment")
    return seg // DEPTH, seg % DEPTH, lax.axis_index("dp") % 2


def split3(value):
    hi = value.astype(BF).astype(F32)
    rest = value - hi
    mid = rest.astype(BF).astype(F32)
    return hi, mid, rest - mid


def pack_rows(values):
    row = lax.broadcasted_iota(jnp.int32, (STAT, C), 0)
    out = jnp.zeros((STAT, C), F32)
    k = 0
    for value in values:
        for part in split3(value):
            out = jnp.where(row == k, jnp.broadcast_to(part, (STAT, C)), out)
            k += 1
    return out.astype(BF)


def unpack_rows(tile):
    t = tile.astype(F32)
    return [t[3 * k : 3 * k + 1] + t[3 * k + 1 : 3 * k + 2] + t[3 * k + 2 : 3 * k + 3] for k in range(3)]


def stack_rows(rows):
    index = lax.broadcasted_iota(jnp.int32, (8, C), 0)
    out = jnp.zeros((8, C), F32)
    for k, row in enumerate(rows):
        out = jnp.where(index == k, jnp.broadcast_to(row, (8, C)), out)
    return out


def prepare_kernel(
    latent_hbm, affine_hbm, w_hbm, bias_hbm, send_ref, styles_ref, demod_ref, energy_ref,
    rows_ref, affine_ref, w_ref, bias_ref, sem,
):
    _, _, core = place()
    mine = pl.ds(pl.multiple_of(core * LANES, LANES), LANES)
    rows_ref[...] = jnp.zeros_like(rows_ref)
    third = ROWS // 3
    loads = [
        pltpu.make_async_copy(affine_hbm, affine_ref, sem.at[0]),
        pltpu.make_async_copy(latent_hbm, rows_ref.at[pl.ds(0, DEPTH)], sem.at[1]),
        pltpu.make_async_copy(bias_hbm, bias_ref, sem.at[2]),
    ] + [
        pltpu.make_async_copy(w_hbm.at[pl.ds(k * third, third)], w_ref.at[pl.ds(k * third, third)], sem.at[3 + k])
        for k in range(3)
    ]
    sends = [
        pltpu.make_async_copy(w_hbm.at[:, mine], send_ref.at[k, pl.ds(0, ROWS)], sem.at[6 + k]) for k in range(DEPTH)
    ]
    for copy in loads + sends:
        copy.start()
    for copy in loads[:3]:
        copy.wait()
    styles = jnp.dot(rows_ref[...], affine_ref[...], precision=HI, preferred_element_type=F32) + 1.0
    energy = jnp.zeros((C, C), F32)
    for tap in range(TAPS):
        if tap % 3 == 0:
            loads[3 + tap // 3].wait()
        part = w_ref[tap * C : (tap + 1) * C, :].astype(F32)
        energy += part * part
    energy_ref[...] = energy
    demod = lax.rsqrt(jnp.dot(styles * styles, energy, precision=HI, preferred_element_type=F32) + EPS)
    styles_ref[...] = styles
    demod_ref[...] = demod
    for k in range(DEPTH):
        tile = pack_rows([styles[k : k + 1], demod[k : k + 1], bias_ref[...]])
        send_ref[k, ROWS : ROWS + STAT, :] = tile[:, :LANES]
        send_ref[k, ROWS + STAT : ROWS + 2 * STAT, :] = tile[:, LANES:]
    for copy in sends:
        copy.wait()


def prepare(latent, affine, w, bias):
    far = [pltpu.with_memory_space_constraint(value, pltpu.HBM) for value in (latent, affine, w, bias)]
    return pl.pallas_call(
        prepare_kernel,
        out_shape=(
            jax.ShapeDtypeStruct((DEPTH, ROWS + 2 * STAT, LANES), BF),
            jax.ShapeDtypeStruct((8, C), F32),
            jax.ShapeDtypeStruct((8, C), F32),
            jax.ShapeDtypeStruct((C, C), F32),
        ),
        in_specs=[pl.BlockSpec(memory_space=pltpu.HBM)] * 4,
        out_specs=(vmem_spec(),) * 4,
        scratch_shapes=[
            pltpu.VMEM((8, latent.shape[1]), F32),
            pltpu.VMEM(affine.shape, F32),
            pltpu.VMEM((ROWS, C), BF),
            pltpu.VMEM((1, C), F32),
            pltpu.SemaphoreType.DMA((6 + DEPTH,)),
        ],
        compiler_params=params(),
        name="prepare",
    )(*far)


def read_stats(a_ref, l):
    return unpack_rows(
        jnp.concatenate(
            [a_ref[l, ROWS : ROWS + STAT, :], a_ref[l, ROWS + STAT : ROWS + 2 * STAT, :]], axis=1
        )
    )


def clear_pads(pad_ref):
    for k in range(3):
        pad_ref[k, 0:ROW, :] = jnp.zeros((ROW, C), BF)
        pad_ref[k, ROW + PX : PAD, :] = jnp.zeros((ROW, C), BF)


def spread(pad_ref, value):
    column = lax.broadcasted_iota(jnp.int32, (PX, C), 0) % ROW
    pad_ref[1, ROW : ROW + PX, :] = value.astype(BF)
    pad_ref[0, ROW : ROW + PX, :] = jnp.where(column == 0, 0.0, pltpu.roll(value, 1, 0)).astype(BF)
    pad_ref[2, ROW : ROW + PX, :] = jnp.where(column == ROW - 1, 0.0, pltpu.roll(value, PX - 1, 0)).astype(BF)


def taps_matmul(pad_ref, w, mirrored):
    out = []
    for start in range(0, PX, BLOCK):
        pieces = []
        for ky in range(3):
            for kx in range(3):
                plane, shift = (2 - kx, 2 - ky) if mirrored else (kx, ky)
                first_row = start + shift * ROW
                pieces.append(pad_ref[plane, first_row : first_row + BLOCK, :])
        out.append(jnp.dot(jnp.concatenate(pieces, axis=1), w, preferred_element_type=F32))
    return jnp.concatenate(out, axis=0)


def forward_layer(x, l, a_ref, b_ref, stat, pad_ref):
    styles, demod, bias = stat
    spread(pad_ref, (x.astype(F32) * styles).astype(BF).astype(F32))
    _, _, core = place()
    w = jnp.concatenate([a_ref[l, 0:ROWS, :], b_ref[l, 0:ROWS, :]], axis=1)
    conv = taps_matmul(pad_ref, w, False)
    return jnp.where(core == 0, conv, jnp.concatenate([conv[:, LANES:], conv[:, :LANES]], axis=1))


def activate(conv, stat):
    _, demod, bias = stat
    hidden = conv * demod + bias
    return (GAIN * hidden * (0.6 + 0.4 * jnp.tanh(hidden))).astype(BF)


def backward_layer(upstream, x, conv, l, flip_ref, stat, pad_ref, send_ref=None):
    styles, demod, bias = stat
    hidden = conv * demod + bias
    t = jnp.tanh(hidden)
    dh = upstream.astype(F32) * (GAIN * (0.6 + 0.4 * t + 0.4 * hidden * (1.0 - t * t)))
    spread(pad_ref, (dh * demod).astype(BF).astype(F32))
    grad_scaled = taps_matmul(pad_ref, flip_ref[l], True).astype(BF).astype(F32)
    if send_ref is not None:
        grad_bias = jnp.sum(dh, axis=0, keepdims=True)
        grad_demod = jnp.sum(dh * conv, axis=0, keepdims=True)
        grad_styles = jnp.sum(grad_scaled * x.astype(F32), axis=0, keepdims=True)
        send_ref[l, 0:PX, :] = pad_ref[1, ROW : ROW + PX, :]
        send_ref[l, PX : PX + STAT, :] = pack_rows([grad_styles, grad_demod, grad_bias])
    return (grad_scaled * styles).astype(BF)


def first_kernel(images_any, a_ref, b_ref, out_ref, x_buf, pad_ref, x_sem):
    _, z, _ = place()
    x_copy = pltpu.make_async_copy(images_any.at[z], x_buf, x_sem)
    x_copy.start()
    clear_pads(pad_ref)
    x_copy.wait()
    x = x_buf[...]
    for l in range(DEPTH):
        stat = read_stats(a_ref, l)
        x = activate(forward_layer(x, l, a_ref, b_ref, stat, pad_ref), stat)
    out_ref[...] = x


def flip_kernel(a_ref, b_ref, flip_ref):
    _, _, core = place()
    for source, half in ((a_ref, core), (b_ref, 1 - core)):
        for l in range(DEPTH):
            for tap in range(TAPS):
                at = pl.ds(pl.multiple_of(tap * C + half * LANES, LANES), LANES)
                flip_ref[l, at, :] = source[l, tap * C : (tap + 1) * C, :].T


def middle_kernel(
    images_any, cot_any, recv_ref, a_ref, b_ref, flip_ref, dx_ref, xs_ref, conv_ref, scaled_ref,
    x_buf, u_buf, pad_ref, x_sem,
):
    half, z, _ = place()
    x_copy = pltpu.make_async_copy(images_any.at[z], x_buf, x_sem.at[0])
    u_copy = pltpu.make_async_copy(cot_any.at[z], u_buf, x_sem.at[1])
    x_copy.start()
    u_copy.start()
    clear_pads(pad_ref)
    x_copy.wait()
    x = jnp.where(half == 1, recv_ref[...], x_buf[...])
    stats = []
    for l in range(DEPTH):
        stats.append(read_stats(a_ref, l))
        xs_ref[l] = x
        conv = forward_layer(x, l, a_ref, b_ref, stats[l], pad_ref)
        conv_ref[l] = conv
        scaled_ref[lax.rem(l - z + DEPTH, DEPTH)] = pad_ref[1, ROW : ROW + PX, :]
        if l < DEPTH - 1:
            x = activate(conv, stats[l])
    u_copy.wait()
    upstream = u_buf[...]
    for l in reversed(range(DEPTH)):
        upstream = backward_layer(upstream, xs_ref[l], conv_ref[l], l, flip_ref, stats[l], pad_ref)
    dx_ref[...] = upstream


def last_kernel(cot_any, recv_ref, xs_ref, conv_ref, flip_ref, a_ref, send_ref, u_buf, pad_ref, u_sem):
    half, z, _ = place()
    u_copy = pltpu.make_async_copy(cot_any.at[z], u_buf, u_sem)
    u_copy.start()
    clear_pads(pad_ref)
    u_copy.wait()
    upstream = jnp.where(half == 1, u_buf[...], recv_ref[...])
    for l in reversed(range(DEPTH)):
        stat = read_stats(a_ref, l)
        upstream = backward_layer(upstream, xs_ref[l], conv_ref[l], l, flip_ref, stat, pad_ref, send_ref)


MAP = jax.ShapeDtypeStruct((PX, C), BF)
KERNELS = jax.ShapeDtypeStruct((DEPTH, ROWS, C), BF)
SENT = jax.ShapeDtypeStruct((DEPTH, PX + STAT, C), BF)


def first(images, a, b):
    return pl.pallas_call(
        first_kernel,
        out_shape=MAP,
        in_specs=[any_spec(), vmem_spec(), vmem_spec()],
        out_specs=vmem_spec(),
        scratch_shapes=[
            pltpu.VMEM((PX, C), BF),
            pltpu.VMEM((3, PAD, C), BF),
            pltpu.SemaphoreType.DMA,
        ],
        compiler_params=params(),
        name="first",
    )(images, a, b)


def flip(a, b):
    return pl.pallas_call(
        flip_kernel,
        out_shape=KERNELS,
        in_specs=[vmem_spec()] * 2,
        out_specs=vmem_spec(),
        compiler_params=params(),
        name="flip",
    )(a, b)


def middle(images, cot, recv, a, b, flipped):
    return pl.pallas_call(
        middle_kernel,
        out_shape=(
            MAP,
            jax.ShapeDtypeStruct((DEPTH, PX, C), BF),
            jax.ShapeDtypeStruct((DEPTH, PX, C), F32),
            jax.ShapeDtypeStruct((DEPTH, PX, C), BF),
        ),
        in_specs=[any_spec(), any_spec()] + [vmem_spec()] * 4,
        out_specs=(vmem_spec(),) * 4,
        scratch_shapes=[
            pltpu.VMEM((PX, C), BF),
            pltpu.VMEM((PX, C), BF),
            pltpu.VMEM((3, PAD, C), BF),
            pltpu.SemaphoreType.DMA((2,)),
        ],
        compiler_params=params(),
        name="middle",
    )(images, cot, recv, a, b, flipped)


def last(cot, recv, xs, conv, flipped, a):
    return pl.pallas_call(
        last_kernel,
        out_shape=SENT,
        in_specs=[any_spec()] + [vmem_spec()] * 5,
        out_specs=vmem_spec(),
        scratch_shapes=[
            pltpu.VMEM((PX, C), BF),
            pltpu.VMEM((3, PAD, C), BF),
            pltpu.SemaphoreType.DMA,
        ],
        compiler_params=params(),
        name="last",
    )(cot, recv, xs, conv, flipped, a)


def half_gradient(flip_ref, pad_ref, w_ref, grad_energy_ref, half, out_ref):
    first_row = pl.multiple_of(half * BLOCK, BLOCK)
    lhs = flip_ref[pl.ds(first_row, BLOCK), :]
    grad_energy = grad_energy_ref[pl.ds(first_row, BLOCK), :]
    for ky in range(3):
        for kx in range(3):
            tap = ky * 3 + kx
            rhs = jnp.concatenate(
                [pad_ref[n, 2 - kx, (2 - ky) * ROW : (2 - ky) * ROW + PX, :] for n in range(DEPTH)], axis=0
            )
            part = jnp.dot(lhs, rhs, preferred_element_type=F32)
            w = w_ref[pl.ds(pl.multiple_of(tap * C + half * BLOCK, BLOCK), BLOCK), :].astype(F32)
            out_ref[tap * BLOCK : (tap + 1) * BLOCK, :] = (part + w * grad_energy).astype(BF)


def turn_kernel(s0_ref, s1_ref, s2_ref, s3_ref, flip_ref):
    for k, ref in enumerate((s0_ref, s1_ref, s2_ref, s3_ref)):
        flip_ref[:, k * PX : (k + 1) * PX] = ref[...].T


def turn(*maps):
    return pl.pallas_call(
        turn_kernel,
        out_shape=jax.ShapeDtypeStruct((C, DEPTH * PX), BF),
        in_specs=[vmem_spec()] * DEPTH,
        out_specs=vmem_spec(),
        compiler_params=params(),
        name="turn",
    )(*maps)


def give_kernel(
    r_ref, flip_ref, w_ref, styles_ref, demod_ref, energy_ref, affine_ref, latent_ref,
    give_ref, extra_ref, grad_latent_ref, pad_ref, grad_energy_ref, rows_ref,
):
    _, z, core = place()
    parts = [unpack_rows(r_ref[n, PX : PX + STAT, :]) for n in range(DEPTH)]
    styles = styles_ref[...]
    demod = demod_ref[...]
    grad_sum = stack_rows([p[1] for p in parts]) * (-0.5) * demod * demod * demod
    squares = styles * styles
    grad_squares = lax.dot_general(
        grad_sum, energy_ref[...], (((1,), (1,)), ((), ())), precision=HI, preferred_element_type=F32
    )
    grad_styles = stack_rows([p[0] for p in parts]) + 2.0 * styles * grad_squares
    grad_bias = parts[0][2] + parts[1][2] + parts[2][2] + parts[3][2]
    rows_ref[...] = jnp.zeros_like(rows_ref)
    rows_ref[0:DEPTH, :] = grad_styles[0:DEPTH]
    rows_ref[DEPTH : DEPTH + 1, :] = grad_bias
    rows_ref[8 : 8 + DEPTH, :] = latent_ref[:, 0:C]
    rows_ref[8 + DEPTH : 8 + 2 * DEPTH, :] = latent_ref[:, C : 2 * C]
    extra = rows_ref[...].astype(BF)
    extra_ref[...] = extra
    give_ref[HALF : HALF + STAT, :] = extra
    grad_latent = lax.dot_general(
        grad_styles, affine_ref[...], (((1,), (1,)), ((), ())), precision=HI, preferred_element_type=F32
    )
    grad_latent_ref[...] = grad_latent[0:DEPTH]
    grad_energy_ref[...] = 2.0 * lax.dot_general(
        squares, grad_sum, (((0,), (0,)), ((), ())), precision=HI, preferred_element_type=F32
    )
    for k in range(DEPTH):
        clear_pads(pad_ref.at[k])
        spread(pad_ref.at[k], r_ref[lax.rem(z - k + DEPTH, DEPTH), 0:PX, :].astype(F32))
    half_gradient(flip_ref, pad_ref, w_ref, grad_energy_ref, 1 - core, give_ref)


def give_half(r, turned, w, styles, demod, energy, affine, latent):
    return pl.pallas_call(
        give_kernel,
        out_shape=(
            jax.ShapeDtypeStruct((HALF + STAT, C), BF),
            jax.ShapeDtypeStruct((STAT, C), BF),
            jax.ShapeDtypeStruct((DEPTH, affine.shape[0]), F32),
            jax.ShapeDtypeStruct((DEPTH, 3, PAD, C), BF),
            jax.ShapeDtypeStruct((C, C), F32),
        ),
        in_specs=[vmem_spec()] * 8,
        out_specs=(vmem_spec(),) * 5,
        scratch_shapes=[pltpu.VMEM((STAT, C), F32)],
        compiler_params=params(),
        name="give",
    )(r, turned, w, styles, demod, energy, affine, latent)


def keep_kernel(flip_ref, pad_ref, w_ref, grad_energy_ref, keep_ref):
    _, _, core = place()
    half_gradient(flip_ref, pad_ref, w_ref, grad_energy_ref, core, keep_ref)


def keep_half(flipped, padded, w, grad_energy):
    return pl.pallas_call(
        keep_kernel,
        out_shape=jax.ShapeDtypeStruct((HALF, C), BF),
        in_specs=[vmem_spec()] * 4,
        out_specs=vmem_spec(),
        compiler_params=params(),
        name="keep",
    )(flipped, padded, w, grad_energy)


def pair_kernel(keep_ref, extra_ref, got_ref, out_ref):
    for k in range(PEERS):
        at = slice(k * SHARE, (k + 1) * SHARE)
        out_ref[k, 0:SHARE, :] = (keep_ref[at, :].astype(F32) + got_ref[at, :].astype(F32)).astype(BF)
        out_ref[k, SHARE : SHARE + STAT, :] = extra_ref[...]
        out_ref[k, SHARE + STAT : SHARE + 2 * STAT, :] = got_ref[HALF : HALF + STAT, :]


def pair(keep, extra, got):
    return pl.pallas_call(
        pair_kernel,
        out_shape=jax.ShapeDtypeStruct((PEERS, SHARE + 2 * STAT, C), BF),
        in_specs=[vmem_spec()] * 3,
        out_specs=vmem_spec(),
        compiler_params=params(),
        name="pair",
    )(keep, extra, got)


def share_kernel(shares_ref, out_ref):
    total = shares_ref[0, 0:SHARE, :].astype(F32)
    for k in range(1, PEERS):
        total += shares_ref[k, 0:SHARE, :].astype(F32)
    total = total.astype(BF)
    for k in range(PEERS):
        out_ref[k] = total


def share(shares):
    return pl.pallas_call(
        share_kernel,
        out_shape=jax.ShapeDtypeStruct((PEERS, SHARE, C), BF),
        in_specs=[vmem_spec()],
        out_specs=vmem_spec(),
        compiler_params=params(),
        name="share",
    )(shares)


def affine_kernel(shares_ref, affine_ref, bias_ref, grads_ref, low_ref, high_ref):
    row = lax.broadcasted_iota(jnp.int32, (STAT, C), 0)
    bias = jnp.zeros((1, C), F32)
    for k in range(2 * PEERS):
        start = SHARE + (k % 2) * STAT
        tile = shares_ref[k // 2, start : start + STAT, :].astype(F32)
        bias += tile[DEPTH : DEPTH + 1]
        at = slice(k * STAT, (k + 1) * STAT)
        grads_ref[at, :] = jnp.where(row < DEPTH, tile, 0.0).astype(BF)
        low_ref[at, :] = pltpu.roll(tile, 8, 0).astype(BF)
        high_ref[at, :] = pltpu.roll(tile, 4, 0).astype(BF)
    bias_ref[...] = bias
    for k, ref in enumerate((low_ref, high_ref)):
        affine_ref[k * C : (k + 1) * C, :] = lax.dot_general(
            ref[...], grads_ref[...], (((0,), (0,)), ((), ())), preferred_element_type=F32
        )


def affine_gradient(shares, width):
    return pl.pallas_call(
        affine_kernel,
        out_shape=(jax.ShapeDtypeStruct((width, C), F32), jax.ShapeDtypeStruct((1, C), F32)),
        in_specs=[vmem_spec()],
        out_specs=(vmem_spec(), vmem_spec()),
        scratch_shapes=[pltpu.VMEM((2 * PEERS * STAT, C), BF)] * 3,
        compiler_params=params(),
        name="affine",
    )(shares)


def widen_half(half, value_ref, out_any, wide_ref, sem):
    value = value_ref[...].reshape(TAPS, BLOCK, C)
    rows = pl.ds(pl.multiple_of(half * BLOCK, BLOCK), BLOCK)
    copies = []
    for k in range(3):
        taps = slice(3 * k, 3 * k + 3)
        wide_ref[taps] = value[taps].astype(F32)
        copies.append(pltpu.make_async_copy(wide_ref.at[taps], out_any.at[taps, rows], sem.at[k]))
        copies[k].start()
    for copy in copies:
        copy.wait()


def own_kernel(value_ref, out_any, wide_ref, sem):
    _, _, core = place()
    widen_half(core, value_ref, out_any, wide_ref, sem)


def rest_kernel(value_ref, target_any, part_ref, moved_ref, out_any, sum_ref, wide_ref, sem):
    _, _, core = place()
    sum_ref[...] = part_ref[...] + moved_ref[...]
    widen_half(1 - core, value_ref, out_any, wide_ref, sem)


WIDE = jax.ShapeDtypeStruct((TAPS, C, C), F32)


def wide_scratch():
    return [pltpu.VMEM((TAPS, BLOCK, C), F32), pltpu.SemaphoreType.DMA((3,))]


def own_half(value):
    return pl.pallas_call(
        own_kernel,
        out_shape=WIDE,
        in_specs=[vmem_spec()],
        out_specs=pl.BlockSpec(memory_space=pltpu.HBM),
        scratch_shapes=wide_scratch(),
        compiler_params=params(),
        name="own",
    )(value)


def rest_half(value, target, part, moved):
    return pl.pallas_call(
        rest_kernel,
        out_shape=(WIDE, jax.ShapeDtypeStruct(part.shape, F32)),
        in_specs=[vmem_spec(), pl.BlockSpec(memory_space=pltpu.HBM), vmem_spec(), vmem_spec()],
        out_specs=(pl.BlockSpec(memory_space=pltpu.HBM), vmem_spec()),
        input_output_aliases={1: 0},
        scratch_shapes=wide_scratch(),
        compiler_params=params(),
        name="rest",
    )(value, target, part, moved)


def body(images, latent, weight, affine, biases, cotangent):
    width = latent.shape[1]
    replicas = lax.axis_size("dp")
    segments = lax.axis_size("segment")
    planes = [list(range(k, k + DEPTH)) for k in range(0, segments, DEPTH)]
    across = [(i, (i + DEPTH) % segments) for i in range(segments)]
    sibling = [(i, i ^ 1) for i in range(replicas)]
    cores = [list(range(k, replicas, 2)) for k in range(2)]

    w = weight.reshape(ROWS, C)
    images = images.reshape(DEPTH, PX, C)
    cotangent = cotangent.reshape(DEPTH, PX, C)

    send, styles, demod, energy = prepare(latent, affine[0], w, biases)
    a = lax.all_to_all(send, "segment", 0, 0, axis_index_groups=planes)
    b = near(lax.ppermute(a, "dp", sibling))
    a = near(a)

    act = first(images, a, b)
    flipped = flip(a, b)
    arrived = near(lax.ppermute(act, "segment", across))
    dx, xs, conv, scaled = middle(images, cotangent, arrived, a, b, flipped)
    returned = near(lax.ppermute(dx, "segment", across))
    maps = [scaled[0]] + [
        near(
            lax.ppermute(
                scaled[k], "segment", [(i, i - i % DEPTH + (i + k) % DEPTH) for i in range(segments)]
            )
        )
        for k in range(1, DEPTH)
    ]
    turned = turn(*maps)
    sent, turned = lax.optimization_barrier((last(cotangent, returned, xs, conv, flipped, a), turned))

    r = near(lax.all_to_all(sent, "segment", 0, 0, axis_index_groups=planes))
    give, extra, part, padded, grad_energy = give_half(
        r, turned, w, styles, demod, energy, affine[0], latent
    )
    got = near(lax.ppermute(give, "dp", sibling))
    keep = keep_half(turned, padded, w, grad_energy)
    shared, part = lax.optimization_barrier((pair(keep, extra, got), part))
    shares = near(lax.all_to_all(near(shared), "dp", 0, 0, axis_index_groups=cores))
    part = part + lax.ppermute(part, "segment", [(i, i ^ 1) for i in range(segments)])
    part = part + lax.ppermute(part, "segment", [(i, i ^ 2) for i in range(segments)])
    spread_share, part = lax.optimization_barrier((share(shares), part))
    mine = lax.all_to_all(near(spread_share), "dp", 0, 0, axis_index_groups=cores)
    other = near(lax.ppermute(mine, "dp", sibling))
    mine, shares, part = lax.optimization_barrier((mine, shares, part))
    moved = lax.ppermute(part, "segment", across)
    grad_affine, grad_bias = affine_gradient(shares, width)
    grad_weight, grad_latent = rest_half(other, own_half(near(mine)), part, moved)
    grad_weight = grad_weight.reshape(weight.shape)
    return (grad_weight, grad_affine[None], grad_bias, grad_latent)


def solution(mesh):
    placed = (
        P("dp", None, None, None),
        P("dp", None),
        P("segment", None, None, None, None),
        P("segment", None, None),
        P("segment", None),
        P("dp", None, None, None),
    )
    return jax.shard_map(
        body,
        mesh=mesh,
        in_specs=placed,
        out_specs=(
            P("segment", None, None, None, None),
            P("segment", None, None),
            P("segment", None),
            P("dp", None),
        ),
        check_vma=False,
    )
```

```python
import math

import jax
import jax.numpy as jnp
from jax import lax
from jax.experimental import pallas as pl
from jax.experimental.pallas import tpu as pltpu
from jax.sharding import PartitionSpec as P

GAIN = math.sqrt(2.0)
EPS = 1e-08
BF = jnp.bfloat16
F32 = jnp.float32
C = 256
PX = 256
TAPS = 9
ROWS = TAPS * C
HALF = ROWS // 2
STAT = 16
DEPTH = 4
PEERS = 8
SHARE = HALF // PEERS
PART = HALF // 2
ROW = 16
BLOCK = 128
PAD = PX + 2 * ROW
HI = lax.Precision.HIGHEST


def any_spec():
    return pl.BlockSpec(memory_space=pl.ANY)


def vmem_spec():
    return pl.BlockSpec(memory_space=pltpu.VMEM)


def params():
    return pltpu.CompilerParams(vmem_limit_bytes=28 << 20)


def near(value):
    return pltpu.with_memory_space_constraint(value, pltpu.VMEM)


def place():
    seg = lax.axis_index("segment")
    return seg // DEPTH, seg % DEPTH, lax.axis_index("dp") % 2


def part_start(core, side):
    return pl.multiple_of(core * HALF + side * PART, PART)


def split3(value):
    hi = value.astype(BF).astype(F32)
    rest = value - hi
    mid = rest.astype(BF).astype(F32)
    return hi, mid, rest - mid


def pack_rows(values):
    row = lax.broadcasted_iota(jnp.int32, (STAT, C), 0)
    out = jnp.zeros((STAT, C), F32)
    k = 0
    for value in values:
        for part in split3(value):
            out = jnp.where(row == k, jnp.broadcast_to(part, (STAT, C)), out)
            k += 1
    return out.astype(BF)


def unpack_rows(tile):
    t = tile.astype(F32)
    return [t[3 * k : 3 * k + 1] + t[3 * k + 1 : 3 * k + 2] + t[3 * k + 2 : 3 * k + 3] for k in range(3)]


def stack_rows(rows):
    index = lax.broadcasted_iota(jnp.int32, (8, C), 0)
    out = jnp.zeros((8, C), F32)
    for k, row in enumerate(rows):
        out = jnp.where(index == k, jnp.broadcast_to(row, (8, C)), out)
    return out


def prepare_kernel(
    latent_hbm, affine_hbm, w_hbm, bias_hbm, down_ref, up_ref, far_ref, tile_ref, styles_ref, demod_ref, energy_ref,
    rows_ref, affine_ref, w_ref, bias_ref, tiles_ref, sem,
):
    _, z, core = place()
    side = (lax.axis_index("dp") // 2) % 2
    mine = pl.ds(pl.multiple_of(core * HALF, HALF), HALF)
    rows_ref[...] = jnp.zeros_like(rows_ref)
    third = ROWS // 3
    loads = [
        pltpu.make_async_copy(affine_hbm, affine_ref, sem.at[0]),
        pltpu.make_async_copy(latent_hbm, rows_ref.at[pl.ds(0, DEPTH)], sem.at[1]),
        pltpu.make_async_copy(bias_hbm, bias_ref, sem.at[2]),
    ] + [
        pltpu.make_async_copy(w_hbm.at[pl.ds(k * third, third)], w_ref.at[pl.ds(k * third, third)], sem.at[3 + k])
        for k in range(3)
    ]
    sends = [
        pltpu.make_async_copy(w_hbm.at[pl.ds(part_start(core, side), PART)], far_ref.at[pl.ds(0, PART)], sem.at[6]),
        pltpu.make_async_copy(w_hbm.at[mine], down_ref.at[pl.ds(0, HALF)], sem.at[7]),
        pltpu.make_async_copy(w_hbm.at[mine], up_ref.at[pl.ds(0, HALF)], sem.at[8]),
    ]
    for copy in loads + sends:
        copy.start()
    for copy in loads[:3]:
        copy.wait()
    styles = jnp.dot(rows_ref[...], affine_ref[...], precision=HI, preferred_element_type=F32) + 1.0
    energy = jnp.zeros((C, C), F32)
    for tap in range(TAPS):
        if tap % 3 == 0:
            loads[3 + tap // 3].wait()
        part = w_ref[tap * C : (tap + 1) * C, :].astype(F32)
        energy += part * part
    energy_ref[...] = energy
    demod = lax.rsqrt(jnp.dot(styles * styles, energy, precision=HI, preferred_element_type=F32) + EPS)
    styles_ref[...] = styles
    demod_ref[...] = demod
    for k in range(DEPTH):
        tiles_ref[k] = pack_rows([styles[k : k + 1], demod[k : k + 1], bias_ref[...]])
    tile_ref[...] = tiles_ref[z]
    down_ref[HALF : HALF + STAT, :] = tiles_ref[lax.rem(z + DEPTH - 1, DEPTH)]
    up_ref[HALF : HALF + STAT, :] = tiles_ref[lax.rem(z + 1, DEPTH)]
    far_ref[PART : PART + STAT, :] = tiles_ref[lax.rem(z + 2, DEPTH)]
    for copy in sends:
        copy.wait()


def prepare(latent, affine, w, bias):
    far = [pltpu.with_memory_space_constraint(value, pltpu.HBM) for value in (latent, affine, w, bias)]
    return pl.pallas_call(
        prepare_kernel,
        out_shape=(
            jax.ShapeDtypeStruct((HALF + STAT, C), BF),
            jax.ShapeDtypeStruct((HALF + STAT, C), BF),
            jax.ShapeDtypeStruct((PART + STAT, C), BF),
            jax.ShapeDtypeStruct((STAT, C), BF),
            jax.ShapeDtypeStruct((8, C), F32),
            jax.ShapeDtypeStruct((8, C), F32),
            jax.ShapeDtypeStruct((C, C), F32),
        ),
        in_specs=[pl.BlockSpec(memory_space=pltpu.HBM)] * 4,
        out_specs=(vmem_spec(),) * 7,
        scratch_shapes=[
            pltpu.VMEM((8, latent.shape[1]), F32),
            pltpu.VMEM(affine.shape, F32),
            pltpu.VMEM((ROWS, C), BF),
            pltpu.VMEM((1, C), F32),
            pltpu.VMEM((DEPTH, STAT, C), BF),
            pltpu.SemaphoreType.DMA((9,)),
        ],
        compiler_params=params(),
        name="prepare",
    )(*far)


def clear_pads(pad_ref):
    for k in range(3):
        pad_ref[k, 0:ROW, :] = jnp.zeros((ROW, C), BF)
        pad_ref[k, ROW + PX : PAD, :] = jnp.zeros((ROW, C), BF)


def spread(pad_ref, value):
    column = lax.broadcasted_iota(jnp.int32, (PX, C), 0) % ROW
    pad_ref[1, ROW : ROW + PX, :] = value.astype(BF)
    pad_ref[0, ROW : ROW + PX, :] = jnp.where(column == 0, 0.0, pltpu.roll(value, 1, 0)).astype(BF)
    pad_ref[2, ROW : ROW + PX, :] = jnp.where(column == ROW - 1, 0.0, pltpu.roll(value, PX - 1, 0)).astype(BF)


def taps_matmul(pad_ref, w, mirrored):
    out = []
    for start in range(0, PX, BLOCK):
        pieces = []
        for ky in range(3):
            for kx in range(3):
                plane, shift = (2 - kx, 2 - ky) if mirrored else (kx, ky)
                first_row = start + shift * ROW
                pieces.append(pad_ref[plane, first_row : first_row + BLOCK, :])
        out.append(jnp.dot(jnp.concatenate(pieces, axis=1), w, preferred_element_type=F32))
    return jnp.concatenate(out, axis=0)


def forward_layer(x, l, w_ref, stat, pad_ref):
    styles, demod, bias = stat
    spread(pad_ref, (x.astype(F32) * styles).astype(BF).astype(F32))
    return taps_matmul(pad_ref, w_ref[l], False)


def activate(conv, stat):
    _, demod, bias = stat
    hidden = conv * demod + bias
    return (GAIN * hidden * (0.6 + 0.4 * jnp.tanh(hidden))).astype(BF)


def backward_layer(upstream, x, conv, l, flip_ref, stat, pad_ref, send_ref=None):
    styles, demod, bias = stat
    hidden = conv * demod + bias
    t = jnp.tanh(hidden)
    dh = upstream.astype(F32) * (GAIN * (0.6 + 0.4 * t + 0.4 * hidden * (1.0 - t * t)))
    spread(pad_ref, (dh * demod).astype(BF).astype(F32))
    grad_scaled = taps_matmul(pad_ref, flip_ref[l], True).astype(BF).astype(F32)
    if send_ref is not None:
        grad_bias = jnp.sum(dh, axis=0, keepdims=True)
        grad_demod = jnp.sum(dh * conv, axis=0, keepdims=True)
        grad_styles = jnp.sum(grad_scaled * x.astype(F32), axis=0, keepdims=True)
        send_ref[l, 0:PX, :] = pad_ref[1, ROW : ROW + PX, :]
        send_ref[l, PX : PX + STAT, :] = pack_rows([grad_styles, grad_demod, grad_bias])
    return (grad_scaled * styles).astype(BF)


def layer_copies(tile_ref, w_any, near_refs, far_refs, w_ref, stat_ref, sem):
    _, z, core = place()
    side = (lax.axis_index("dp") // 2) % 2
    layer = [lax.rem(z + k, DEPTH) for k in range(DEPTH)]
    copies = [
        pltpu.make_async_copy(w_any, w_ref.at[layer[0]], sem.at[0]),
        pltpu.make_async_copy(tile_ref, stat_ref.at[layer[0]], sem.at[1]),
    ]

    def add(source, target):
        copies.append(pltpu.make_async_copy(source, target, sem.at[len(copies)]))

    for k, (a_ref, b_ref) in near_refs:
        for ref, half in ((a_ref, core), (b_ref, 1 - core)):
            add(ref.at[pl.ds(0, HALF)], w_ref.at[layer[k], pl.ds(pl.multiple_of(half * HALF, HALF), HALF)])
        add(a_ref.at[pl.ds(HALF, STAT)], stat_ref.at[layer[k]])
    for index, ref in enumerate(far_refs):
        half = core if index < 2 else 1 - core
        which = side if index % 2 == 0 else 1 - side
        add(ref.at[pl.ds(0, PART)], w_ref.at[layer[2], pl.ds(part_start(half, which), PART)])
    add(far_refs[0].at[pl.ds(PART, STAT)], stat_ref.at[layer[2]])
    return copies


def first_kernel(
    images_any, w_any, tile_ref, a1_ref, b1_ref, a3_ref, b3_ref, f0_ref, f1_ref, f2_ref, f3_ref,
    out_ref, w_ref, stat_ref, x_buf, pad_ref, sem, x_sem,
):
    _, z, _ = place()
    copies = layer_copies(
        tile_ref, w_any, ((1, (a1_ref, b1_ref)), (3, (a3_ref, b3_ref))), (f0_ref, f1_ref, f2_ref, f3_ref),
        w_ref, stat_ref, sem,
    )
    x_copy = pltpu.make_async_copy(images_any.at[z], x_buf, x_sem)
    x_copy.start()
    for copy in copies:
        copy.start()
    clear_pads(pad_ref)
    x_copy.wait()
    x = x_buf[...]
    for copy in copies:
        copy.wait()
    for l in range(DEPTH):
        stat = unpack_rows(stat_ref[l])
        x = activate(forward_layer(x, l, w_ref, stat, pad_ref), stat)
    out_ref[...] = x


def flip_kernel(w_ref, flip_ref):
    for l in range(DEPTH):
        for tap in range(TAPS):
            at = slice(tap * C, (tap + 1) * C)
            flip_ref[l, at, :] = w_ref[l, at, :].T


def middle_kernel(
    images_any, cot_any, recv_ref, w_ref, flip_ref, stat_ref, dx_ref, xs_ref, conv_ref, scaled_ref,
    x_buf, u_buf, pad_ref, x_sem,
):
    half, z, _ = place()
    x_copy = pltpu.make_async_copy(images_any.at[z], x_buf, x_sem.at[0])
    u_copy = pltpu.make_async_copy(cot_any.at[z], u_buf, x_sem.at[1])
    x_copy.start()
    u_copy.start()
    clear_pads(pad_ref)
    x_copy.wait()
    x = jnp.where(half == 1, recv_ref[...], x_buf[...])
    stats = []
    for l in range(DEPTH):
        stats.append(unpack_rows(stat_ref[l]))
        xs_ref[l] = x
        conv = forward_layer(x, l, w_ref, stats[l], pad_ref)
        conv_ref[l] = conv
        scaled_ref[lax.rem(l - z + DEPTH, DEPTH)] = pad_ref[1, ROW : ROW + PX, :]
        if l < DEPTH - 1:
            x = activate(conv, stats[l])
    u_copy.wait()
    upstream = u_buf[...]
    for l in reversed(range(DEPTH)):
        upstream = backward_layer(upstream, xs_ref[l], conv_ref[l], l, flip_ref, stats[l], pad_ref)
    dx_ref[...] = upstream


def last_kernel(cot_any, recv_ref, xs_ref, conv_ref, flip_ref, stat_ref, send_ref, u_buf, pad_ref, u_sem):
    half, z, _ = place()
    u_copy = pltpu.make_async_copy(cot_any.at[z], u_buf, u_sem)
    u_copy.start()
    clear_pads(pad_ref)
    u_copy.wait()
    upstream = jnp.where(half == 1, u_buf[...], recv_ref[...])
    for l in reversed(range(DEPTH)):
        stat = unpack_rows(stat_ref[l])
        upstream = backward_layer(upstream, xs_ref[l], conv_ref[l], l, flip_ref, stat, pad_ref, send_ref)


MAP = jax.ShapeDtypeStruct((PX, C), BF)
KERNELS = jax.ShapeDtypeStruct((DEPTH, ROWS, C), BF)
SENT = jax.ShapeDtypeStruct((DEPTH, PX + STAT, C), BF)


def first(images, w, tile, *parts):
    return pl.pallas_call(
        first_kernel,
        out_shape=(MAP, KERNELS, jax.ShapeDtypeStruct((DEPTH, STAT, C), BF)),
        in_specs=[pl.BlockSpec(memory_space=pltpu.HBM), any_spec()] + [vmem_spec()] * 9,
        out_specs=(vmem_spec(),) * 3,
        scratch_shapes=[
            pltpu.VMEM((PX, C), BF),
            pltpu.VMEM((3, PAD, C), BF),
            pltpu.SemaphoreType.DMA((13,)),
            pltpu.SemaphoreType.DMA,
        ],
        compiler_params=params(),
        name="first",
    )(pltpu.with_memory_space_constraint(images, pltpu.HBM), w, tile, *parts)


def flip(w):
    return pl.pallas_call(
        flip_kernel,
        out_shape=KERNELS,
        in_specs=[vmem_spec()],
        out_specs=vmem_spec(),
        compiler_params=params(),
        name="flip",
    )(w)


def middle(images, cot, recv, w, flipped, stat):
    return pl.pallas_call(
        middle_kernel,
        out_shape=(
            MAP,
            jax.ShapeDtypeStruct((DEPTH, PX, C), BF),
            jax.ShapeDtypeStruct((DEPTH, PX, C), F32),
            jax.ShapeDtypeStruct((DEPTH, PX, C), BF),
        ),
        in_specs=[any_spec(), any_spec()] + [vmem_spec()] * 4,
        out_specs=(vmem_spec(),) * 4,
        scratch_shapes=[
            pltpu.VMEM((PX, C), BF),
            pltpu.VMEM((PX, C), BF),
            pltpu.VMEM((3, PAD, C), BF),
            pltpu.SemaphoreType.DMA((2,)),
        ],
        compiler_params=params(),
        name="middle",
    )(images, cot, recv, w, flipped, stat)


def last(cot, recv, xs, conv, flipped, stat):
    return pl.pallas_call(
        last_kernel,
        out_shape=SENT,
        in_specs=[any_spec()] + [vmem_spec()] * 5,
        out_specs=vmem_spec(),
        scratch_shapes=[
            pltpu.VMEM((PX, C), BF),
            pltpu.VMEM((3, PAD, C), BF),
            pltpu.SemaphoreType.DMA,
        ],
        compiler_params=params(),
        name="last",
    )(cot, recv, xs, conv, flipped, stat)


def half_gradient(flip_ref, pad_ref, w_ref, grad_energy_ref, half, out_ref):
    first_row = pl.multiple_of(half * BLOCK, BLOCK)
    lhs = flip_ref[pl.ds(first_row, BLOCK), :]
    grad_energy = grad_energy_ref[pl.ds(first_row, BLOCK), :]
    for ky in range(3):
        for kx in range(3):
            tap = ky * 3 + kx
            rhs = jnp.concatenate(
                [pad_ref[n, 2 - kx, (2 - ky) * ROW : (2 - ky) * ROW + PX, :] for n in range(DEPTH)], axis=0
            )
            part = jnp.dot(lhs, rhs, preferred_element_type=F32)
            w = w_ref[pl.ds(pl.multiple_of(tap * C + half * BLOCK, BLOCK), BLOCK), :].astype(F32)
            out_ref[tap * BLOCK : (tap + 1) * BLOCK, :] = (part + w * grad_energy).astype(BF)


def turn_kernel(s0_ref, s1_ref, s2_ref, s3_ref, flip_ref):
    for k, ref in enumerate((s0_ref, s1_ref, s2_ref, s3_ref)):
        flip_ref[:, k * PX : (k + 1) * PX] = ref[...].T


def turn(*maps):
    return pl.pallas_call(
        turn_kernel,
        out_shape=jax.ShapeDtypeStruct((C, DEPTH * PX), BF),
        in_specs=[vmem_spec()] * DEPTH,
        out_specs=vmem_spec(),
        compiler_params=params(),
        name="turn",
    )(*maps)


def give_kernel(
    r_ref, flip_ref, w_ref, styles_ref, demod_ref, energy_ref, affine_ref, latent_ref,
    give_ref, extra_ref, grad_latent_ref, pad_ref, grad_energy_ref, rows_ref,
):
    _, z, core = place()
    parts = [unpack_rows(r_ref[n, PX : PX + STAT, :]) for n in range(DEPTH)]
    styles = styles_ref[...]
    demod = demod_ref[...]
    grad_sum = stack_rows([p[1] for p in parts]) * (-0.5) * demod * demod * demod
    squares = styles * styles
    grad_squares = lax.dot_general(
        grad_sum, energy_ref[...], (((1,), (1,)), ((), ())), precision=HI, preferred_element_type=F32
    )
    grad_styles = stack_rows([p[0] for p in parts]) + 2.0 * styles * grad_squares
    grad_bias = parts[0][2] + parts[1][2] + parts[2][2] + parts[3][2]
    rows_ref[...] = jnp.zeros_like(rows_ref)
    rows_ref[0:DEPTH, :] = grad_styles[0:DEPTH]
    rows_ref[DEPTH : DEPTH + 1, :] = grad_bias
    rows_ref[8 : 8 + DEPTH, :] = latent_ref[:, 0:C]
    rows_ref[8 + DEPTH : 8 + 2 * DEPTH, :] = latent_ref[:, C : 2 * C]
    extra = rows_ref[...].astype(BF)
    extra_ref[...] = extra
    give_ref[HALF : HALF + STAT, :] = extra
    grad_latent = lax.dot_general(
        grad_styles, affine_ref[...], (((1,), (1,)), ((), ())), precision=HI, preferred_element_type=F32
    )
    grad_latent_ref[...] = grad_latent[0:DEPTH]
    grad_energy_ref[...] = 2.0 * lax.dot_general(
        squares, grad_sum, (((0,), (0,)), ((), ())), precision=HI, preferred_element_type=F32
    )
    for k in range(DEPTH):
        clear_pads(pad_ref.at[k])
        spread(pad_ref.at[k], r_ref[lax.rem(z - k + DEPTH, DEPTH), 0:PX, :].astype(F32))
    half_gradient(flip_ref, pad_ref, w_ref, grad_energy_ref, 1 - core, give_ref)


def give_half(r, turned, w, styles, demod, energy, affine, latent):
    return pl.pallas_call(
        give_kernel,
        out_shape=(
            jax.ShapeDtypeStruct((HALF + STAT, C), BF),
            jax.ShapeDtypeStruct((STAT, C), BF),
            jax.ShapeDtypeStruct((DEPTH, affine.shape[0]), F32),
            jax.ShapeDtypeStruct((DEPTH, 3, PAD, C), BF),
            jax.ShapeDtypeStruct((C, C), F32),
        ),
        in_specs=[vmem_spec()] * 8,
        out_specs=(vmem_spec(),) * 5,
        scratch_shapes=[pltpu.VMEM((STAT, C), F32)],
        compiler_params=params(),
        name="give",
    )(r, turned, w, styles, demod, energy, affine, latent)


def keep_kernel(flip_ref, pad_ref, w_ref, grad_energy_ref, keep_ref):
    _, _, core = place()
    half_gradient(flip_ref, pad_ref, w_ref, grad_energy_ref, core, keep_ref)


def keep_half(flipped, padded, w, grad_energy):
    return pl.pallas_call(
        keep_kernel,
        out_shape=jax.ShapeDtypeStruct((HALF, C), BF),
        in_specs=[vmem_spec()] * 4,
        out_specs=vmem_spec(),
        compiler_params=params(),
        name="keep",
    )(flipped, padded, w, grad_energy)


def pair_kernel(keep_ref, extra_ref, got_ref, out_ref):
    for k in range(PEERS):
        at = slice(k * SHARE, (k + 1) * SHARE)
        out_ref[k, 0:SHARE, :] = (keep_ref[at, :].astype(F32) + got_ref[at, :].astype(F32)).astype(BF)
        out_ref[k, SHARE : SHARE + STAT, :] = extra_ref[...]
        out_ref[k, SHARE + STAT : SHARE + 2 * STAT, :] = got_ref[HALF : HALF + STAT, :]


def pair(keep, extra, got):
    return pl.pallas_call(
        pair_kernel,
        out_shape=jax.ShapeDtypeStruct((PEERS, SHARE + 2 * STAT, C), BF),
        in_specs=[vmem_spec()] * 3,
        out_specs=vmem_spec(),
        compiler_params=params(),
        name="pair",
    )(keep, extra, got)


def share_kernel(shares_ref, out_ref):
    total = shares_ref[0, 0:SHARE, :].astype(F32)
    for k in range(1, PEERS):
        total += shares_ref[k, 0:SHARE, :].astype(F32)
    total = total.astype(BF)
    for k in range(PEERS):
        out_ref[k] = total


def share(shares):
    return pl.pallas_call(
        share_kernel,
        out_shape=jax.ShapeDtypeStruct((PEERS, SHARE, C), BF),
        in_specs=[vmem_spec()],
        out_specs=vmem_spec(),
        compiler_params=params(),
        name="share",
    )(shares)


def affine_kernel(shares_ref, affine_ref, bias_ref, grads_ref, low_ref, high_ref):
    row = lax.broadcasted_iota(jnp.int32, (STAT, C), 0)
    bias = jnp.zeros((1, C), F32)
    for k in range(2 * PEERS):
        start = SHARE + (k % 2) * STAT
        tile = shares_ref[k // 2, start : start + STAT, :].astype(F32)
        bias += tile[DEPTH : DEPTH + 1]
        at = slice(k * STAT, (k + 1) * STAT)
        grads_ref[at, :] = jnp.where(row < DEPTH, tile, 0.0).astype(BF)
        low_ref[at, :] = pltpu.roll(tile, 8, 0).astype(BF)
        high_ref[at, :] = pltpu.roll(tile, 4, 0).astype(BF)
    bias_ref[...] = bias
    for k, ref in enumerate((low_ref, high_ref)):
        affine_ref[k * C : (k + 1) * C, :] = lax.dot_general(
            ref[...], grads_ref[...], (((0,), (0,)), ((), ())), preferred_element_type=F32
        )


def affine_gradient(shares, width):
    return pl.pallas_call(
        affine_kernel,
        out_shape=(jax.ShapeDtypeStruct((width, C), F32), jax.ShapeDtypeStruct((1, C), F32)),
        in_specs=[vmem_spec()],
        out_specs=(vmem_spec(), vmem_spec()),
        scratch_shapes=[pltpu.VMEM((2 * PEERS * STAT, C), BF)] * 3,
        compiler_params=params(),
        name="affine",
    )(shares)


def widen_half(half, value_ref, out_any, wide_ref, sem):
    value = value_ref[...].reshape(TAPS, BLOCK, C)
    rows = pl.ds(pl.multiple_of(half * BLOCK, BLOCK), BLOCK)
    copies = []
    for k in range(3):
        taps = slice(3 * k, 3 * k + 3)
        wide_ref[taps] = value[taps].astype(F32)
        copies.append(pltpu.make_async_copy(wide_ref.at[taps], out_any.at[taps, rows], sem.at[k]))
        copies[k].start()
    for copy in copies:
        copy.wait()


def own_kernel(value_ref, out_any, wide_ref, sem):
    _, _, core = place()
    widen_half(core, value_ref, out_any, wide_ref, sem)


def rest_kernel(value_ref, target_any, part_ref, moved_ref, out_any, sum_ref, wide_ref, sem):
    _, _, core = place()
    sum_ref[...] = part_ref[...] + moved_ref[...]
    widen_half(1 - core, value_ref, out_any, wide_ref, sem)


WIDE = jax.ShapeDtypeStruct((TAPS, C, C), F32)


def wide_scratch():
    return [pltpu.VMEM((TAPS, BLOCK, C), F32), pltpu.SemaphoreType.DMA((3,))]


def own_half(value):
    return pl.pallas_call(
        own_kernel,
        out_shape=WIDE,
        in_specs=[vmem_spec()],
        out_specs=pl.BlockSpec(memory_space=pltpu.HBM),
        scratch_shapes=wide_scratch(),
        compiler_params=params(),
        name="own",
    )(value)


def rest_half(value, target, part, moved):
    return pl.pallas_call(
        rest_kernel,
        out_shape=(WIDE, jax.ShapeDtypeStruct(part.shape, F32)),
        in_specs=[vmem_spec(), pl.BlockSpec(memory_space=pltpu.HBM), vmem_spec(), vmem_spec()],
        out_specs=(pl.BlockSpec(memory_space=pltpu.HBM), vmem_spec()),
        input_output_aliases={1: 0},
        scratch_shapes=wide_scratch(),
        compiler_params=params(),
        name="rest",
    )(value, target, part, moved)


def body(images, latent, weight, affine, biases, cotangent):
    width = latent.shape[1]
    replicas = lax.axis_size("dp")
    segments = lax.axis_size("segment")
    planes = [list(range(k, k + DEPTH)) for k in range(0, segments, DEPTH)]
    across = [(i, (i + DEPTH) % segments) for i in range(segments)]
    sibling = [(i, i ^ 1) for i in range(replicas)]
    cores = [list(range(k, replicas, 2)) for k in range(2)]

    w = weight.reshape(ROWS, C)
    images = images.reshape(DEPTH, PX, C)
    cotangent = cotangent.reshape(DEPTH, PX, C)

    def along(value, shift):
        pairs = [(i, i - i % DEPTH + (i + shift) % DEPTH) for i in range(segments)]
        return near(lax.ppermute(value, "segment", pairs))

    def swap(value):
        return near(lax.ppermute(value, "dp", sibling))

    beside = [(i, i ^ 2) for i in range(replicas)]
    down, up, far, tile, styles, demod, energy = prepare(latent, affine[0], w, biases)
    f0 = along(far, 2)
    f0, down, up = lax.optimization_barrier((f0, down, up))
    f1 = near(lax.ppermute(f0, "dp", beside))
    a1 = along(down, DEPTH - 1)
    a3 = along(up, 1)
    act, kernels, stat = first(images, w, tile, a1, swap(a1), a3, swap(a3), f0, f1, swap(f0), swap(f1))
    flipped = flip(kernels)
    arrived = near(lax.ppermute(act, "segment", across))
    dx, xs, conv, scaled = middle(images, cotangent, arrived, kernels, flipped, stat)
    returned = near(lax.ppermute(dx, "segment", across))
    maps = [scaled[0]] + [
        near(
            lax.ppermute(
                scaled[k], "segment", [(i, i - i % DEPTH + (i + k) % DEPTH) for i in range(segments)]
            )
        )
        for k in range(1, DEPTH)
    ]
    turned = turn(*maps)
    sent, turned = lax.optimization_barrier((last(cotangent, returned, xs, conv, flipped, stat), turned))

    r = near(lax.all_to_all(sent, "segment", 0, 0, axis_index_groups=planes))
    give, extra, part, padded, grad_energy = give_half(
        r, turned, w, styles, demod, energy, affine[0], latent
    )
    got = near(lax.ppermute(give, "dp", sibling))
    keep = keep_half(turned, padded, w, grad_energy)
    shared, part = lax.optimization_barrier((pair(keep, extra, got), part))
    shares = near(lax.all_to_all(near(shared), "dp", 0, 0, axis_index_groups=cores))
    part = part + lax.ppermute(part, "segment", [(i, i ^ 1) for i in range(segments)])
    part = part + lax.ppermute(part, "segment", [(i, i ^ 2) for i in range(segments)])
    spread_share, part = lax.optimization_barrier((share(shares), part))
    mine = lax.all_to_all(near(spread_share), "dp", 0, 0, axis_index_groups=cores)
    other = near(lax.ppermute(mine, "dp", sibling))
    mine, shares, part = lax.optimization_barrier((mine, shares, part))
    moved = lax.ppermute(part, "segment", across)
    grad_affine, grad_bias = affine_gradient(shares, width)
    grad_weight, grad_latent = rest_half(other, own_half(near(mine)), part, moved)
    grad_weight = grad_weight.reshape(weight.shape)
    return (grad_weight, grad_affine[None], grad_bias, grad_latent)


def solution(mesh):
    placed = (
        P("dp", None, None, None),
        P("dp", None),
        P("segment", None, None, None, None),
        P("segment", None, None),
        P("segment", None),
        P("dp", None, None, None),
    )
    return jax.shard_map(
        body,
        mesh=mesh,
        in_specs=placed,
        out_specs=(
            P("segment", None, None, None, None),
            P("segment", None, None),
            P("segment", None),
            P("dp", None),
        ),
        check_vma=False,
    )
```

```python
import math

import jax
import jax.numpy as jnp
from jax import lax
from jax.experimental import pallas as pl
from jax.experimental.pallas import tpu as pltpu
from jax.sharding import PartitionSpec as P

GAIN = math.sqrt(2.0)
EPS = 1e-08
BF = jnp.bfloat16
F32 = jnp.float32
C = 256
PX = 256
TAPS = 9
ROWS = TAPS * C
HALF = ROWS // 2
STAT = 16
DEPTH = 4
PEERS = 8
SHARE = HALF // PEERS
PART = HALF // 2
ROW = 16
BLOCK = 128
PAD = PX + 2 * ROW
HI = lax.Precision.HIGHEST


def any_spec():
    return pl.BlockSpec(memory_space=pl.ANY)


def vmem_spec():
    return pl.BlockSpec(memory_space=pltpu.VMEM)


def params():
    return pltpu.CompilerParams(vmem_limit_bytes=28 << 20)


def near(value):
    return pltpu.with_memory_space_constraint(value, pltpu.VMEM)


def place():
    seg = lax.axis_index("segment")
    return seg // DEPTH, seg % DEPTH, lax.axis_index("dp") % 2


def part_start(core, side):
    return pl.multiple_of(core * HALF + side * PART, PART)


def split3(value):
    hi = value.astype(BF).astype(F32)
    rest = value - hi
    mid = rest.astype(BF).astype(F32)
    return hi, mid, rest - mid


def pack_rows(values):
    row = lax.broadcasted_iota(jnp.int32, (STAT, C), 0)
    out = jnp.zeros((STAT, C), F32)
    k = 0
    for value in values:
        for part in split3(value):
            out = jnp.where(row == k, jnp.broadcast_to(part, (STAT, C)), out)
            k += 1
    return out.astype(BF)


def unpack_rows(tile):
    t = tile.astype(F32)
    return [t[3 * k : 3 * k + 1] + t[3 * k + 1 : 3 * k + 2] + t[3 * k + 2 : 3 * k + 3] for k in range(3)]


def stack_rows(rows):
    index = lax.broadcasted_iota(jnp.int32, (8, C), 0)
    out = jnp.zeros((8, C), F32)
    for k, row in enumerate(rows):
        out = jnp.where(index == k, jnp.broadcast_to(row, (8, C)), out)
    return out


def prepare_kernel(
    latent_hbm, affine_hbm, w_hbm, bias_hbm, down_ref, up_ref, far_ref, tile_ref, styles_ref, demod_ref, energy_ref,
    rows_ref, affine_ref, w_ref, bias_ref, tiles_ref, sem,
):
    _, z, core = place()
    side = (lax.axis_index("dp") // 2) % 2
    mine = pl.ds(pl.multiple_of(core * HALF, HALF), HALF)
    rows_ref[...] = jnp.zeros_like(rows_ref)
    third = ROWS // 3
    loads = [
        pltpu.make_async_copy(affine_hbm, affine_ref, sem.at[0]),
        pltpu.make_async_copy(latent_hbm, rows_ref.at[pl.ds(0, DEPTH)], sem.at[1]),
        pltpu.make_async_copy(bias_hbm, bias_ref, sem.at[2]),
    ] + [
        pltpu.make_async_copy(w_hbm.at[pl.ds(k * third, third)], w_ref.at[pl.ds(k * third, third)], sem.at[3 + k])
        for k in range(3)
    ]
    sends = [
        pltpu.make_async_copy(w_hbm.at[pl.ds(part_start(core, side), PART)], far_ref.at[pl.ds(0, PART)], sem.at[6]),
        pltpu.make_async_copy(w_hbm.at[mine], down_ref.at[pl.ds(0, HALF)], sem.at[7]),
        pltpu.make_async_copy(w_hbm.at[mine], up_ref.at[pl.ds(0, HALF)], sem.at[8]),
    ]
    for copy in loads + sends:
        copy.start()
    for copy in loads[:3]:
        copy.wait()
    styles = jnp.dot(rows_ref[...], affine_ref[...], precision=HI, preferred_element_type=F32) + 1.0
    energy = jnp.zeros((C, C), F32)
    for tap in range(TAPS):
        if tap % 3 == 0:
            loads[3 + tap // 3].wait()
        part = w_ref[tap * C : (tap + 1) * C, :].astype(F32)
        energy += part * part
    energy_ref[...] = energy
    demod = lax.rsqrt(jnp.dot(styles * styles, energy, precision=HI, preferred_element_type=F32) + EPS)
    styles_ref[...] = styles
    demod_ref[...] = demod
    for k in range(DEPTH):
        tiles_ref[k] = pack_rows([styles[k : k + 1], demod[k : k + 1], bias_ref[...]])
    tile_ref[...] = tiles_ref[z]
    down_ref[HALF : HALF + STAT, :] = tiles_ref[lax.rem(z + DEPTH - 1, DEPTH)]
    up_ref[HALF : HALF + STAT, :] = tiles_ref[lax.rem(z + 1, DEPTH)]
    far_ref[PART : PART + STAT, :] = tiles_ref[lax.rem(z + 2, DEPTH)]
    for copy in sends:
        copy.wait()


def prepare(latent, affine, w, bias):
    far = [pltpu.with_memory_space_constraint(value, pltpu.HBM) for value in (latent, affine, w, bias)]
    return pl.pallas_call(
        prepare_kernel,
        out_shape=(
            jax.ShapeDtypeStruct((HALF + STAT, C), BF),
            jax.ShapeDtypeStruct((HALF + STAT, C), BF),
            jax.ShapeDtypeStruct((PART + STAT, C), BF),
            jax.ShapeDtypeStruct((STAT, C), BF),
            jax.ShapeDtypeStruct((8, C), F32),
            jax.ShapeDtypeStruct((8, C), F32),
            jax.ShapeDtypeStruct((C, C), F32),
        ),
        in_specs=[pl.BlockSpec(memory_space=pltpu.HBM)] * 4,
        out_specs=(vmem_spec(),) * 7,
        scratch_shapes=[
            pltpu.VMEM((8, latent.shape[1]), F32),
            pltpu.VMEM(affine.shape, F32),
            pltpu.VMEM((ROWS, C), BF),
            pltpu.VMEM((1, C), F32),
            pltpu.VMEM((DEPTH, STAT, C), BF),
            pltpu.SemaphoreType.DMA((9,)),
        ],
        compiler_params=params(),
        name="prepare",
    )(*far)


def clear_pads(pad_ref):
    for k in range(3):
        pad_ref[k, 0:ROW, :] = jnp.zeros((ROW, C), BF)
        pad_ref[k, ROW + PX : PAD, :] = jnp.zeros((ROW, C), BF)


def spread(pad_ref, value):
    column = lax.broadcasted_iota(jnp.int32, (PX, C), 0) % ROW
    pad_ref[1, ROW : ROW + PX, :] = value.astype(BF)
    pad_ref[0, ROW : ROW + PX, :] = jnp.where(column == 0, 0.0, pltpu.roll(value, 1, 0)).astype(BF)
    pad_ref[2, ROW : ROW + PX, :] = jnp.where(column == ROW - 1, 0.0, pltpu.roll(value, PX - 1, 0)).astype(BF)


def taps_matmul(pad_ref, w, mirrored):
    out = []
    for start in range(0, PX, BLOCK):
        pieces = []
        for ky in range(3):
            for kx in range(3):
                plane, shift = (2 - kx, 2 - ky) if mirrored else (kx, ky)
                first_row = start + shift * ROW
                pieces.append(pad_ref[plane, first_row : first_row + BLOCK, :])
        out.append(jnp.dot(jnp.concatenate(pieces, axis=1), w, preferred_element_type=F32))
    return jnp.concatenate(out, axis=0)


def forward_layer(x, l, w_ref, stat, pad_ref):
    styles, demod, bias = stat
    spread(pad_ref, (x.astype(F32) * styles).astype(BF).astype(F32))
    return taps_matmul(pad_ref, w_ref[l], False)


def activate(conv, stat):
    _, demod, bias = stat
    hidden = conv * demod + bias
    return (GAIN * hidden * (0.6 + 0.4 * jnp.tanh(hidden))).astype(BF)


def backward_layer(upstream, x, conv, l, flip_ref, stat, pad_ref, send_ref=None):
    styles, demod, bias = stat
    hidden = conv * demod + bias
    t = jnp.tanh(hidden)
    dh = upstream.astype(F32) * (GAIN * (0.6 + 0.4 * t + 0.4 * hidden * (1.0 - t * t)))
    spread(pad_ref, (dh * demod).astype(BF).astype(F32))
    grad_scaled = taps_matmul(pad_ref, flip_ref[l], True).astype(BF).astype(F32)
    if send_ref is not None:
        grad_bias = jnp.sum(dh, axis=0, keepdims=True)
        grad_demod = jnp.sum(dh * conv, axis=0, keepdims=True)
        grad_styles = jnp.sum(grad_scaled * x.astype(F32), axis=0, keepdims=True)
        send_ref[l, 0:PX, :] = pad_ref[1, ROW : ROW + PX, :]
        send_ref[l, PX : PX + STAT, :] = pack_rows([grad_styles, grad_demod, grad_bias])
    return (grad_scaled * styles).astype(BF)


def layer_copies(tile_ref, w_any, near_refs, far_refs, w_ref, stat_ref, sem):
    _, z, core = place()
    side = (lax.axis_index("dp") // 2) % 2
    layer = [lax.rem(z + k, DEPTH) for k in range(DEPTH)]
    copies = [
        pltpu.make_async_copy(w_any, w_ref.at[layer[0]], sem.at[0]),
        pltpu.make_async_copy(tile_ref, stat_ref.at[layer[0]], sem.at[1]),
    ]

    def add(source, target):
        copies.append(pltpu.make_async_copy(source, target, sem.at[len(copies)]))

    for k, (a_ref, b_ref) in near_refs:
        for ref, half in ((a_ref, core), (b_ref, 1 - core)):
            add(ref.at[pl.ds(0, HALF)], w_ref.at[layer[k], pl.ds(pl.multiple_of(half * HALF, HALF), HALF)])
        add(a_ref.at[pl.ds(HALF, STAT)], stat_ref.at[layer[k]])
    for index, ref in enumerate(far_refs):
        half = core if index < 2 else 1 - core
        which = side if index % 2 == 0 else 1 - side
        add(ref.at[pl.ds(0, PART)], w_ref.at[layer[2], pl.ds(part_start(half, which), PART)])
    add(far_refs[0].at[pl.ds(PART, STAT)], stat_ref.at[layer[2]])
    return copies


def first_kernel(
    images_any, w_any, tile_ref, a1_ref, b1_ref, a3_ref, b3_ref, f0_ref, f1_ref, f2_ref, f3_ref,
    out_ref, w_ref, stat_ref, x_buf, pad_ref, sem, x_sem,
):
    _, z, _ = place()
    copies = layer_copies(
        tile_ref, w_any, ((1, (a1_ref, b1_ref)), (3, (a3_ref, b3_ref))), (f0_ref, f1_ref, f2_ref, f3_ref),
        w_ref, stat_ref, sem,
    )
    x_copy = pltpu.make_async_copy(images_any.at[z], x_buf, x_sem)
    x_copy.start()
    for copy in copies:
        copy.start()
    clear_pads(pad_ref)
    x_copy.wait()
    x = x_buf[...]
    for copy in copies:
        copy.wait()
    for l in range(DEPTH):
        stat = unpack_rows(stat_ref[l])
        x = activate(forward_layer(x, l, w_ref, stat, pad_ref), stat)
    out_ref[...] = x


def flip_kernel(w_ref, flip_ref):
    for l in range(DEPTH):
        for tap in range(TAPS):
            at = slice(tap * C, (tap + 1) * C)
            flip_ref[l, at, :] = w_ref[l, at, :].T


def middle_kernel(
    images_any, cot_any, recv_ref, w_ref, flip_ref, stat_ref, dx_ref, xs_ref, conv_ref, scaled_ref,
    x_buf, u_buf, pad_ref, x_sem,
):
    half, z, _ = place()
    x_copy = pltpu.make_async_copy(images_any.at[z], x_buf, x_sem.at[0])
    u_copy = pltpu.make_async_copy(cot_any.at[z], u_buf, x_sem.at[1])
    x_copy.start()
    u_copy.start()
    clear_pads(pad_ref)
    x_copy.wait()
    x = jnp.where(half == 1, recv_ref[...], x_buf[...])
    stats = []
    for l in range(DEPTH):
        stats.append(unpack_rows(stat_ref[l]))
        xs_ref[l] = x
        conv = forward_layer(x, l, w_ref, stats[l], pad_ref)
        conv_ref[l] = conv
        scaled_ref[lax.rem(l - z + DEPTH, DEPTH)] = pad_ref[1, ROW : ROW + PX, :]
        if l < DEPTH - 1:
            x = activate(conv, stats[l])
    u_copy.wait()
    upstream = u_buf[...]
    for l in reversed(range(DEPTH)):
        upstream = backward_layer(upstream, xs_ref[l], conv_ref[l], l, flip_ref, stats[l], pad_ref)
    dx_ref[...] = upstream


def last_kernel(cot_any, recv_ref, xs_ref, conv_ref, flip_ref, stat_ref, send_ref, u_buf, pad_ref, u_sem):
    half, z, _ = place()
    u_copy = pltpu.make_async_copy(cot_any.at[z], u_buf, u_sem)
    u_copy.start()
    clear_pads(pad_ref)
    u_copy.wait()
    upstream = jnp.where(half == 1, u_buf[...], recv_ref[...])
    for l in reversed(range(DEPTH)):
        stat = unpack_rows(stat_ref[l])
        upstream = backward_layer(upstream, xs_ref[l], conv_ref[l], l, flip_ref, stat, pad_ref, send_ref)


MAP = jax.ShapeDtypeStruct((PX, C), BF)
KERNELS = jax.ShapeDtypeStruct((DEPTH, ROWS, C), BF)
SENT = jax.ShapeDtypeStruct((DEPTH, PX + STAT, C), BF)


def first(images, w, tile, *parts):
    return pl.pallas_call(
        first_kernel,
        out_shape=(MAP, KERNELS, jax.ShapeDtypeStruct((DEPTH, STAT, C), BF)),
        in_specs=[pl.BlockSpec(memory_space=pltpu.HBM), any_spec()] + [vmem_spec()] * 9,
        out_specs=(vmem_spec(),) * 3,
        scratch_shapes=[
            pltpu.VMEM((PX, C), BF),
            pltpu.VMEM((3, PAD, C), BF),
            pltpu.SemaphoreType.DMA((13,)),
            pltpu.SemaphoreType.DMA,
        ],
        compiler_params=params(),
        name="first",
    )(pltpu.with_memory_space_constraint(images, pltpu.HBM), w, tile, *parts)


def flip(w):
    return pl.pallas_call(
        flip_kernel,
        out_shape=KERNELS,
        in_specs=[vmem_spec()],
        out_specs=vmem_spec(),
        compiler_params=params(),
        name="flip",
    )(w)


def middle(images, cot, recv, w, flipped, stat):
    return pl.pallas_call(
        middle_kernel,
        out_shape=(
            MAP,
            jax.ShapeDtypeStruct((DEPTH, PX, C), BF),
            jax.ShapeDtypeStruct((DEPTH, PX, C), F32),
            jax.ShapeDtypeStruct((DEPTH, PX, C), BF),
        ),
        in_specs=[any_spec(), any_spec()] + [vmem_spec()] * 4,
        out_specs=(vmem_spec(),) * 4,
        scratch_shapes=[
            pltpu.VMEM((PX, C), BF),
            pltpu.VMEM((PX, C), BF),
            pltpu.VMEM((3, PAD, C), BF),
            pltpu.SemaphoreType.DMA((2,)),
        ],
        compiler_params=params(),
        name="middle",
    )(images, cot, recv, w, flipped, stat)


def last(cot, recv, xs, conv, flipped, stat):
    return pl.pallas_call(
        last_kernel,
        out_shape=SENT,
        in_specs=[any_spec()] + [vmem_spec()] * 5,
        out_specs=vmem_spec(),
        scratch_shapes=[
            pltpu.VMEM((PX, C), BF),
            pltpu.VMEM((3, PAD, C), BF),
            pltpu.SemaphoreType.DMA,
        ],
        compiler_params=params(),
        name="last",
    )(cot, recv, xs, conv, flipped, stat)


def half_gradient(flip_ref, pad_ref, w_ref, grad_energy_ref, half, out_ref):
    first_row = pl.multiple_of(half * BLOCK, BLOCK)
    lhs = flip_ref[pl.ds(first_row, BLOCK), :]
    grad_energy = grad_energy_ref[pl.ds(first_row, BLOCK), :]
    for ky in range(3):
        for kx in range(3):
            tap = ky * 3 + kx
            rhs = jnp.concatenate(
                [pad_ref[n, 2 - kx, (2 - ky) * ROW : (2 - ky) * ROW + PX, :] for n in range(DEPTH)], axis=0
            )
            part = jnp.dot(lhs, rhs, preferred_element_type=F32)
            w = w_ref[pl.ds(pl.multiple_of(tap * C + half * BLOCK, BLOCK), BLOCK), :].astype(F32)
            out_ref[tap * BLOCK : (tap + 1) * BLOCK, :] = (part + w * grad_energy).astype(BF)


def turn_kernel(s0_ref, s1_ref, s2_ref, s3_ref, flip_ref):
    for k, ref in enumerate((s0_ref, s1_ref, s2_ref, s3_ref)):
        flip_ref[:, k * PX : (k + 1) * PX] = ref[...].T


def turn(*maps):
    return pl.pallas_call(
        turn_kernel,
        out_shape=jax.ShapeDtypeStruct((C, DEPTH * PX), BF),
        in_specs=[vmem_spec()] * DEPTH,
        out_specs=vmem_spec(),
        compiler_params=params(),
        name="turn",
    )(*maps)


def give_kernel(
    r_ref, flip_ref, w_ref, styles_ref, demod_ref, energy_ref, affine_ref, latent_ref,
    give_ref, extra_ref, grad_latent_ref, pad_ref, grad_energy_ref, rows_ref,
):
    _, z, core = place()
    parts = [unpack_rows(r_ref[n, PX : PX + STAT, :]) for n in range(DEPTH)]
    styles = styles_ref[...]
    demod = demod_ref[...]
    grad_sum = stack_rows([p[1] for p in parts]) * (-0.5) * demod * demod * demod
    squares = styles * styles
    grad_squares = lax.dot_general(
        grad_sum, energy_ref[...], (((1,), (1,)), ((), ())), precision=HI, preferred_element_type=F32
    )
    grad_styles = stack_rows([p[0] for p in parts]) + 2.0 * styles * grad_squares
    grad_bias = parts[0][2] + parts[1][2] + parts[2][2] + parts[3][2]
    rows_ref[...] = jnp.zeros_like(rows_ref)
    rows_ref[0:DEPTH, :] = grad_styles[0:DEPTH]
    rows_ref[DEPTH : DEPTH + 1, :] = grad_bias
    rows_ref[8 : 8 + DEPTH, :] = latent_ref[:, 0:C]
    rows_ref[8 + DEPTH : 8 + 2 * DEPTH, :] = latent_ref[:, C : 2 * C]
    extra = rows_ref[...].astype(BF)
    extra_ref[...] = extra
    give_ref[HALF : HALF + STAT, :] = extra
    grad_latent = lax.dot_general(
        grad_styles, affine_ref[...], (((1,), (1,)), ((), ())), precision=HI, preferred_element_type=F32
    )
    grad_latent_ref[...] = grad_latent[0:DEPTH]
    grad_energy_ref[...] = 2.0 * lax.dot_general(
        squares, grad_sum, (((0,), (0,)), ((), ())), precision=HI, preferred_element_type=F32
    )
    for k in range(DEPTH):
        clear_pads(pad_ref.at[k])
        spread(pad_ref.at[k], r_ref[lax.rem(z - k + DEPTH, DEPTH), 0:PX, :].astype(F32))
    half_gradient(flip_ref, pad_ref, w_ref, grad_energy_ref, 1 - core, give_ref)


def give_half(r, turned, w, styles, demod, energy, affine, latent):
    return pl.pallas_call(
        give_kernel,
        out_shape=(
            jax.ShapeDtypeStruct((HALF + STAT, C), BF),
            jax.ShapeDtypeStruct((STAT, C), BF),
            jax.ShapeDtypeStruct((DEPTH, affine.shape[0]), F32),
            jax.ShapeDtypeStruct((DEPTH, 3, PAD, C), BF),
            jax.ShapeDtypeStruct((C, C), F32),
        ),
        in_specs=[vmem_spec()] * 8,
        out_specs=(vmem_spec(),) * 5,
        scratch_shapes=[pltpu.VMEM((STAT, C), F32)],
        compiler_params=params(),
        name="give",
    )(r, turned, w, styles, demod, energy, affine, latent)


def keep_kernel(flip_ref, pad_ref, w_ref, grad_energy_ref, keep_ref):
    _, _, core = place()
    half_gradient(flip_ref, pad_ref, w_ref, grad_energy_ref, core, keep_ref)


def keep_half(flipped, padded, w, grad_energy):
    return pl.pallas_call(
        keep_kernel,
        out_shape=jax.ShapeDtypeStruct((HALF, C), BF),
        in_specs=[vmem_spec()] * 4,
        out_specs=vmem_spec(),
        compiler_params=params(),
        name="keep",
    )(flipped, padded, w, grad_energy)


def pair_kernel(keep_ref, extra_ref, got_ref, out_ref):
    for k in range(PEERS):
        at = slice(k * SHARE, (k + 1) * SHARE)
        out_ref[k, 0:SHARE, :] = (keep_ref[at, :].astype(F32) + got_ref[at, :].astype(F32)).astype(BF)
        out_ref[k, SHARE : SHARE + STAT, :] = extra_ref[...]
        out_ref[k, SHARE + STAT : SHARE + 2 * STAT, :] = got_ref[HALF : HALF + STAT, :]


def pair(keep, extra, got):
    return pl.pallas_call(
        pair_kernel,
        out_shape=jax.ShapeDtypeStruct((PEERS, SHARE + 2 * STAT, C), BF),
        in_specs=[vmem_spec()] * 3,
        out_specs=vmem_spec(),
        compiler_params=params(),
        name="pair",
    )(keep, extra, got)


def share_kernel(shares_ref, out_ref):
    total = shares_ref[0, 0:SHARE, :].astype(F32)
    for k in range(1, PEERS):
        total += shares_ref[k, 0:SHARE, :].astype(F32)
    total = total.astype(BF)
    for k in range(PEERS):
        out_ref[k] = total


def share(shares):
    return pl.pallas_call(
        share_kernel,
        out_shape=jax.ShapeDtypeStruct((PEERS, SHARE, C), BF),
        in_specs=[vmem_spec()],
        out_specs=vmem_spec(),
        compiler_params=params(),
        name="share",
    )(shares)


def affine_kernel(shares_ref, affine_ref, bias_ref, grads_ref, low_ref, high_ref):
    row = lax.broadcasted_iota(jnp.int32, (STAT, C), 0)
    bias = jnp.zeros((1, C), F32)
    for k in range(2 * PEERS):
        start = SHARE + (k % 2) * STAT
        tile = shares_ref[k // 2, start : start + STAT, :].astype(F32)
        bias += tile[DEPTH : DEPTH + 1]
        at = slice(k * STAT, (k + 1) * STAT)
        grads_ref[at, :] = jnp.where(row < DEPTH, tile, 0.0).astype(BF)
        low_ref[at, :] = pltpu.roll(tile, 8, 0).astype(BF)
        high_ref[at, :] = pltpu.roll(tile, 4, 0).astype(BF)
    bias_ref[...] = bias
    for k, ref in enumerate((low_ref, high_ref)):
        affine_ref[k * C : (k + 1) * C, :] = lax.dot_general(
            ref[...], grads_ref[...], (((0,), (0,)), ((), ())), preferred_element_type=F32
        )


def affine_gradient(shares, width):
    return pl.pallas_call(
        affine_kernel,
        out_shape=(jax.ShapeDtypeStruct((width, C), F32), jax.ShapeDtypeStruct((1, C), F32)),
        in_specs=[vmem_spec()],
        out_specs=(vmem_spec(), vmem_spec()),
        scratch_shapes=[pltpu.VMEM((2 * PEERS * STAT, C), BF)] * 3,
        compiler_params=params(),
        name="affine",
    )(shares)


def widen_half(half, value_ref, out_any, wide_ref, sem):
    value = value_ref[...].reshape(TAPS, BLOCK, C)
    rows = pl.ds(pl.multiple_of(half * BLOCK, BLOCK), BLOCK)
    copies = []
    for k in range(3):
        taps = slice(3 * k, 3 * k + 3)
        wide_ref[taps] = value[taps].astype(F32)
        copies.append(pltpu.make_async_copy(wide_ref.at[taps], out_any.at[taps, rows], sem.at[k]))
        copies[k].start()
    for copy in copies:
        copy.wait()


def own_kernel(value_ref, out_any, wide_ref, sem):
    _, _, core = place()
    widen_half(core, value_ref, out_any, wide_ref, sem)


def rest_kernel(value_ref, target_any, part_ref, moved_ref, out_any, sum_ref, wide_ref, sem):
    _, _, core = place()
    sum_ref[...] = part_ref[...] + moved_ref[...]
    widen_half(1 - core, value_ref, out_any, wide_ref, sem)


WIDE = jax.ShapeDtypeStruct((TAPS, C, C), F32)


def wide_scratch():
    return [pltpu.VMEM((TAPS, BLOCK, C), F32), pltpu.SemaphoreType.DMA((3,))]


def own_half(value):
    return pl.pallas_call(
        own_kernel,
        out_shape=WIDE,
        in_specs=[vmem_spec()],
        out_specs=pl.BlockSpec(memory_space=pltpu.HBM),
        scratch_shapes=wide_scratch(),
        compiler_params=params(),
        name="own",
    )(value)


def rest_half(value, target, part, moved):
    return pl.pallas_call(
        rest_kernel,
        out_shape=(WIDE, jax.ShapeDtypeStruct(part.shape, F32)),
        in_specs=[vmem_spec(), pl.BlockSpec(memory_space=pltpu.HBM), vmem_spec(), vmem_spec()],
        out_specs=(pl.BlockSpec(memory_space=pltpu.HBM), vmem_spec()),
        input_output_aliases={1: 0},
        scratch_shapes=wide_scratch(),
        compiler_params=params(),
        name="rest",
    )(value, target, part, moved)


def body(images, latent, weight, affine, biases, cotangent):
    width = latent.shape[1]
    replicas = lax.axis_size("dp")
    segments = lax.axis_size("segment")
    planes = [list(range(k, k + DEPTH)) for k in range(0, segments, DEPTH)]
    across = [(i, (i + DEPTH) % segments) for i in range(segments)]
    sibling = [(i, i ^ 1) for i in range(replicas)]
    cores = [list(range(k, replicas, 2)) for k in range(2)]

    w = weight.reshape(ROWS, C)
    images = images.reshape(DEPTH, PX, C)
    cotangent = cotangent.reshape(DEPTH, PX, C)

    def along(value, shift):
        pairs = [(i, i - i % DEPTH + (i + shift) % DEPTH) for i in range(segments)]
        return near(lax.ppermute(value, "segment", pairs))

    def swap(value):
        return near(lax.ppermute(value, "dp", sibling))

    beside = [(i, i ^ 2) for i in range(replicas)]
    down, up, far, tile, styles, demod, energy = prepare(latent, affine[0], w, biases)
    f0 = along(far, 2)
    f0, up = lax.optimization_barrier((f0, up))
    f1 = near(lax.ppermute(f0, "dp", beside))
    a1 = along(down, DEPTH - 1)
    a3 = along(up, 1)
    act, kernels, stat = first(images, w, tile, a1, swap(a1), a3, swap(a3), f0, f1, swap(f0), swap(f1))
    flipped = flip(kernels)
    arrived = near(lax.ppermute(act, "segment", across))
    dx, xs, conv, scaled = middle(images, cotangent, arrived, kernels, flipped, stat)
    returned = near(lax.ppermute(dx, "segment", across))
    maps = [scaled[0]] + [
        near(
            lax.ppermute(
                scaled[k], "segment", [(i, i - i % DEPTH + (i + k) % DEPTH) for i in range(segments)]
            )
        )
        for k in range(1, DEPTH)
    ]
    turned = turn(*maps)
    sent, turned = lax.optimization_barrier((last(cotangent, returned, xs, conv, flipped, stat), turned))

    r = near(lax.all_to_all(sent, "segment", 0, 0, axis_index_groups=planes))
    give, extra, part, padded, grad_energy = give_half(
        r, turned, w, styles, demod, energy, affine[0], latent
    )
    got = near(lax.ppermute(give, "dp", sibling))
    keep = keep_half(turned, padded, w, grad_energy)
    shared, part = lax.optimization_barrier((pair(keep, extra, got), part))
    shares = near(lax.all_to_all(near(shared), "dp", 0, 0, axis_index_groups=cores))
    part = part + lax.ppermute(part, "segment", [(i, i ^ 1) for i in range(segments)])
    part = part + lax.ppermute(part, "segment", [(i, i ^ 2) for i in range(segments)])
    spread_share, part = lax.optimization_barrier((share(shares), part))
    mine = lax.all_to_all(near(spread_share), "dp", 0, 0, axis_index_groups=cores)
    other = near(lax.ppermute(mine, "dp", sibling))
    mine, shares, part = lax.optimization_barrier((mine, shares, part))
    moved = lax.ppermute(part, "segment", across)
    grad_affine, grad_bias = affine_gradient(shares, width)
    grad_weight, grad_latent = rest_half(other, own_half(near(mine)), part, moved)
    grad_weight = grad_weight.reshape(weight.shape)
    return (grad_weight, grad_affine[None], grad_bias, grad_latent)


def solution(mesh):
    placed = (
        P("dp", None, None, None),
        P("dp", None),
        P("segment", None, None, None, None),
        P("segment", None, None),
        P("segment", None),
        P("dp", None, None, None),
    )
    return jax.shard_map(
        body,
        mesh=mesh,
        in_specs=placed,
        out_specs=(
            P("segment", None, None, None, None),
            P("segment", None, None),
            P("segment", None),
            P("dp", None),
        ),
        check_vma=False,
    )
```
